32 devices in a mesh: gx: 4 (over y, x), gy: 4 (over z), gz: 2 (over core).
Axes of the slice: x: 2, y: 2, z: 4, core: 2. Of those that a mesh axis runs over, the one named last changes fastest.
Arguments:
- offsets: float32 [3, 4, 4, 6, 128], P(None, 'gx', 'gy', 'gz'), may hold values from 0 to 1
- velocity: float32 [3, 4, 4, 6, 128], P(None, 'gx', 'gy', 'gz'), may hold values from -6 to 6
- counts: int32 [4, 4, 6], P('gx', 'gy', 'gz'), may hold values from 0 to 128, as said below
- neighbours: int32 [4, 4, 6, 27], P('gx', 'gy', 'gz'), may hold values from 0 to 27, as said below
Outputs:
- velocity_star: float32 [3, 4, 4, 6, 128], P(None, 'gx', 'gy', 'gz')
- pressure: float32 [4, 4, 6, 128], P('gx', 'gy', 'gz')
The draws below stay inside these ranges and needn't reach their ends.
Inputs may be any that keep to these rules, and one draw needn't show every extreme that they name: `counts`: each column along the entry direction is filled up to a surface height of at least its lowest block; blocks above it are empty, blocks below hold 42 or more particles, and some hold 128. `neighbours`: for each block, the codes 9 (dx + 1) + 3 (dy + 1) + (dz + 1) of the adjacent blocks, itself included, that lie in the grid and hold particles, in increasing order, then the code 27 to fill 27 entries.
All inputs are finite; a program needn't handle non-finite values.
Results may differ from the reference program's by a relative error of at most 0.0003.
Values sent between devices are 32-bit elements; how exact they have to be, the bound alone decides.
No kernel may reach another device: no remote copies, remote signals or barrier semaphores. Data moves between devices by JAX's collectives and lax.ppermute only.
A program may use at most 64 MiB of HBM per device.

```python
import jax
import jax.numpy as jnp
from jax import lax

BLK = 128
ITERS_V = 3
ITERS_P = 2
NXB = 4
NYB = 4
NZB = 6


def wet_counts(key):
    inner = jax.random.fold_in(key, 11)
    first, second = jax.random.split(inner)
    surface = jax.random.randint(first, (NYB, NZB), max(1, NXB // 4), NXB + 1)
    level = jnp.arange(NXB, dtype=jnp.int32)[:, None, None]
    wet = level < surface[None]
    filled = jax.random.randint(second, (NXB, NYB, NZB), BLK // 3, 2 * BLK)
    return jnp.where(wet, jnp.minimum(filled, BLK), 0).astype(jnp.int32)


def draw_counts(key, part):
    return wet_counts(key)


def draw_neighbours(key, part):
    wet = jnp.pad(wet_counts(key) > 0, 1)
    listed = []
    for code in range(27):
        step_x = code // 9
        step_y = code // 3 % 3
        step_z = code % 3
        present = wet[step_x:step_x + NXB, step_y:step_y + NYB, step_z:step_z + NZB]
        listed.append(jnp.where(present, code, 27))
    return jnp.sort(jnp.stack(listed, -1), axis=-1).astype(jnp.int32)


def block_levels(key, extent, shards, smallest, top_value):
    factor_of = 1.0
    for axis_at, blocks in shards:
        draws = jax.random.uniform(jax.random.fold_in(jax.random.fold_in(key, 6), axis_at), (blocks,), jnp.float32, smallest / len(shards), top_value / len(shards))
        factor_of = factor_of * jnp.repeat(jnp.exp(draws), extent[axis_at] // blocks).reshape((-1,) + (1,) * (len(extent) - 1 - axis_at))
    return factor_of


def gaussian(stream_key, shape, scale, limit, cuts=(), kind=jnp.bfloat16):
    drawn = jax.random.normal(stream_key, shape, jnp.float32) * scale
    if len(cuts) > 0:
        drawn = block_levels(stream_key, shape, cuts, -0.22, 0.18) * drawn
    return jnp.clip(drawn, min=-limit, max=limit).astype(kind)


def setup_inputs(seed: int = 0) -> dict:
    key_of = jax.random.split(jax.random.key(seed), 5)
    return {
        "offsets": jnp.clip(1.0 * jax.random.uniform(key_of[0], (3, NXB, NYB, NZB, BLK), jnp.float32) ** block_levels(key_of[0], (3, NXB, NYB, NZB, BLK), ((1, 4), (2, 4), (3, 2)), -0.2, 0.2), 0.0, 1.0),
        "velocity": gaussian(key_of[1], (3, NXB, NYB, NZB, BLK), 1.0, 6.0, ((1, 4), (2, 4), (3, 2)), jnp.float32),
        "counts": draw_counts(jax.random.fold_in(key_of[4], 71), 0),
        "neighbours": draw_neighbours(jax.random.fold_in(key_of[4], 71), 0),
    }


VISCOUS = 4.0
STIFFNESS = 0.25
GRAVITY_STEP = 0.5
HIGHEST = lax.Precision.HIGHEST


def code_shift(codes):
    live = codes < 27
    shift_x = jnp.where(live, codes // 9 - 1, 0)
    shift_y = jnp.where(live, (codes // 3) % 3 - 1, 0)
    shift_z = jnp.where(live, codes % 3 - 1, 0)
    return live, shift_x, shift_y, shift_z


def block_tile(own_block, near_block, live_block, shift_block):
    width = own_block.shape[-1]
    squared = jnp.zeros((near_block.shape[1], width, width), jnp.float32)
    for axis in range(3):
        apart = shift_block[axis][:, None, None] + near_block[axis][:, None, :] - own_block[axis][None, :, None]
        squared = squared + apart * apart
    bump = jnp.maximum(1.0 - squared, 0.0)
    weight = bump * bump * bump * (2.0 / width)
    return weight * live_block[:, None, None] * own_block[3][None, :, None] * near_block[3][:, None, :]


def reference(offsets, velocity, counts, neighbours):
    total_blocks = NXB * NYB * NZB
    slots = jnp.arange(BLK, dtype=jnp.int32)
    valid = (slots < counts[..., None]).astype(jnp.float32)
    geometry = jnp.concatenate([offsets, valid[None]], 0)
    pad_y = NYB + 2
    pad_z = NZB + 2

    def padded_flat(field):
        return jnp.pad(field, ((0, 0), (1, 1), (1, 1), (1, 1), (0, 0))).reshape(field.shape[0], -1, BLK)

    geometry_flat = padded_flat(geometry)
    own_geometry = geometry.reshape(4, total_blocks, BLK)
    codes = neighbours.reshape(total_blocks, 27)
    live, shift_x, shift_y, shift_z = code_shift(codes)
    index_x = jnp.arange(NXB, dtype=jnp.int32)[:, None, None]
    index_y = jnp.arange(NYB, dtype=jnp.int32)[None, :, None]
    index_z = jnp.arange(NZB, dtype=jnp.int32)[None, None, :]
    anchor = (((index_x + 1) * pad_y + index_y + 1) * pad_z + index_z + 1).reshape(total_blocks)
    index = (anchor[:, None] + (shift_x * pad_y + shift_y) * pad_z + shift_z).astype(jnp.int32)
    shifts = jnp.stack([shift_x, shift_y, shift_z]).astype(jnp.float32)
    live_weight = live.astype(jnp.float32)
    columns = jnp.arange(NXB * NYB, dtype=jnp.int32)

    def column_tiles(column):
        start = (column * NZB).astype(jnp.int32)
        own = lax.dynamic_slice_in_dim(own_geometry, start, NZB, 1)
        where_from = lax.dynamic_slice_in_dim(index, start, NZB, 0)
        near = geometry_flat[:, where_from]
        live_part = lax.dynamic_slice_in_dim(live_weight, start, NZB, 0)
        shift_part = lax.dynamic_slice_in_dim(shifts, start, NZB, 1)
        tiles = jax.vmap(block_tile, in_axes=(1, 1, 0, 1))(own, near, live_part, shift_part)
        return tiles, near, where_from, start, own, shift_part

    def laplacian(vector):
        parts = vector.shape[0]
        flat = padded_flat(vector.reshape(parts, NXB, NYB, NZB, BLK))

        def one_column(column):
            tiles, near, where_from, start, own, shift_part = column_tiles(column)
            beside_all = flat[:, where_from]
            centre = lax.dynamic_slice_in_dim(vector, start, NZB, 1)
            row_total = jnp.sum(jnp.sum(tiles, axis=3), axis=1)
            mixed = jnp.einsum("bkij,cbkj->cbi", tiles, beside_all, precision=HIGHEST)
            return row_total * centre - mixed

        result = lax.map(one_column, columns)
        return jnp.moveaxis(result, 0, 1).reshape(parts, total_blocks, BLK)

    def conjugate(right, operate, iterations):
        solution = jnp.zeros_like(right)
        residual = right
        direction = right
        current = jnp.sum(residual * residual, axis=(1, 2))
        for step in range(iterations):
            image = operate(direction)
            alpha = current / jnp.sum(direction * image, axis=(1, 2))
            solution = solution + alpha[:, None, None] * direction
            residual = residual - alpha[:, None, None] * image
            following = jnp.sum(residual * residual, axis=(1, 2))
            direction = residual + (following / current)[:, None, None] * direction
            current = following
        return solution

    def viscous(vector):
        return vector + VISCOUS * laplacian(vector)

    def poisson(vector):
        return STIFFNESS * vector + laplacian(vector)

    gravity = jnp.array([GRAVITY_STEP, 0.0, 0.0], jnp.float32)[:, None, None]
    right = own_geometry[3][None] * (velocity.reshape(3, total_blocks, BLK) + gravity)
    star = conjugate(right, viscous, ITERS_V)

    star_flat = padded_flat(star.reshape(3, NXB, NYB, NZB, BLK))

    def column_divergence(column):
        tiles, near, where_from, start, own, shift_part = column_tiles(column)
        beside_all = star_flat[:, where_from]
        near_offsets = near[0:3]
        stacked = jnp.concatenate([beside_all, beside_all * near_offsets, near_offsets], 0)
        mixed = jnp.einsum("bkij,ybkj->ybki", tiles, stacked, precision=HIGHEST)
        w_velocity = mixed[0:3]
        w_product = mixed[3:6]
        w_offset = mixed[6:9]
        centre_velocity = lax.dynamic_slice_in_dim(star, start, NZB, 1)[:, :, None, :]
        centre_offset = own[0:3][:, :, None, :]
        reach = jnp.sum(tiles, axis=3)[None]
        terms = shift_part[..., None] * (w_velocity - centre_velocity * reach) + w_product - centre_offset * w_velocity - centre_velocity * w_offset + centre_velocity * centre_offset * reach
        return jnp.sum(terms, axis=(0, 2))

    divergence = lax.map(column_divergence, columns).reshape(total_blocks, BLK)
    source = -divergence
    pressure = conjugate(source[None], poisson, ITERS_P)
    return star.reshape(3, NXB, NYB, NZB, BLK), pressure.reshape(NXB, NYB, NZB, BLK)
```

```python
import functools

import jax
import jax.numpy as jnp
from jax import lax
from jax.experimental import pallas as pl
from jax.experimental.pallas import tpu as pltpu
from jax.sharding import PartitionSpec as P

VISCOUS = 4.0
STIFFNESS = 0.25
GRAVITY_STEP = 0.5
AXES = ("gx", "gy", "gz")
FAR = 1.0e4
LANES = 128


def exchange(send):
    return lax.all_to_all(send, AXES, 0, 0, tiled=True)


class Plan:
    def __init__(self, mesh, blocks, width):
        self.count = [mesh.shape[axis] for axis in AXES]
        self.devices = self.count[0] * self.count[1] * self.count[2]
        self.blocks = blocks
        self.width = width
        self.deep = blocks + 2
        self.ring = 9 * self.deep
        self.pad = -(-self.ring // 8) * 8
        self.cube = (2.0 / width) ** (1.0 / 3.0)
        self.unit = self.cube ** 0.5

    def own(self, block):
        return 4 * self.deep + block + 1

    def beside(self, block, code):
        return (code // 3) * self.deep + block + code % 3


def rows_of(plan, field):
    return slice(field * plan.pad, field * plan.pad + plan.ring)


def slots(plan):
    place = [lax.axis_index(axis) for axis in AXES]
    found = {}
    for code in range(27):
        at = [place[0] + code // 9 - 1, place[1] + code // 3 % 3 - 1, place[2] + code % 3 - 1]
        present = None
        slot = 0
        for value, count in zip(at, plan.count):
            inside = jnp.logical_and(value >= 0, value < count)
            present = inside if present is None else jnp.logical_and(present, inside)
            slot = slot * count + jnp.clip(value, 0, count - 1)
        found[code] = (slot, present)
    return found


def gather_ring(plan, found, recv, fields, store):
    for column in range(9):
        for level in range(plan.deep):
            if level == 0:
                code, block = column * 3, plan.blocks - 1
            elif level == plan.deep - 1:
                code, block = column * 3 + 2, 0
            else:
                code, block = column * 3 + 1, level - 1
            slot, present = found[code]
            for field in range(fields):
                row = recv[slot, field * plan.blocks + block]
                store(field, column * plan.deep + level, column, level, row, present)


def ring_into(plan, found, recv, fields, ref):
    def store(field, at, column, level, row, present):
        ref[pl.ds(field * plan.pad + at, 1), :] = row

    gather_ring(plan, found, recv, fields, store)


def lane_ids():
    return lax.broadcasted_iota(jnp.int32, (1, LANES), 1)


def totals(recv, row, number):
    summed = jnp.sum(recv[:, row], axis=0)
    lane = lane_ids()
    return [
        jnp.sum(jnp.where(lane == m, summed, 0.0), axis=1, keepdims=True) for m in range(number)
    ]


def pack(partials):
    lane = lane_ids()
    row = jnp.zeros((1, LANES), jnp.float32)
    for m, partial in enumerate(partials):
        row = jnp.where(lane == m, jnp.sum(partial, axis=1, keepdims=True), row)
    return row


def dot(first, second):
    total = first[0] * second[0]
    for a, b in zip(first[1:], second[1:]):
        total = total + a * b
    return total


def spread(plan, send, rows):
    def body(slot, carry):
        for r, row in enumerate(rows):
            send[slot, r] = row
        return carry

    lax.fori_loop(0, plan.devices, body, 0)


def columns_to_rows(plan, cols, rows, number):
    for block in range(plan.blocks):
        flipped = jnp.transpose(cols[block])
        rows[block] = flipped[0:8]


def apply_tiles(plan, tiles, fields, cols, chunk):
    lane = lax.broadcasted_iota(jnp.int32, (chunk, LANES), 1)

    def body(step, carry):
        start = pl.multiple_of(step * chunk, chunk)
        for block in range(plan.blocks):
            sums = [None] * len(fields)
            for code in range(27):
                at = plan.beside(block, code)
                tile = tiles[block * 27 + code, pl.ds(start, chunk), :]
                for f, (ref, base) in enumerate(fields):
                    term = tile * ref[pl.ds(base + at, 1), :]
                    sums[f] = term if sums[f] is None else sums[f] + term
            merged = jnp.zeros((chunk, LANES), jnp.float32)
            for f, total in enumerate(sums):
                merged = jnp.where(lane == f, jnp.sum(total, axis=1, keepdims=True), merged)
            cols[block, pl.ds(start, chunk), :] = merged
        return carry

    lax.fori_loop(0, plan.width // chunk, body, 0)


def pack_kernel(plan, counts, offsets, velocity, send):
    lane = lane_ids()
    rows = []
    for axis in range(3):
        for block in range(plan.blocks):
            valid = lane < counts[0, 0, block]
            row = offsets[axis, 0, 0, pl.ds(block, 1), :]
            rows.append(jnp.where(valid, row, FAR) if axis == 0 else row)
    for axis in range(3):
        for block in range(plan.blocks):
            valid = lane < counts[0, 0, block]
            row = velocity[axis, 0, 0, pl.ds(block, 1), :]
            if axis == 0:
                row = row + GRAVITY_STEP
            rows.append(jnp.where(valid, row, 0.0))
    spread(plan, send, rows)


def build_kernel(plan, recv, send, tiles, where, right, state, cols, rows):
    found = slots(plan)

    def store(field, at, column, level, row, present):
        if field < 3:
            shift = (column // 3 - 1, column % 3 - 1, level - 1)[field]
            row = plan.unit * (row + shift)
            if field == 0:
                row = jnp.where(present, row, FAR)
            where[pl.ds(field * plan.pad + at, 1), :] = row
        else:
            row = jnp.where(present, row, 0.0)
            right[pl.ds((field - 3) * plan.pad + at, 1), :] = row

    gather_ring(plan, found, recv, 6, store)
    chunk = 32
    lane = lax.broadcasted_iota(jnp.int32, (chunk, LANES), 1)
    sub = lax.broadcasted_iota(jnp.int32, (chunk, LANES), 0)

    def body(step, carry):
        start = pl.multiple_of(step * chunk, chunk)
        eye = lane == sub + start
        for block in range(plan.blocks):
            centre = []
            for axis in range(3):
                row = where[pl.ds(axis * plan.pad + plan.own(block), 1), :]
                if axis == 0:
                    row = jnp.where(row > 0.25 * FAR, -FAR, row)
                column = jnp.sum(jnp.where(eye, row, 0.0), axis=1, keepdims=True)
                centre.append(jnp.broadcast_to(column, (chunk, LANES)))
            sums = [None] * 7
            for code in range(27):
                at = plan.beside(block, code)
                near = [where[pl.ds(axis * plan.pad + at, 1), :] for axis in range(3)]
                rest = plan.cube
                for axis in range(3):
                    apart = near[axis] - centre[axis]
                    rest = rest - apart * apart
                bump = jnp.maximum(rest, 0.0)
                tile = bump * bump * bump
                tiles[block * 27 + code, pl.ds(start, chunk), :] = tile
                terms = [tile]
                for axis in range(3):
                    terms.append(tile * right[pl.ds(axis * plan.pad + at, 1), :])
                for axis in range(3):
                    terms.append(tile * near[axis])
                sums = [t if s is None else s + t for s, t in zip(sums, terms)]
            merged = jnp.zeros((chunk, LANES), jnp.float32)
            for f, total in enumerate(sums):
                merged = jnp.where(lane == f, jnp.sum(total, axis=1, keepdims=True), merged)
            cols[block, pl.ds(start, chunk), :] = merged
        return carry

    lax.fori_loop(0, plan.width // chunk, body, 0)
    columns_to_rows(plan, cols, rows, 7)
    image = [[None] * plan.blocks for _ in range(3)]
    whole = [[None] * plan.blocks for _ in range(3)]
    start = [[None] * plan.blocks for _ in range(3)]
    for block in range(plan.blocks):
        reach = rows[block, pl.ds(0, 1), :]
        state[pl.ds(block, 1), :] = reach
        for axis in range(3):
            field = right[pl.ds(axis * plan.pad + plan.own(block), 1), :]
            start[axis][block] = field
            image[axis][block] = reach * field - rows[block, pl.ds(1 + axis, 1), :]
            whole[axis][block] = field + VISCOUS * image[axis][block]
            spot = where[pl.ds(axis * plan.pad + plan.own(block), 1), :]
            state[pl.ds((1 + axis) * plan.blocks + block, 1), :] = (
                reach * spot - rows[block, pl.ds(4 + axis, 1), :]
            )
    partials = []
    for axis in range(3):
        partials.append(dot(start[axis], start[axis]))
        partials.append(dot(start[axis], whole[axis]))
        partials.append(dot(whole[axis], whole[axis]))
    spread(plan, send, sum(image, []) + [pack(partials)])


def second_kernel(plan, recv, tiles, right, state, send, residual, direction, scalars, image, cols, rows):
    found = slots(plan)
    ring_into(plan, found, recv, 3, image)
    sums = totals(recv, 3 * plan.blocks, 9)
    for axis in range(3):
        current, curve, square = sums[3 * axis : 3 * axis + 3]
        alpha = current / curve
        following = jnp.maximum(alpha * alpha * square - current, 0.0)
        beta = following / current
        span = rows_of(plan, axis)
        field = right[span, :]
        left = field - alpha * (field + VISCOUS * image[span, :])
        residual[span, :] = left
        direction[span, :] = left + beta * field
        scalars[pl.ds(axis, 1), :] = jnp.broadcast_to(alpha, (1, LANES))
        for block in range(plan.blocks):
            at = 3 + axis * plan.blocks + block
            scalars[pl.ds(at, 1), :] = image[pl.ds(axis * plan.pad + plan.own(block), 1), :]
    apply_tiles(plan, tiles, [(direction, axis * plan.pad) for axis in range(3)], cols, 64)
    columns_to_rows(plan, cols, rows, 3)
    out = []
    partials = []
    for axis in range(3):
        left, ahead, shot, whole = [], [], [], []
        for block in range(plan.blocks):
            at = axis * plan.pad + plan.own(block)
            left.append(residual[pl.ds(at, 1), :])
            ahead.append(direction[pl.ds(at, 1), :])
            shot.append(state[pl.ds(block, 1), :] * ahead[block] - rows[block, pl.ds(axis, 1), :])
            whole.append(ahead[block] + VISCOUS * shot[block])
        out.extend(shot)
        partials.append(dot(left, left))
        partials.append(dot(ahead, whole))
        partials.append(dot(left, whole))
        partials.append(dot(whole, whole))
    spread(plan, send, out + [pack(partials)])


def third_kernel(
    plan, recv, tiles, where, right, residual, direction, state, scalars,
    send, ends, image, sofar, ahead, product, moved, cols, rows,
):
    found = slots(plan)
    ring_into(plan, found, recv, 3, image)
    sums = totals(recv, 3 * plan.blocks, 12)
    alphas = []
    left = []
    for axis in range(3):
        current, curve, cross, square = sums[4 * axis : 4 * axis + 4]
        alpha = current / curve
        following = jnp.maximum(current - 2.0 * alpha * cross + alpha * alpha * square, 0.0)
        beta = following / current
        alphas.append(alpha)
        span = rows_of(plan, axis)
        field = direction[span, :]
        rest = residual[span, :] - alpha * (field + VISCOUS * image[span, :])
        image[span, :] = rest
        fresh = rest + beta * field
        ahead[span, :] = fresh
        spot = where[span, :]
        product[span, :] = fresh * spot
        first = scalars[pl.ds(axis, 1), :]
        made = first * right[span, :] + alpha * field
        sofar[span, :] = made
        if axis == 0:
            carried = made * spot
        else:
            carried = carried + made * spot
    moved[rows_of(plan, 0), :] = carried
    fields = [(ahead, axis * plan.pad) for axis in range(3)]
    fields += [(product, axis * plan.pad) for axis in range(3)]
    fields += [(moved, 0)]
    apply_tiles(plan, tiles, fields, cols, 32)
    columns_to_rows(plan, cols, rows, 7)
    scale = 1.0 / plan.unit
    base = []
    each = [[None] * plan.blocks for _ in range(3)]
    rests = [[None] * plan.blocks for _ in range(3)]
    heads = [[None] * plan.blocks for _ in range(3)]
    wholes = [[None] * plan.blocks for _ in range(3)]
    for block in range(plan.blocks):
        reach = state[pl.ds(block, 1), :]
        own = plan.own(block)
        total = rows[block, pl.ds(6, 1), :] - reach * moved[pl.ds(own, 1), :]
        for axis in range(3):
            at = axis * plan.pad + own
            head = ahead[pl.ds(at, 1), :]
            spot = where[pl.ds(at, 1), :]
            lean = state[pl.ds((1 + axis) * plan.blocks + block, 1), :]
            shot = reach * head - rows[block, pl.ds(axis, 1), :]
            twice = reach * product[pl.ds(at, 1), :] - rows[block, pl.ds(3 + axis, 1), :]
            each[axis][block] = scale * (spot * shot + head * lean - twice)
            made = sofar[pl.ds(at, 1), :]
            first = scalars[pl.ds(axis, 1), :]
            before = scalars[pl.ds(3 + axis * plan.blocks + block, 1), :]
            latest = recv_own(plan, recv, found, axis, block)
            total = total + spot * (first * before + alphas[axis] * latest) + made * lean
            rests[axis][block] = image[pl.ds(at, 1), :]
            heads[axis][block] = head
            wholes[axis][block] = head + VISCOUS * shot
            ends[pl.ds(axis * plan.blocks + block, 1), :] = made
            ends[pl.ds((3 + axis) * plan.blocks + block, 1), :] = head
        base.append(scale * total)
    partials = []
    for axis in range(3):
        partials.append(dot(rests[axis], rests[axis]))
        partials.append(dot(heads[axis], wholes[axis]))
    spread(plan, send, base + sum(each, []) + [pack(partials)])


def recv_own(plan, recv, found, axis, block):
    return recv[found[13][0], axis * plan.blocks + block]


def fourth_kernel(plan, recv, tiles, ends, state, send, star, source, parts, cols, rows):
    found = slots(plan)
    ring_into(plan, found, recv, 4, parts)
    sums = totals(recv, 4 * plan.blocks, 6)
    gathered = parts[rows_of(plan, 0), :]
    for axis in range(3):
        alpha = sums[2 * axis] / sums[2 * axis + 1]
        gathered = gathered + alpha * parts[rows_of(plan, 1 + axis), :]
        for block in range(plan.blocks):
            star[axis, 0, 0, pl.ds(block, 1), :] = (
                ends[pl.ds(axis * plan.blocks + block, 1), :]
                + alpha * ends[pl.ds((3 + axis) * plan.blocks + block, 1), :]
            )
    source[rows_of(plan, 0), :] = -gathered
    apply_tiles(plan, tiles, [(source, 0)], cols, plan.width)
    columns_to_rows(plan, cols, rows, 1)
    field, shot, whole = [], [], []
    for block in range(plan.blocks):
        field.append(source[pl.ds(plan.own(block), 1), :])
        shot.append(state[pl.ds(block, 1), :] * field[block] - rows[block, pl.ds(0, 1), :])
        whole.append(STIFFNESS * field[block] + shot[block])
    spread(plan, send, shot + [pack([dot(field, field), dot(field, whole), dot(whole, whole)])])


def fifth_kernel(plan, recv, tiles, source, state, send, ends, image, ahead, cols, rows):
    found = slots(plan)
    ring_into(plan, found, recv, 1, image)
    current, curve, square = totals(recv, plan.blocks, 3)
    alpha = current / curve
    beta = jnp.maximum(alpha * alpha * square - current, 0.0) / current
    span = rows_of(plan, 0)
    field = source[span, :]
    left = field - alpha * (STIFFNESS * field + image[span, :])
    image[span, :] = left
    ahead[span, :] = left + beta * field
    apply_tiles(plan, tiles, [(ahead, 0)], cols, plan.width)
    columns_to_rows(plan, cols, rows, 1)
    rests, heads, wholes = [], [], []
    for block in range(plan.blocks):
        own = plan.own(block)
        rests.append(image[pl.ds(own, 1), :])
        heads.append(ahead[pl.ds(own, 1), :])
        shot = state[pl.ds(block, 1), :] * heads[block] - rows[block, pl.ds(0, 1), :]
        wholes.append(STIFFNESS * heads[block] + shot)
        ends[pl.ds(block, 1), :] = alpha * source[pl.ds(own, 1), :]
        ends[pl.ds(plan.blocks + block, 1), :] = heads[block]
    spread(plan, send, [pack([dot(rests, rests), dot(heads, wholes)])])


def last_kernel(plan, recv, ends, pressure):
    current, curve = totals(recv, 0, 2)
    alpha = current / curve
    for block in range(plan.blocks):
        pressure[0, 0, pl.ds(block, 1), :] = (
            ends[pl.ds(block, 1), :] + alpha * ends[pl.ds(plan.blocks + block, 1), :]
        )


def call(plan, kernel, operands, outs, scratch=(), smem=0):
    in_specs = [
        pl.BlockSpec(memory_space=pltpu.SMEM if i < smem else pltpu.VMEM)
        for i in range(len(operands))
    ]
    return pl.pallas_call(
        functools.partial(kernel, plan),
        out_shape=[jax.ShapeDtypeStruct(shape, jnp.float32) for shape in outs],
        in_specs=in_specs,
        out_specs=[pl.BlockSpec(memory_space=pltpu.VMEM) for _ in outs],
        scratch_shapes=[pltpu.VMEM(shape, jnp.float32) for shape in scratch],
        compiler_params=pltpu.CompilerParams(vmem_limit_bytes=48 * 1024 * 1024),
        name=kernel.__name__,
    )(*operands)


def local(mesh, offsets, velocity, counts, neighbours):
    blocks = counts.shape[2]
    width = offsets.shape[-1]
    plan = Plan(mesh, blocks, width)
    slot = lambda rows: (plan.devices, rows, 1, width)
    ring = lambda fields: (fields * plan.pad, width)
    cols = (blocks, width, LANES)
    rows = (blocks, 8, LANES)
    (send,) = call(plan, pack_kernel, [counts, offsets, velocity], [slot(6 * blocks)], smem=1)
    recv = exchange(send)
    send, tiles, where, right, state = call(
        plan, build_kernel, [recv],
        [slot(3 * blocks + 1), (27 * blocks, width, width), ring(3), ring(3), (4 * blocks, width)],
        [cols, rows],
    )
    recv = exchange(send)
    send, residual, direction, scalars = call(
        plan, second_kernel, [recv, tiles, right, state],
        [slot(3 * blocks + 1), ring(3), ring(3), (3 + 3 * blocks, width)],
        [ring(3), cols, rows],
    )
    recv = exchange(send)
    send, ends = call(
        plan, third_kernel, [recv, tiles, where, right, residual, direction, state, scalars],
        [slot(4 * blocks + 1), (6 * blocks, width)],
        [ring(3), ring(3), ring(3), ring(3), ring(1), cols, rows],
    )
    recv = exchange(send)
    send, star, source = call(
        plan, fourth_kernel, [recv, tiles, ends, state],
        [slot(blocks + 1), (3, 1, 1, blocks, width), ring(1)],
        [ring(4), cols, rows],
    )
    recv = exchange(send)
    send, ends = call(
        plan, fifth_kernel, [recv, tiles, source, state],
        [slot(1), (2 * blocks, width)],
        [ring(1), ring(1), cols, rows],
    )
    recv = exchange(send)
    (pressure,) = call(plan, last_kernel, [recv, ends], [(1, 1, blocks, width)])
    return star, pressure


def solution(mesh):
    in_specs = (
        P(None, "gx", "gy", "gz", None),
        P(None, "gx", "gy", "gz", None),
        P("gx", "gy", "gz"),
        P("gx", "gy", "gz", None),
    )
    out_specs = (P(None, "gx", "gy", "gz", None), P("gx", "gy", "gz", None))
    return jax.shard_map(
        functools.partial(local, mesh),
        mesh=mesh, in_specs=in_specs, out_specs=out_specs, check_vma=False,
    )
```

```python
import functools

import jax
import jax.numpy as jnp
from jax import lax
from jax.experimental import pallas as pl
from jax.experimental.pallas import tpu as pltpu
from jax.sharding import PartitionSpec as P

VISCOUS = 4.0
STIFFNESS = 0.25
GRAVITY_STEP = 0.5
AXES = ("gx", "gy", "gz")
FAR = 1.0e3
LANES = 128


def exchange(send):
    return lax.all_to_all(send, AXES, 0, 0, tiled=True)


class Plan:
    def __init__(self, mesh, blocks, width):
        self.count = [mesh.shape[axis] for axis in AXES]
        self.devices = self.count[0] * self.count[1] * self.count[2]
        self.blocks = blocks
        self.width = width
        self.deep = blocks + 2
        self.ring = 9 * self.deep
        self.cube = (2.0 / width) ** (1.0 / 3.0)
        self.unit = self.cube ** 0.5

    def own(self, block):
        return 4 * self.deep + block + 1


def slots(plan):
    place = [lax.axis_index(axis) for axis in AXES]
    found = {}
    for code in range(27):
        at = [place[0] + code // 9 - 1, place[1] + code // 3 % 3 - 1, place[2] + code % 3 - 1]
        present = None
        slot = 0
        for value, count in zip(at, plan.count):
            inside = jnp.logical_and(value >= 0, value < count)
            present = inside if present is None else jnp.logical_and(present, inside)
            slot = slot * count + jnp.clip(value, 0, count - 1)
        found[code] = (slot, present)
    return found


def gather_ring(plan, found, recv, fields, store):
    for column in range(9):
        for level in range(plan.deep):
            if level == 0:
                code, block = column * 3, plan.blocks - 1
            elif level == plan.deep - 1:
                code, block = column * 3 + 2, 0
            else:
                code, block = column * 3 + 1, level - 1
            slot, present = found[code]
            rows = [recv[slot, field * plan.blocks + block] for field in range(fields)]
            store(column * plan.deep + level, column, level, rows, present)


def ring_into(plan, found, recv, fields, ref):
    def store(at, column, level, rows, present):
        for field, row in enumerate(rows):
            ref[at, pl.ds(field, 1), :] = row

    gather_ring(plan, found, recv, fields, store)


def lane_ids(sublanes=1):
    return lax.broadcasted_iota(jnp.int32, (sublanes, LANES), 1)


def sublane_ids():
    return lax.broadcasted_iota(jnp.int32, (8, LANES), 0)


def totals(recv, row, number):
    summed = jnp.broadcast_to(jnp.sum(recv[:, row], axis=0), (8, LANES))
    place = lane_ids(8) - sublane_ids()
    return [
        jnp.broadcast_to(
            jnp.sum(jnp.where(place == 8 * m, summed, 0.0), axis=1, keepdims=True), (8, LANES)
        )
        for m in range(number)
    ]


def pack(groups):
    lane = lane_ids()
    row = jnp.zeros((1, LANES), jnp.float32)
    for m, group in enumerate(groups):
        for c, partial in enumerate(group):
            row = jnp.where(lane == 8 * m + c, jnp.sum(partial, axis=1, keepdims=True), row)
    return row


def dot(first, second):
    total = first[0] * second[0]
    for a, b in zip(first[1:], second[1:]):
        total = total + a * b
    return total


def spread(plan, send, rows):
    def body(slot, carry):
        for r, row in enumerate(rows):
            send[slot, r] = row
        return carry

    lax.fori_loop(0, plan.devices, body, 0)


def coarse(value):
    return value.astype(jnp.bfloat16).astype(jnp.float32)


def split(value):
    first = coarse(value)
    rest = value - first
    second = coarse(rest)
    return first, second, rest - second


def split_ring(plan, ref, packed):
    for at in range(plan.ring):
        first, second, third = split(ref[at])
        stacked = jnp.concatenate([first, second, third, jnp.zeros_like(third)], axis=0)
        packed[:, pl.ds(at * LANES, LANES)] = stacked.astype(jnp.bfloat16)


def tile_sum(plan, tiles, packed, block, column):
    ahead = packed[:, pl.ds((column * plan.deep + block) * LANES, 3 * LANES)]
    return jnp.dot(
        jnp.concatenate([ahead, ahead], axis=1),
        tiles[block * 9 + column],
        preferred_element_type=jnp.float32,
    )


def fold(total):
    return total[0:8] + total[8:16] + total[16:24]


def apply_tiles(plan, tiles, ring, packed, rows):
    split_ring(plan, ring, packed)
    for block in range(plan.blocks):
        total = tile_sum(plan, tiles, packed, block, 0)
        for column in range(1, 9):
            total = total + tile_sum(plan, tiles, packed, block, column)
        rows[block] = fold(total)


def pack_kernel(plan, counts, offsets, velocity, send):
    lane = lane_ids()
    rows = []
    for axis in range(3):
        for block in range(plan.blocks):
            valid = lane < counts[0, 0, block]
            row = offsets[axis * plan.blocks + block]
            rows.append(jnp.where(valid, row, FAR) if axis == 0 else row)
    for axis in range(3):
        for block in range(plan.blocks):
            valid = lane < counts[0, 0, block]
            row = velocity[axis * plan.blocks + block]
            if axis == 0:
                row = row + GRAVITY_STEP
            rows.append(jnp.where(valid, row, 0.0))
    spread(plan, send, rows)


def build_kernel(plan, recv, send, tiles, where, right, state, points, flipped, mixed, packed, rows):
    found = slots(plan)

    def store(at, column, level, got, present):
        shift = (column // 3 - 1, column % 3 - 1, level - (plan.deep - 1) // 2)
        spots = [plan.unit * (got[axis] + shift[axis]) for axis in range(3)]
        spots[0] = jnp.where(present, spots[0], FAR)
        points[at, pl.ds(3, 1), :] = spots[0] * spots[0] + spots[1] * spots[1] + spots[2] * spots[2]
        points[at, pl.ds(4, 1), :] = jnp.ones((1, LANES), jnp.float32)
        points[at, pl.ds(5, 3), :] = jnp.zeros((3, LANES), jnp.float32)
        mixed[at, pl.ds(3, 1), :] = jnp.ones((1, LANES), jnp.float32)
        mixed[at, pl.ds(7, 1), :] = jnp.zeros((1, LANES), jnp.float32)
        for axis in range(3):
            points[at, pl.ds(axis, 1), :] = spots[axis]
            where[at, pl.ds(axis, 1), :] = spots[axis]
            mixed[at, pl.ds(4 + axis, 1), :] = spots[axis]
            field = jnp.where(present, got[3 + axis], 0.0)
            right[at, pl.ds(axis, 1), :] = field
            mixed[at, pl.ds(axis, 1), :] = field

    gather_ring(plan, found, recv, 6, store)
    for at in range(plan.ring):
        first, second, third = split(points[at])
        stacked = jnp.concatenate([first, second, third, first, second, first], axis=0)
        padded = jnp.concatenate([stacked, jnp.zeros((LANES - 48, LANES), jnp.float32)], axis=0)
        flipped[pl.ds(at * plan.width, plan.width), :] = jnp.transpose(padded).astype(jnp.bfloat16)
    split_ring(plan, mixed, packed)
    sub = sublane_ids()
    for block in range(plan.blocks):
        own = points[plan.own(block)]
        own = jnp.where(jnp.logical_and(sub == 0, own > 0.25 * FAR), -FAR, own)
        square = jnp.broadcast_to(own[3:4], (8, LANES))
        own = jnp.where(sub < 3, 2.0 * own, 0.0)
        own = jnp.where(sub == 3, -1.0, own)
        own = jnp.where(sub == 4, plan.cube - square, own)
        first, second, third = split(own)
        stacked = jnp.concatenate([first, first, first, second, second, third], axis=0)
        padded = jnp.concatenate([stacked, jnp.zeros((LANES - 48, LANES), jnp.float32)], axis=0)
        centre = padded.astype(jnp.bfloat16)
        total = None
        for column in range(9):
            at = (column * plan.deep + block) * plan.width
            rest = jnp.dot(
                flipped[pl.ds(at, 3 * plan.width), :], centre, preferred_element_type=jnp.float32
            )
            bump = jnp.maximum(rest, 0.0)
            weight = bump * bump * bump
            high = weight.astype(jnp.bfloat16)
            tiles[block * 9 + column, pl.ds(0, 3 * plan.width), :] = high
            tiles[block * 9 + column, pl.ds(3 * plan.width, 3 * plan.width), :] = (
                weight - high.astype(jnp.float32)
            ).astype(jnp.bfloat16)
            part = tile_sum(plan, tiles, packed, block, column)
            total = part if total is None else total + part
        rows[block] = fold(total)
    image = [[None] * plan.blocks for _ in range(3)]
    whole = [[None] * plan.blocks for _ in range(3)]
    start = [[None] * plan.blocks for _ in range(3)]
    for block in range(plan.blocks):
        own = plan.own(block)
        reach = rows[block, pl.ds(3, 1), :]
        state[pl.ds(block, 1), :] = reach
        for axis in range(3):
            field = right[own, pl.ds(axis, 1), :]
            start[axis][block] = field
            image[axis][block] = reach * field - rows[block, pl.ds(axis, 1), :]
            whole[axis][block] = field + VISCOUS * image[axis][block]
            spot = where[own, pl.ds(axis, 1), :]
            state[pl.ds((1 + axis) * plan.blocks + block, 1), :] = (
                reach * spot - rows[block, pl.ds(4 + axis, 1), :]
            )
    groups = [
        [dot(start[axis], start[axis]) for axis in range(3)],
        [dot(start[axis], whole[axis]) for axis in range(3)],
        [dot(whole[axis], whole[axis]) for axis in range(3)],
    ]
    spread(plan, send, sum(image, []) + [pack(groups)])


def second_kernel(plan, recv, tiles, right, state, send, residual, direction, scalars, image, packed, rows):
    found = slots(plan)
    ring_into(plan, found, recv, 3, image)
    current, curve, square = totals(recv, 3 * plan.blocks, 3)
    alpha = current / curve
    following = jnp.maximum(alpha * alpha * square - current, 0.0)
    beta = following / current
    for at in range(plan.ring):
        field = right[at]
        left = field - alpha * (field + VISCOUS * image[at])
        residual[at] = left
        direction[at] = left + beta * field
    scalars[plan.blocks] = alpha
    for block in range(plan.blocks):
        scalars[block] = image[plan.own(block)]
    apply_tiles(plan, tiles, direction, packed, rows)
    out = []
    groups = [[], [], [], []]
    for axis in range(3):
        left, ahead, shot, whole = [], [], [], []
        for block in range(plan.blocks):
            own = plan.own(block)
            left.append(residual[own, pl.ds(axis, 1), :])
            ahead.append(direction[own, pl.ds(axis, 1), :])
            shot.append(state[pl.ds(block, 1), :] * ahead[block] - rows[block, pl.ds(axis, 1), :])
            whole.append(ahead[block] + VISCOUS * shot[block])
        out.extend(shot)
        groups[0].append(dot(left, left))
        groups[1].append(dot(ahead, whole))
        groups[2].append(dot(left, whole))
        groups[3].append(dot(whole, whole))
    spread(plan, send, out + [pack(groups)])


def third_kernel(
    plan, recv, tiles, where, right, residual, direction, state, scalars,
    send, ends, image, sofar, ahead, steps, packed, rows,
):
    found = slots(plan)
    ring_into(plan, found, recv, 3, image)
    current, curve, cross, square = totals(recv, 3 * plan.blocks, 4)
    alpha = current / curve
    following = jnp.maximum(current - 2.0 * alpha * cross + alpha * alpha * square, 0.0)
    beta = following / current
    first = scalars[plan.blocks]
    steps[...] = alpha
    sub = sublane_ids()
    for block in range(plan.blocks):
        own = plan.own(block)
        rows[block] = first * scalars[block] + alpha * image[own]
    latest = [
        [rows[block, pl.ds(axis, 1), :] for axis in range(3)] for block in range(plan.blocks)
    ]
    for at in range(plan.ring):
        field = direction[at]
        rest = residual[at] - alpha * (field + VISCOUS * image[at])
        fresh = rest + beta * field
        spot = where[at]
        made = first * right[at] + alpha * field
        moved = made * spot
        moved = pltpu.roll(moved, 6, 0) + pltpu.roll(moved, 5, 0) + pltpu.roll(moved, 4, 0)
        joined = jnp.where(sub < 3, fresh, pltpu.roll(fresh * spot, 3, 0))
        ahead[at] = jnp.where(sub < 6, joined, moved)
        if at - plan.own(0) in range(plan.blocks):
            image[at] = rest
            sofar[at - plan.own(0)] = made
    apply_tiles(plan, tiles, ahead, packed, rows)
    scale = 1.0 / plan.unit
    base = []
    each = [[None] * plan.blocks for _ in range(3)]
    rests = [[None] * plan.blocks for _ in range(3)]
    heads = [[None] * plan.blocks for _ in range(3)]
    wholes = [[None] * plan.blocks for _ in range(3)]
    for block in range(plan.blocks):
        reach = state[pl.ds(block, 1), :]
        own = plan.own(block)
        total = rows[block, pl.ds(6, 1), :] - reach * ahead[own, pl.ds(6, 1), :]
        for axis in range(3):
            head = ahead[own, pl.ds(axis, 1), :]
            spot = where[own, pl.ds(axis, 1), :]
            lean = state[pl.ds((1 + axis) * plan.blocks + block, 1), :]
            shot = reach * head - rows[block, pl.ds(axis, 1), :]
            twice = reach * ahead[own, pl.ds(3 + axis, 1), :] - rows[block, pl.ds(3 + axis, 1), :]
            each[axis][block] = scale * (spot * shot + head * lean - twice)
            made = sofar[block, pl.ds(axis, 1), :]
            total = total + spot * latest[block][axis] + made * lean
            rests[axis][block] = image[own, pl.ds(axis, 1), :]
            heads[axis][block] = head
            wholes[axis][block] = head + VISCOUS * shot
            ends[pl.ds(axis * plan.blocks + block, 1), :] = made
            ends[pl.ds((3 + axis) * plan.blocks + block, 1), :] = head
        base.append(scale * total)
    groups = [
        [dot(rests[axis], rests[axis]) for axis in range(3)],
        [dot(heads[axis], wholes[axis]) for axis in range(3)],
    ]
    spread(plan, send, base + sum(each, []) + [pack(groups)])


def fourth_kernel(plan, recv, tiles, ends, state, send, star, source, parts, steps, packed, rows):
    found = slots(plan)
    ring_into(plan, found, recv, 4, parts)
    current, curve = totals(recv, 4 * plan.blocks, 2)
    sub = sublane_ids()
    steps[...] = current / curve
    factor = jnp.where(sub == 0, 1.0, pltpu.roll(steps[...], 1, 0))
    for at in range(plan.ring):
        gathered = jnp.where(sub < 4, parts[at] * factor, 0.0)
        source[at] = jnp.broadcast_to(-jnp.sum(gathered, axis=0, keepdims=True), (8, LANES))
    for axis in range(3):
        alpha = steps[pl.ds(axis, 1), :]
        for block in range(plan.blocks):
            star[axis * plan.blocks + block] = (
                ends[pl.ds(axis * plan.blocks + block, 1), :]
                + alpha * ends[pl.ds((3 + axis) * plan.blocks + block, 1), :]
            )
    apply_tiles(plan, tiles, source, packed, rows)
    field, shot, whole = [], [], []
    for block in range(plan.blocks):
        field.append(source[plan.own(block), pl.ds(0, 1), :])
        shot.append(state[pl.ds(block, 1), :] * field[block] - rows[block, pl.ds(0, 1), :])
        whole.append(STIFFNESS * field[block] + shot[block])
    groups = [[dot(field, field)], [dot(field, whole)], [dot(whole, whole)]]
    spread(plan, send, shot + [pack(groups)])


def fifth_kernel(plan, recv, tiles, source, state, send, ends, image, ahead, steps, packed, rows):
    found = slots(plan)
    ring_into(plan, found, recv, 1, image)
    current, curve, square = totals(recv, plan.blocks, 3)
    steps[...] = current / curve
    alpha = steps[pl.ds(0, 1), :]
    steps[...] = jnp.maximum(alpha * alpha * square - current, 0.0) / current
    beta = steps[pl.ds(0, 1), :]
    for at in range(plan.ring):
        field = source[at]
        left = field - alpha * (STIFFNESS * field + image[at])
        image[at] = left
        ahead[at] = left + beta * field
    apply_tiles(plan, tiles, ahead, packed, rows)
    rests, heads, wholes = [], [], []
    for block in range(plan.blocks):
        own = plan.own(block)
        rests.append(image[own, pl.ds(0, 1), :])
        heads.append(ahead[own, pl.ds(0, 1), :])
        shot = state[pl.ds(block, 1), :] * heads[block] - rows[block, pl.ds(0, 1), :]
        wholes.append(STIFFNESS * heads[block] + shot)
        ends[pl.ds(block, 1), :] = alpha * source[own, pl.ds(0, 1), :]
        ends[pl.ds(plan.blocks + block, 1), :] = heads[block]
    spread(plan, send, [pack([[dot(rests, rests)], [dot(heads, wholes)]])])


def last_kernel(plan, recv, ends, pressure, steps):
    current, curve = totals(recv, 0, 2)
    steps[...] = current / curve
    alpha = steps[pl.ds(0, 1), :]
    for block in range(plan.blocks):
        pressure[block] = (
            ends[pl.ds(block, 1), :] + alpha * ends[pl.ds(plan.blocks + block, 1), :]
        )


def call(plan, kernel, operands, outs, scratch=(), smem=0):
    in_specs = [
        pl.BlockSpec(memory_space=pltpu.SMEM if i < smem else pltpu.VMEM)
        for i in range(len(operands))
    ]
    typed = lambda shape: (shape, jnp.float32) if isinstance(shape[0], int) else shape
    return pl.pallas_call(
        functools.partial(kernel, plan),
        out_shape=[jax.ShapeDtypeStruct(*typed(shape)) for shape in outs],
        in_specs=in_specs,
        out_specs=[pl.BlockSpec(memory_space=pltpu.VMEM) for _ in outs],
        scratch_shapes=[pltpu.VMEM(*typed(shape)) for shape in scratch],
        compiler_params=pltpu.CompilerParams(vmem_limit_bytes=24 * 1024 * 1024),
        name=kernel.__name__,
    )(*operands)


def local(mesh, offsets, velocity, counts, neighbours):
    blocks = counts.shape[2]
    width = offsets.shape[-1]
    plan = Plan(mesh, blocks, width)
    lined = lambda field: field.transpose(0, 1, 3, 2, 4).reshape(3 * blocks, 1, width)
    slot = lambda rows: (plan.devices, rows, 1, width)
    ring = (plan.ring, 8, width)
    tile = (8, width)
    rows = (blocks, 8, width)
    packed = ((32, plan.ring * width), jnp.bfloat16)
    (send,) = call(
        plan, pack_kernel, [counts, lined(offsets), lined(velocity)], [slot(6 * blocks)], smem=1
    )
    recv = exchange(send)
    send, tiles, where, right, state = call(
        plan, build_kernel, [recv],
        [
            slot(3 * blocks + 1), ((9 * blocks, 6 * width, width), jnp.bfloat16),
            ring, ring, (4 * blocks, width),
        ],
        [ring, ((plan.ring * width, LANES), jnp.bfloat16), ring, packed, rows],
    )
    recv = exchange(send)
    send, residual, direction, scalars = call(
        plan, second_kernel, [recv, tiles, right, state],
        [slot(3 * blocks + 1), ring, ring, (blocks + 1, 8, width)],
        [ring, packed, rows],
    )
    recv = exchange(send)
    send, ends = call(
        plan, third_kernel, [recv, tiles, where, right, residual, direction, state, scalars],
        [slot(4 * blocks + 1), (6 * blocks, width)],
        [ring, rows, ring, tile, packed, rows],
    )
    recv = exchange(send)
    send, star, source = call(
        plan, fourth_kernel, [recv, tiles, ends, state],
        [slot(blocks + 1), (3 * blocks, 1, width), ring],
        [ring, tile, packed, rows],
    )
    recv = exchange(send)
    send, ends = call(
        plan, fifth_kernel, [recv, tiles, source, state],
        [slot(1), (2 * blocks, width)],
        [ring, ring, tile, packed, rows],
    )
    recv = exchange(send)
    (pressure,) = call(plan, last_kernel, [recv, ends], [(blocks, 1, width)], [tile])
    star = star.reshape(3, 1, blocks, 1, width).transpose(0, 1, 3, 2, 4)
    pressure = pressure.reshape(1, blocks, 1, width).transpose(0, 2, 1, 3)
    return star, pressure


def solution(mesh):
    in_specs = (
        P(None, "gx", "gy", "gz", None),
        P(None, "gx", "gy", "gz", None),
        P("gx", "gy", "gz"),
        P("gx", "gy", "gz", None),
    )
    out_specs = (P(None, "gx", "gy", "gz", None), P("gx", "gy", "gz", None))
    return jax.shard_map(
        functools.partial(local, mesh),
        mesh=mesh, in_specs=in_specs, out_specs=out_specs, check_vma=False,
    )
```

```python
import functools

import jax
import jax.numpy as jnp
from jax import lax
from jax.experimental import pallas as pl
from jax.experimental.pallas import tpu as pltpu
from jax.sharding import PartitionSpec as P

VISCOUS = 4.0
STIFFNESS = 0.25
GRAVITY_STEP = 0.5
AXES = ("gx", "gy", "gz")
FAR = 1.0e3
LANES = 128


def exchange(send):
    return lax.all_to_all(send, AXES, 0, 0, tiled=True)


def exchange_layers(plan, send):
    level = lax.all_to_all(send, AXES[:2], 0, 0, tiled=True)
    deep = plan.count[2]
    if deep == 2:
        return [level, lax.ppermute(level, AXES[2], [(0, 1), (1, 0)])]
    forward = [(i, i + 1) for i in range(deep - 1)]
    backward = [(target, source) for source, target in forward]
    return [level] + [lax.ppermute(level, AXES[2], pairs) for pairs in (forward, backward)]


class Plan:
    def __init__(self, mesh, blocks, width):
        self.count = [mesh.shape[axis] for axis in AXES]
        self.devices = self.count[0] * self.count[1] * self.count[2]
        self.blocks = blocks
        self.width = width
        self.deep = blocks + 2
        self.ring = 9 * self.deep
        self.cube = (2.0 / width) ** (1.0 / 3.0)
        self.unit = self.cube ** 0.5

    def own(self, block):
        return 4 * self.deep + block + 1


def slots(plan, axes=3):
    place = [lax.axis_index(axis) for axis in AXES]
    found = {}
    for code in range(27):
        at = [place[0] + code // 9 - 1, place[1] + code // 3 % 3 - 1, place[2] + code % 3 - 1]
        present = None
        slot = 0
        for axis, (value, count) in enumerate(zip(at, plan.count)):
            inside = jnp.logical_and(value >= 0, value < count)
            present = inside if present is None else jnp.logical_and(present, inside)
            if axis < axes:
                slot = slot * count + jnp.clip(value, 0, count - 1)
        found[code] = (slot, present)
    return found


def gather_ring(plan, found, layers, fields, store):
    for column in range(9):
        for level in range(plan.deep):
            if level == 0:
                step, block = 0, plan.blocks - 1
            elif level == plan.deep - 1:
                step, block = 2, 0
            else:
                step, block = 1, level - 1
            slot, present = found[column * 3 + step]
            rows = [layers[step][slot, field * plan.blocks + block] for field in range(fields)]
            store(column * plan.deep + level, column, level, rows, present)


def ring_into(plan, found, recv, fields, ref):
    def store(at, column, level, rows, present):
        for field, row in enumerate(rows):
            ref[at, pl.ds(field, 1), :] = row

    gather_ring(plan, found, [recv] * 3, fields, store)


def lane_ids(sublanes=1):
    return lax.broadcasted_iota(jnp.int32, (sublanes, LANES), 1)


def sublane_ids():
    return lax.broadcasted_iota(jnp.int32, (8, LANES), 0)


def totals(recv, row, number):
    summed = jnp.broadcast_to(jnp.sum(recv[:, row], axis=0), (8, LANES))
    place = lane_ids(8) - sublane_ids()
    return [
        jnp.broadcast_to(
            jnp.sum(jnp.where(place == 8 * m, summed, 0.0), axis=1, keepdims=True), (8, LANES)
        )
        for m in range(number)
    ]


def pack(groups):
    lane = lane_ids()
    row = jnp.zeros((1, LANES), jnp.float32)
    for m, group in enumerate(groups):
        for c, partial in enumerate(group):
            row = jnp.where(lane == 8 * m + c, jnp.sum(partial, axis=1, keepdims=True), row)
    return row


def dot(first, second):
    total = first[0] * second[0]
    for a, b in zip(first[1:], second[1:]):
        total = total + a * b
    return total


def spread(send, rows):
    def body(slot, carry):
        for r, row in enumerate(rows):
            send[slot, r] = row
        return carry

    lax.fori_loop(0, send.shape[0], body, 0, unroll=4)


def coarse(value):
    return value.astype(jnp.bfloat16).astype(jnp.float32)


def split(value):
    first = coarse(value)
    rest = value - first
    second = coarse(rest)
    return first, second, rest - second


def split_ring(plan, ref, packed):
    for at in range(plan.ring):
        first, second, third = split(ref[at])
        stacked = jnp.concatenate([first, second, third, jnp.zeros_like(third)], axis=0)
        packed[:, pl.ds(at * LANES, LANES)] = stacked.astype(jnp.bfloat16)


def tile_sum(plan, tiles, packed, block, column):
    ahead = packed[:, pl.ds((column * plan.deep + block) * LANES, 3 * LANES)]
    return jnp.dot(
        jnp.concatenate([ahead, ahead], axis=1),
        tiles[block * 9 + column],
        preferred_element_type=jnp.float32,
    )


def fold(total):
    return total[0:8] + total[8:16] + total[16:24]


def apply_tiles(plan, tiles, ring, packed, rows):
    split_ring(plan, ring, packed)
    for block in range(plan.blocks):
        total = tile_sum(plan, tiles, packed, block, 0)
        for column in range(1, 9):
            total = total + tile_sum(plan, tiles, packed, block, column)
        rows[block] = fold(total)


def pack_kernel(plan, counts_in, offsets_in, velocity_in, send, counts, offsets, velocity, sems):
    pairs = [(counts_in, counts), (offsets_in, offsets), (velocity_in, velocity)]
    copies = [pltpu.make_async_copy(a, b, sems.at[i]) for i, (a, b) in enumerate(pairs)]
    for copy in copies:
        copy.start()
    for copy in copies:
        copy.wait()
    lane = lane_ids()
    rows = []
    for axis in range(3):
        for block in range(plan.blocks):
            valid = lane < counts[0, block]
            row = offsets[axis * plan.blocks + block]
            rows.append(jnp.where(valid, row, FAR) if axis == 0 else row)
    for axis in range(3):
        for block in range(plan.blocks):
            valid = lane < counts[0, block]
            row = velocity[axis * plan.blocks + block]
            if axis == 0:
                row = row + GRAVITY_STEP
            rows.append(jnp.where(valid, row, 0.0))
    spread(send, rows)


def build_kernel(plan, *refs):
    level, others = refs[0], refs[1:-10]
    send, tiles, where, right, state, points, flipped, mixed, packed, rows = refs[-10:]
    layers = [others[0], level, others[-1]]
    found = slots(plan, 2)

    def store(at, column, level, got, present):
        shift = (column // 3 - 1, column % 3 - 1, level - (plan.deep - 1) // 2)
        spots = [plan.unit * (got[axis] + shift[axis]) for axis in range(3)]
        spots[0] = jnp.where(present, spots[0], FAR)
        points[at, pl.ds(3, 1), :] = spots[0] * spots[0] + spots[1] * spots[1] + spots[2] * spots[2]
        points[at, pl.ds(4, 1), :] = jnp.ones((1, LANES), jnp.float32)
        points[at, pl.ds(5, 3), :] = jnp.zeros((3, LANES), jnp.float32)
        mixed[at, pl.ds(3, 1), :] = jnp.ones((1, LANES), jnp.float32)
        mixed[at, pl.ds(7, 1), :] = jnp.zeros((1, LANES), jnp.float32)
        for axis in range(3):
            points[at, pl.ds(axis, 1), :] = spots[axis]
            where[at, pl.ds(axis, 1), :] = spots[axis]
            mixed[at, pl.ds(4 + axis, 1), :] = spots[axis]
            field = jnp.where(present, got[3 + axis], 0.0)
            right[at, pl.ds(axis, 1), :] = field
            mixed[at, pl.ds(axis, 1), :] = field

    gather_ring(plan, found, layers, 6, store)
    for at in range(plan.ring):
        first, second, third = split(points[at])
        stacked = jnp.concatenate([first, second, third, first, second, first], axis=0)
        padded = jnp.concatenate([stacked, jnp.zeros((LANES - 48, LANES), jnp.float32)], axis=0)
        flipped[pl.ds(at * plan.width, plan.width), :] = jnp.transpose(padded).astype(jnp.bfloat16)
    split_ring(plan, mixed, packed)
    sub = sublane_ids()
    for block in range(plan.blocks):
        own = points[plan.own(block)]
        own = jnp.where(jnp.logical_and(sub == 0, own > 0.25 * FAR), -FAR, own)
        square = jnp.broadcast_to(own[3:4], (8, LANES))
        own = jnp.where(sub < 3, 2.0 * own, 0.0)
        own = jnp.where(sub == 3, -1.0, own)
        own = jnp.where(sub == 4, plan.cube - square, own)
        first, second, third = split(own)
        stacked = jnp.concatenate([first, first, first, second, second, third], axis=0)
        padded = jnp.concatenate([stacked, jnp.zeros((LANES - 48, LANES), jnp.float32)], axis=0)
        centre = padded.astype(jnp.bfloat16)
        total = None
        for column in range(9):
            at = (column * plan.deep + block) * plan.width
            rest = jnp.dot(
                flipped[pl.ds(at, 3 * plan.width), :], centre, preferred_element_type=jnp.float32
            )
            bump = jnp.maximum(rest, 0.0)
            weight = bump * bump * bump
            high = weight.astype(jnp.bfloat16)
            tiles[block * 9 + column, pl.ds(0, 3 * plan.width), :] = high
            tiles[block * 9 + column, pl.ds(3 * plan.width, 3 * plan.width), :] = (
                weight - high.astype(jnp.float32)
            ).astype(jnp.bfloat16)
            part = tile_sum(plan, tiles, packed, block, column)
            total = part if total is None else total + part
        rows[block] = fold(total)
    image = [[None] * plan.blocks for _ in range(3)]
    whole = [[None] * plan.blocks for _ in range(3)]
    start = [[None] * plan.blocks for _ in range(3)]
    for block in range(plan.blocks):
        own = plan.own(block)
        reach = rows[block, pl.ds(3, 1), :]
        state[pl.ds(block, 1), :] = reach
        for axis in range(3):
            field = right[own, pl.ds(axis, 1), :]
            start[axis][block] = field
            image[axis][block] = reach * field - rows[block, pl.ds(axis, 1), :]
            whole[axis][block] = field + VISCOUS * image[axis][block]
            spot = where[own, pl.ds(axis, 1), :]
            state[pl.ds((1 + axis) * plan.blocks + block, 1), :] = (
                reach * spot - rows[block, pl.ds(4 + axis, 1), :]
            )
    groups = [
        [dot(start[axis], start[axis]) for axis in range(3)],
        [dot(start[axis], whole[axis]) for axis in range(3)],
        [dot(whole[axis], whole[axis]) for axis in range(3)],
    ]
    spread(send, sum(image, []) + [pack(groups)])


def second_kernel(plan, recv, tiles, right, state, send, residual, direction, scalars, image, packed, rows):
    found = slots(plan)
    ring_into(plan, found, recv, 3, image)
    current, curve, square = totals(recv, 3 * plan.blocks, 3)
    alpha = current / curve
    following = jnp.maximum(alpha * alpha * square - current, 0.0)
    beta = following / current
    for at in range(plan.ring):
        field = right[at]
        left = field - alpha * (field + VISCOUS * image[at])
        residual[at] = left
        direction[at] = left + beta * field
    scalars[plan.blocks] = alpha
    for block in range(plan.blocks):
        scalars[block] = image[plan.own(block)]
    apply_tiles(plan, tiles, direction, packed, rows)
    out = []
    groups = [[], [], [], []]
    for axis in range(3):
        left, ahead, shot, whole = [], [], [], []
        for block in range(plan.blocks):
            own = plan.own(block)
            left.append(residual[own, pl.ds(axis, 1), :])
            ahead.append(direction[own, pl.ds(axis, 1), :])
            shot.append(state[pl.ds(block, 1), :] * ahead[block] - rows[block, pl.ds(axis, 1), :])
            whole.append(ahead[block] + VISCOUS * shot[block])
        out.extend(shot)
        groups[0].append(dot(left, left))
        groups[1].append(dot(ahead, whole))
        groups[2].append(dot(left, whole))
        groups[3].append(dot(whole, whole))
    spread(send, out + [pack(groups)])


def third_kernel(
    plan, recv, tiles, where, right, residual, direction, state, scalars,
    send, ends, image, sofar, ahead, steps, packed, rows,
):
    found = slots(plan)
    ring_into(plan, found, recv, 3, image)
    current, curve, cross, square = totals(recv, 3 * plan.blocks, 4)
    alpha = current / curve
    following = jnp.maximum(current - 2.0 * alpha * cross + alpha * alpha * square, 0.0)
    beta = following / current
    first = scalars[plan.blocks]
    steps[...] = alpha
    sub = sublane_ids()
    for block in range(plan.blocks):
        own = plan.own(block)
        rows[block] = first * scalars[block] + alpha * image[own]
    latest = [
        [rows[block, pl.ds(axis, 1), :] for axis in range(3)] for block in range(plan.blocks)
    ]
    for at in range(plan.ring):
        field = direction[at]
        rest = residual[at] - alpha * (field + VISCOUS * image[at])
        fresh = rest + beta * field
        spot = where[at]
        made = first * right[at] + alpha * field
        moved = made * spot
        moved = pltpu.roll(moved, 6, 0) + pltpu.roll(moved, 5, 0) + pltpu.roll(moved, 4, 0)
        joined = jnp.where(sub < 3, fresh, pltpu.roll(fresh * spot, 3, 0))
        ahead[at] = jnp.where(sub < 6, joined, moved)
        if at - plan.own(0) in range(plan.blocks):
            image[at] = rest
            sofar[at - plan.own(0)] = made
    apply_tiles(plan, tiles, ahead, packed, rows)
    scale = 1.0 / plan.unit
    base = []
    each = [[None] * plan.blocks for _ in range(3)]
    rests = [[None] * plan.blocks for _ in range(3)]
    heads = [[None] * plan.blocks for _ in range(3)]
    wholes = [[None] * plan.blocks for _ in range(3)]
    for block in range(plan.blocks):
        reach = state[pl.ds(block, 1), :]
        own = plan.own(block)
        total = rows[block, pl.ds(6, 1), :] - reach * ahead[own, pl.ds(6, 1), :]
        for axis in range(3):
            head = ahead[own, pl.ds(axis, 1), :]
            spot = where[own, pl.ds(axis, 1), :]
            lean = state[pl.ds((1 + axis) * plan.blocks + block, 1), :]
            shot = reach * head - rows[block, pl.ds(axis, 1), :]
            twice = reach * ahead[own, pl.ds(3 + axis, 1), :] - rows[block, pl.ds(3 + axis, 1), :]
            each[axis][block] = scale * (spot * shot + head * lean - twice)
            made = sofar[block, pl.ds(axis, 1), :]
            total = total + spot * latest[block][axis] + made * lean
            rests[axis][block] = image[own, pl.ds(axis, 1), :]
            heads[axis][block] = head
            wholes[axis][block] = head + VISCOUS * shot
            ends[pl.ds(axis * plan.blocks + block, 1), :] = made
            ends[pl.ds((3 + axis) * plan.blocks + block, 1), :] = head
        base.append(scale * total)
    groups = [
        [dot(rests[axis], rests[axis]) for axis in range(3)],
        [dot(heads[axis], wholes[axis]) for axis in range(3)],
    ]
    spread(send, base + sum(each, []) + [pack(groups)])


def fourth_kernel(plan, recv, tiles, state, send, source, steps, parts, packed, rows):
    found = slots(plan)
    ring_into(plan, found, recv, 4, parts)
    current, curve = totals(recv, 4 * plan.blocks, 2)
    sub = sublane_ids()
    steps[...] = current / curve
    factor = jnp.where(sub == 0, 1.0, pltpu.roll(steps[...], 1, 0))
    for at in range(plan.ring):
        gathered = jnp.where(sub < 4, parts[at] * factor, 0.0)
        source[at] = jnp.broadcast_to(-jnp.sum(gathered, axis=0, keepdims=True), (8, LANES))
    apply_tiles(plan, tiles, source, packed, rows)
    field, shot, whole = [], [], []
    for block in range(plan.blocks):
        field.append(source[plan.own(block), pl.ds(0, 1), :])
        shot.append(state[pl.ds(block, 1), :] * field[block] - rows[block, pl.ds(0, 1), :])
        whole.append(STIFFNESS * field[block] + shot[block])
    groups = [[dot(field, field)], [dot(field, whole)], [dot(whole, whole)]]
    spread(send, shot + [pack(groups)])


def fifth_kernel(plan, recv, tiles, source, state, send, ends, image, ahead, steps, packed, rows):
    found = slots(plan)
    ring_into(plan, found, recv, 1, image)
    current, curve, square = totals(recv, plan.blocks, 3)
    steps[...] = current / curve
    alpha = steps[pl.ds(0, 1), :]
    steps[...] = jnp.maximum(alpha * alpha * square - current, 0.0) / current
    beta = steps[pl.ds(0, 1), :]
    for at in range(plan.ring):
        field = source[at]
        left = field - alpha * (STIFFNESS * field + image[at])
        image[at] = left
        ahead[at] = left + beta * field
    apply_tiles(plan, tiles, ahead, packed, rows)
    rests, heads, wholes = [], [], []
    for block in range(plan.blocks):
        own = plan.own(block)
        rests.append(image[own, pl.ds(0, 1), :])
        heads.append(ahead[own, pl.ds(0, 1), :])
        shot = state[pl.ds(block, 1), :] * heads[block] - rows[block, pl.ds(0, 1), :]
        wholes.append(STIFFNESS * heads[block] + shot)
        ends[pl.ds(block, 1), :] = alpha * source[own, pl.ds(0, 1), :]
        ends[pl.ds(plan.blocks + block, 1), :] = heads[block]
    spread(send, [pack([[dot(rests, rests)], [dot(heads, wholes)]])])


def last_kernel(plan, recv, speeds, final, ends, star, pressure, steps):
    current, curve = totals(recv, 0, 2)
    steps[...] = current / curve
    alpha = steps[pl.ds(0, 1), :]
    for block in range(plan.blocks):
        pressure[block] = (
            ends[pl.ds(block, 1), :] + alpha * ends[pl.ds(plan.blocks + block, 1), :]
        )
    for axis in range(3):
        alpha = final[pl.ds(axis, 1), :]
        for block in range(plan.blocks):
            at = axis * plan.blocks + block
            star[at] = (
                speeds[pl.ds(at, 1), :] + alpha * speeds[pl.ds(3 * plan.blocks + at, 1), :]
            )


def call(plan, kernel, operands, outs, scratch=(), space=pltpu.VMEM):
    typed = lambda shape: (shape, jnp.float32) if isinstance(shape[0], int) else shape
    held = lambda item: pltpu.VMEM(*typed(item)) if isinstance(item, tuple) else item
    return pl.pallas_call(
        functools.partial(kernel, plan),
        out_shape=[jax.ShapeDtypeStruct(*typed(shape)) for shape in outs],
        in_specs=[pl.BlockSpec(memory_space=space) for _ in operands],
        out_specs=[pl.BlockSpec(memory_space=pltpu.VMEM) for _ in outs],
        scratch_shapes=[held(item) for item in scratch],
        compiler_params=pltpu.CompilerParams(vmem_limit_bytes=24 * 1024 * 1024),
        name=kernel.__name__,
    )(*operands)


def local(mesh, offsets, velocity, counts, neighbours):
    blocks = counts.shape[2]
    width = offsets.shape[-1]
    plan = Plan(mesh, blocks, width)
    lined = lambda field: field.transpose(0, 1, 3, 2, 4).reshape(3 * blocks, 1, width)
    slot = lambda rows: (plan.devices, rows, 1, width)
    ring = (plan.ring, 8, width)
    tile = (8, width)
    rows = (blocks, 8, width)
    packed = ((32, plan.ring * width), jnp.bfloat16)
    (send,) = call(
        plan, pack_kernel, [counts.reshape(1, blocks), lined(offsets), lined(velocity)],
        [(plan.count[0] * plan.count[1], 6 * blocks, 1, width)],
        [
            pltpu.SMEM((1, blocks), jnp.int32), (3 * blocks, 1, width), (3 * blocks, 1, width),
            pltpu.SemaphoreType.DMA((3,)),
        ],
        pltpu.HBM,
    )
    send, tiles, where, right, state = call(
        plan, build_kernel, exchange_layers(plan, send),
        [
            slot(3 * blocks + 1), ((9 * blocks, 6 * width, width), jnp.bfloat16),
            ring, ring, (4 * blocks, width),
        ],
        [ring, ((plan.ring * width, LANES), jnp.bfloat16), ring, packed, rows],
    )
    recv = exchange(send)
    send, residual, direction, scalars = call(
        plan, second_kernel, [recv, tiles, right, state],
        [slot(3 * blocks + 1), ring, ring, (blocks + 1, 8, width)],
        [ring, packed, rows],
    )
    recv = exchange(send)
    send, speeds = call(
        plan, third_kernel, [recv, tiles, where, right, residual, direction, state, scalars],
        [slot(4 * blocks + 1), (6 * blocks, width)],
        [ring, rows, ring, tile, packed, rows],
    )
    recv = exchange(send)
    send, source, final = call(
        plan, fourth_kernel, [recv, tiles, state],
        [slot(blocks + 1), ring, tile],
        [ring, packed, rows],
    )
    recv = exchange(send)
    send, ends = call(
        plan, fifth_kernel, [recv, tiles, source, state],
        [slot(1), (2 * blocks, width)],
        [ring, ring, tile, packed, rows],
    )
    recv = exchange(send)
    star, pressure = call(
        plan, last_kernel, [recv, speeds, final, ends],
        [(3 * blocks, 1, width), (blocks, 1, width)], [tile],
    )
    star = star.reshape(3, 1, blocks, 1, width).transpose(0, 1, 3, 2, 4)
    pressure = pressure.reshape(1, blocks, 1, width).transpose(0, 2, 1, 3)
    return star, pressure


def solution(mesh):
    in_specs = (
        P(None, "gx", "gy", "gz", None),
        P(None, "gx", "gy", "gz", None),
        P("gx", "gy", "gz"),
        P("gx", "gy", "gz", None),
    )
    out_specs = (P(None, "gx", "gy", "gz", None), P("gx", "gy", "gz", None))
    return jax.shard_map(
        functools.partial(local, mesh),
        mesh=mesh, in_specs=in_specs, out_specs=out_specs, check_vma=False,
    )
```

```python
import functools

import jax
import jax.numpy as jnp
from jax import lax
from jax.experimental import pallas as pl
from jax.experimental.pallas import tpu as pltpu
from jax.sharding import PartitionSpec as P

VISCOUS = 4.0
STIFFNESS = 0.25
GRAVITY_STEP = 0.5
AXES = ("gx", "gy", "gz")
FAR = 1.0e3
LANES = 128


def exchange(send):
    return lax.all_to_all(send, AXES, 0, 0, tiled=True)


def exchange_layers(plan, send):
    level = lax.all_to_all(send, AXES[:2], 0, 0, tiled=True)
    deep = plan.count[2]
    if deep == 2:
        return [level, lax.ppermute(level, AXES[2], [(0, 1), (1, 0)])]
    forward = [(i, i + 1) for i in range(deep - 1)]
    backward = [(target, source) for source, target in forward]
    return [level] + [lax.ppermute(level, AXES[2], pairs) for pairs in (forward, backward)]


class Plan:
    def __init__(self, mesh, blocks, width):
        self.count = [mesh.shape[axis] for axis in AXES]
        self.devices = self.count[0] * self.count[1] * self.count[2]
        self.blocks = blocks
        self.width = width
        self.deep = blocks + 2
        self.ring = 9 * self.deep
        self.cube = (2.0 / width) ** (1.0 / 3.0)
        self.unit = self.cube ** 0.5

    def own(self, block):
        return 4 * self.deep + block + 1


def slots(plan, axes=3):
    place = [lax.axis_index(axis) for axis in AXES]
    found = {}
    for code in range(27):
        at = [place[0] + code // 9 - 1, place[1] + code // 3 % 3 - 1, place[2] + code % 3 - 1]
        present = None
        slot = 0
        for axis, (value, count) in enumerate(zip(at, plan.count)):
            inside = jnp.logical_and(value >= 0, value < count)
            present = inside if present is None else jnp.logical_and(present, inside)
            if axis < axes:
                slot = slot * count + jnp.clip(value, 0, count - 1)
        found[code] = (slot, present)
    return found


def gather_ring(plan, found, layers, fields, store):
    for column in range(9):
        for level in range(plan.deep):
            if level == 0:
                step, block = 0, plan.blocks - 1
            elif level == plan.deep - 1:
                step, block = 2, 0
            else:
                step, block = 1, level - 1
            slot, present = found[column * 3 + step]
            rows = [layers[step][slot, field * plan.blocks + block] for field in range(fields)]
            store(column * plan.deep + level, column, level, rows, present)


def ring_into(plan, found, recv, fields, ref):
    def store(at, column, level, rows, present):
        for field, row in enumerate(rows):
            ref[at, pl.ds(field, 1), :] = row

    gather_ring(plan, found, [recv] * 3, fields, store)


def lane_ids(sublanes=1):
    return lax.broadcasted_iota(jnp.int32, (sublanes, LANES), 1)


def sublane_ids():
    return lax.broadcasted_iota(jnp.int32, (8, LANES), 0)


def totals(recv, row, number):
    summed = jnp.broadcast_to(jnp.sum(recv[:, row], axis=0), (8, LANES))
    place = lane_ids(8) - sublane_ids()
    return [
        jnp.broadcast_to(
            jnp.sum(jnp.where(place == 8 * m, summed, 0.0), axis=1, keepdims=True), (8, LANES)
        )
        for m in range(number)
    ]


def pack(groups):
    lane = lane_ids()
    row = jnp.zeros((1, LANES), jnp.float32)
    for m, group in enumerate(groups):
        for c, partial in enumerate(group):
            row = jnp.where(lane == 8 * m + c, jnp.sum(partial, axis=1, keepdims=True), row)
    return row


def dot(first, second):
    total = first[0] * second[0]
    for a, b in zip(first[1:], second[1:]):
        total = total + a * b
    return total


def spread(send, rows):
    def body(slot, carry):
        for r, row in enumerate(rows):
            send[slot, r] = row
        return carry

    lax.fori_loop(0, send.shape[0], body, 0, unroll=4)


def coarse(value):
    return value.astype(jnp.bfloat16).astype(jnp.float32)


def split(value):
    first = coarse(value)
    rest = value - first
    second = coarse(rest)
    return first, second, rest - second


def split_ring(plan, ref, packed):
    for at in range(plan.ring):
        first, second, third = split(ref[at])
        stacked = jnp.concatenate([first, second, third, jnp.zeros_like(third)], axis=0)
        packed[:, pl.ds(at * LANES, LANES)] = stacked.astype(jnp.bfloat16)


def tile_sum(plan, tiles, packed, block, group):
    span = 3 * plan.width
    columns = range(2 * group, min(2 * group + 2, 9))
    ahead = [packed[:, pl.ds((c * plan.deep + block) * LANES, span)] for c in columns]
    return jnp.dot(
        jnp.concatenate(ahead, axis=1),
        tiles[block, pl.ds(2 * group * span, len(ahead) * span), :],
        preferred_element_type=jnp.float32,
    )


def fold(total):
    both = total[:, :LANES] + total[:, LANES:]
    return both[0:8] + both[8:16] + both[16:24]


def apply_tiles(plan, tiles, ring, packed, rows):
    split_ring(plan, ring, packed)
    for block in range(plan.blocks):
        total = tile_sum(plan, tiles, packed, block, 0)
        for group in range(1, 5):
            total = total + tile_sum(plan, tiles, packed, block, group)
        rows[block] = fold(total)


def pack_kernel(plan, counts_in, offsets_in, velocity_in, send, counts, offsets, velocity, sems):
    pairs = [(counts_in, counts), (offsets_in, offsets), (velocity_in, velocity)]
    copies = [pltpu.make_async_copy(a, b, sems.at[i]) for i, (a, b) in enumerate(pairs)]
    for copy in copies:
        copy.start()
    for copy in copies:
        copy.wait()
    lane = lane_ids()
    rows = []
    for axis in range(3):
        for block in range(plan.blocks):
            valid = lane < counts[0, block]
            row = offsets[axis * plan.blocks + block]
            rows.append(jnp.where(valid, row, FAR) if axis == 0 else row)
    for axis in range(3):
        for block in range(plan.blocks):
            valid = lane < counts[0, block]
            row = velocity[axis * plan.blocks + block]
            if axis == 0:
                row = row + GRAVITY_STEP
            rows.append(jnp.where(valid, row, 0.0))
    spread(send, rows)


def build_kernel(plan, *refs):
    level, others = refs[0], refs[1:-10]
    send, tiles, where, right, state, points, flipped, mixed, packed, rows = refs[-10:]
    layers = [others[0], level, others[-1]]
    found = slots(plan, 2)

    def store(at, column, level, got, present):
        shift = (column // 3 - 1, column % 3 - 1, level - (plan.deep - 1) // 2)
        spots = [plan.unit * (got[axis] + shift[axis]) for axis in range(3)]
        spots[0] = jnp.where(present, spots[0], FAR)
        points[at, pl.ds(3, 1), :] = spots[0] * spots[0] + spots[1] * spots[1] + spots[2] * spots[2]
        points[at, pl.ds(4, 1), :] = jnp.ones((1, LANES), jnp.float32)
        points[at, pl.ds(5, 3), :] = jnp.zeros((3, LANES), jnp.float32)
        mixed[at, pl.ds(3, 1), :] = jnp.ones((1, LANES), jnp.float32)
        mixed[at, pl.ds(7, 1), :] = jnp.zeros((1, LANES), jnp.float32)
        for axis in range(3):
            points[at, pl.ds(axis, 1), :] = spots[axis]
            where[at, pl.ds(axis, 1), :] = spots[axis]
            mixed[at, pl.ds(4 + axis, 1), :] = spots[axis]
            field = jnp.where(present, got[3 + axis], 0.0)
            right[at, pl.ds(axis, 1), :] = field
            mixed[at, pl.ds(axis, 1), :] = field

    gather_ring(plan, found, layers, 6, store)
    for at in range(plan.ring):
        first, second, third = split(points[at])
        stacked = jnp.concatenate([first, second, third, first, second, first], axis=0)
        padded = jnp.concatenate([stacked, jnp.zeros((LANES - 48, LANES), jnp.float32)], axis=0)
        flipped[pl.ds(at * plan.width, plan.width), :] = jnp.transpose(padded).astype(jnp.bfloat16)
    split_ring(plan, mixed, packed)
    sub = sublane_ids()
    for block in range(plan.blocks):
        own = points[plan.own(block)]
        own = jnp.where(jnp.logical_and(sub == 0, own > 0.25 * FAR), -FAR, own)
        square = jnp.broadcast_to(own[3:4], (8, LANES))
        own = jnp.where(sub < 3, 2.0 * own, 0.0)
        own = jnp.where(sub == 3, -1.0, own)
        own = jnp.where(sub == 4, plan.cube - square, own)
        first, second, third = split(own)
        stacked = jnp.concatenate([first, first, first, second, second, third], axis=0)
        padded = jnp.concatenate([stacked, jnp.zeros((LANES - 48, LANES), jnp.float32)], axis=0)
        centre = padded.astype(jnp.bfloat16)
        total = None
        for column in range(9):
            at = (column * plan.deep + block) * plan.width
            rest = jnp.dot(
                flipped[pl.ds(at, 3 * plan.width), :], centre, preferred_element_type=jnp.float32
            )
            bump = jnp.maximum(rest, 0.0)
            weight = bump * bump * bump
            high = weight.astype(jnp.bfloat16)
            span = pl.ds(3 * column * plan.width, 3 * plan.width)
            tiles[block, span, pl.ds(0, LANES)] = high
            tiles[block, span, pl.ds(LANES, LANES)] = (
                weight - high.astype(jnp.float32)
            ).astype(jnp.bfloat16)
            if column % 2 == 1 or column == 8:
                part = tile_sum(plan, tiles, packed, block, column // 2)
                total = part if total is None else total + part
        rows[block] = fold(total)
    image = [[None] * plan.blocks for _ in range(3)]
    whole = [[None] * plan.blocks for _ in range(3)]
    start = [[None] * plan.blocks for _ in range(3)]
    for block in range(plan.blocks):
        own = plan.own(block)
        reach = rows[block, pl.ds(3, 1), :]
        state[pl.ds(block, 1), :] = reach
        for axis in range(3):
            field = right[own, pl.ds(axis, 1), :]
            start[axis][block] = field
            image[axis][block] = reach * field - rows[block, pl.ds(axis, 1), :]
            whole[axis][block] = field + VISCOUS * image[axis][block]
            spot = where[own, pl.ds(axis, 1), :]
            state[pl.ds((1 + axis) * plan.blocks + block, 1), :] = (
                reach * spot - rows[block, pl.ds(4 + axis, 1), :]
            )
    groups = [
        [dot(start[axis], start[axis]) for axis in range(3)],
        [dot(start[axis], whole[axis]) for axis in range(3)],
        [dot(whole[axis], whole[axis]) for axis in range(3)],
    ]
    spread(send, sum(image, []) + [pack(groups)])


def second_kernel(plan, recv, tiles, right, state, send, residual, direction, scalars, image, packed, rows):
    found = slots(plan)
    ring_into(plan, found, recv, 3, image)
    current, curve, square = totals(recv, 3 * plan.blocks, 3)
    alpha = current / curve
    following = jnp.maximum(alpha * alpha * square - current, 0.0)
    beta = following / current
    for at in range(plan.ring):
        field = right[at]
        left = field - alpha * (field + VISCOUS * image[at])
        residual[at] = left
        direction[at] = left + beta * field
    scalars[plan.blocks] = alpha
    for block in range(plan.blocks):
        scalars[block] = image[plan.own(block)]
    apply_tiles(plan, tiles, direction, packed, rows)
    out = []
    groups = [[], [], [], []]
    for axis in range(3):
        left, ahead, shot, whole = [], [], [], []
        for block in range(plan.blocks):
            own = plan.own(block)
            left.append(residual[own, pl.ds(axis, 1), :])
            ahead.append(direction[own, pl.ds(axis, 1), :])
            shot.append(state[pl.ds(block, 1), :] * ahead[block] - rows[block, pl.ds(axis, 1), :])
            whole.append(ahead[block] + VISCOUS * shot[block])
        out.extend(shot)
        groups[0].append(dot(left, left))
        groups[1].append(dot(ahead, whole))
        groups[2].append(dot(left, whole))
        groups[3].append(dot(whole, whole))
    spread(send, out + [pack(groups)])


def third_kernel(
    plan, recv, tiles, where, right, residual, direction, state, scalars,
    send, ends, image, sofar, ahead, steps, packed, rows,
):
    found = slots(plan)
    ring_into(plan, found, recv, 3, image)
    current, curve, cross, square = totals(recv, 3 * plan.blocks, 4)
    alpha = current / curve
    following = jnp.maximum(current - 2.0 * alpha * cross + alpha * alpha * square, 0.0)
    beta = following / current
    first = scalars[plan.blocks]
    steps[...] = alpha
    sub = sublane_ids()
    for block in range(plan.blocks):
        own = plan.own(block)
        rows[block] = first * scalars[block] + alpha * image[own]
    latest = [
        [rows[block, pl.ds(axis, 1), :] for axis in range(3)] for block in range(plan.blocks)
    ]
    for at in range(plan.ring):
        field = direction[at]
        rest = residual[at] - alpha * (field + VISCOUS * image[at])
        fresh = rest + beta * field
        spot = where[at]
        made = first * right[at] + alpha * field
        moved = made * spot
        moved = pltpu.roll(moved, 6, 0) + pltpu.roll(moved, 5, 0) + pltpu.roll(moved, 4, 0)
        joined = jnp.where(sub < 3, fresh, pltpu.roll(fresh * spot, 3, 0))
        ahead[at] = jnp.where(sub < 6, joined, moved)
        if at - plan.own(0) in range(plan.blocks):
            image[at] = rest
            sofar[at - plan.own(0)] = made
    apply_tiles(plan, tiles, ahead, packed, rows)
    scale = 1.0 / plan.unit
    base = []
    each = [[None] * plan.blocks for _ in range(3)]
    rests = [[None] * plan.blocks for _ in range(3)]
    heads = [[None] * plan.blocks for _ in range(3)]
    wholes = [[None] * plan.blocks for _ in range(3)]
    for block in range(plan.blocks):
        reach = state[pl.ds(block, 1), :]
        own = plan.own(block)
        total = rows[block, pl.ds(6, 1), :] - reach * ahead[own, pl.ds(6, 1), :]
        for axis in range(3):
            head = ahead[own, pl.ds(axis, 1), :]
            spot = where[own, pl.ds(axis, 1), :]
            lean = state[pl.ds((1 + axis) * plan.blocks + block, 1), :]
            shot = reach * head - rows[block, pl.ds(axis, 1), :]
            twice = reach * ahead[own, pl.ds(3 + axis, 1), :] - rows[block, pl.ds(3 + axis, 1), :]
            each[axis][block] = scale * (spot * shot + head * lean - twice)
            made = sofar[block, pl.ds(axis, 1), :]
            total = total + spot * latest[block][axis] + made * lean
            rests[axis][block] = image[own, pl.ds(axis, 1), :]
            heads[axis][block] = head
            wholes[axis][block] = head + VISCOUS * shot
            ends[pl.ds(axis * plan.blocks + block, 1), :] = made
            ends[pl.ds((3 + axis) * plan.blocks + block, 1), :] = head
        base.append(scale * total)
    groups = [
        [dot(rests[axis], rests[axis]) for axis in range(3)],
        [dot(heads[axis], wholes[axis]) for axis in range(3)],
    ]
    spread(send, base + sum(each, []) + [pack(groups)])


def fourth_kernel(plan, recv, tiles, state, send, source, steps, parts, packed, rows):
    found = slots(plan)
    ring_into(plan, found, recv, 4, parts)
    current, curve = totals(recv, 4 * plan.blocks, 2)
    sub = sublane_ids()
    steps[...] = current / curve
    factor = jnp.where(sub == 0, 1.0, pltpu.roll(steps[...], 1, 0))
    for at in range(plan.ring):
        gathered = jnp.where(sub < 4, parts[at] * factor, 0.0)
        source[at] = jnp.broadcast_to(-jnp.sum(gathered, axis=0, keepdims=True), (8, LANES))
    apply_tiles(plan, tiles, source, packed, rows)
    field, shot, whole = [], [], []
    for block in range(plan.blocks):
        field.append(source[plan.own(block), pl.ds(0, 1), :])
        shot.append(state[pl.ds(block, 1), :] * field[block] - rows[block, pl.ds(0, 1), :])
        whole.append(STIFFNESS * field[block] + shot[block])
    groups = [[dot(field, field)], [dot(field, whole)], [dot(whole, whole)]]
    spread(send, shot + [pack(groups)])


def fifth_kernel(plan, recv, tiles, source, state, send, ends, image, ahead, steps, packed, rows):
    found = slots(plan)
    ring_into(plan, found, recv, 1, image)
    current, curve, square = totals(recv, plan.blocks, 3)
    steps[...] = current / curve
    alpha = steps[pl.ds(0, 1), :]
    steps[...] = jnp.maximum(alpha * alpha * square - current, 0.0) / current
    beta = steps[pl.ds(0, 1), :]
    for at in range(plan.ring):
        field = source[at]
        left = field - alpha * (STIFFNESS * field + image[at])
        image[at] = left
        ahead[at] = left + beta * field
    apply_tiles(plan, tiles, ahead, packed, rows)
    rests, heads, wholes = [], [], []
    for block in range(plan.blocks):
        own = plan.own(block)
        rests.append(image[own, pl.ds(0, 1), :])
        heads.append(ahead[own, pl.ds(0, 1), :])
        shot = state[pl.ds(block, 1), :] * heads[block] - rows[block, pl.ds(0, 1), :]
        wholes.append(STIFFNESS * heads[block] + shot)
        ends[pl.ds(block, 1), :] = alpha * source[own, pl.ds(0, 1), :]
        ends[pl.ds(plan.blocks + block, 1), :] = heads[block]
    spread(send, [pack([[dot(rests, rests)], [dot(heads, wholes)]])])


def last_kernel(plan, recv, speeds, final, ends, star, pressure, steps):
    current, curve = totals(recv, 0, 2)
    steps[...] = current / curve
    alpha = steps[pl.ds(0, 1), :]
    for block in range(plan.blocks):
        pressure[block] = (
            ends[pl.ds(block, 1), :] + alpha * ends[pl.ds(plan.blocks + block, 1), :]
        )
    for axis in range(3):
        alpha = final[pl.ds(axis, 1), :]
        for block in range(plan.blocks):
            at = axis * plan.blocks + block
            star[at] = (
                speeds[pl.ds(at, 1), :] + alpha * speeds[pl.ds(3 * plan.blocks + at, 1), :]
            )


def call(plan, kernel, operands, outs, scratch=(), space=pltpu.VMEM):
    typed = lambda shape: (shape, jnp.float32) if isinstance(shape[0], int) else shape
    held = lambda item: pltpu.VMEM(*typed(item)) if isinstance(item, tuple) else item
    return pl.pallas_call(
        functools.partial(kernel, plan),
        out_shape=[jax.ShapeDtypeStruct(*typed(shape)) for shape in outs],
        in_specs=[pl.BlockSpec(memory_space=space) for _ in operands],
        out_specs=[pl.BlockSpec(memory_space=pltpu.VMEM) for _ in outs],
        scratch_shapes=[held(item) for item in scratch],
        compiler_params=pltpu.CompilerParams(vmem_limit_bytes=24 * 1024 * 1024),
        name=kernel.__name__,
    )(*operands)


def local(mesh, offsets, velocity, counts, neighbours):
    blocks = counts.shape[2]
    width = offsets.shape[-1]
    plan = Plan(mesh, blocks, width)
    lined = lambda field: field.transpose(0, 1, 3, 2, 4).reshape(3 * blocks, 1, width)
    slot = lambda rows: (plan.devices, rows, 1, width)
    ring = (plan.ring, 8, width)
    tile = (8, width)
    rows = (blocks, 8, width)
    packed = ((32, plan.ring * width), jnp.bfloat16)
    (send,) = call(
        plan, pack_kernel,
        [
            pltpu.with_memory_space_constraint(field, pltpu.HBM)
            for field in (counts.reshape(1, blocks), lined(offsets), lined(velocity))
        ],
        [(plan.count[0] * plan.count[1], 6 * blocks, 1, width)],
        [
            pltpu.SMEM((1, blocks), jnp.int32), (3 * blocks, 1, width), (3 * blocks, 1, width),
            pltpu.SemaphoreType.DMA((3,)),
        ],
        pltpu.HBM,
    )
    send, tiles, where, right, state = call(
        plan, build_kernel, exchange_layers(plan, send),
        [
            slot(3 * blocks + 1), ((blocks, 27 * width, 2 * width), jnp.bfloat16),
            ring, ring, (4 * blocks, width),
        ],
        [ring, ((plan.ring * width, LANES), jnp.bfloat16), ring, packed, rows],
    )
    recv = exchange(send)
    send, residual, direction, scalars = call(
        plan, second_kernel, [recv, tiles, right, state],
        [slot(3 * blocks + 1), ring, ring, (blocks + 1, 8, width)],
        [ring, packed, rows],
    )
    recv = exchange(send)
    send, speeds = call(
        plan, third_kernel, [recv, tiles, where, right, residual, direction, state, scalars],
        [slot(4 * blocks + 1), (6 * blocks, width)],
        [ring, rows, ring, tile, packed, rows],
    )
    recv = exchange(send)
    send, source, final = call(
        plan, fourth_kernel, [recv, tiles, state],
        [slot(blocks + 1), ring, tile],
        [ring, packed, rows],
    )
    recv = exchange(send)
    send, ends = call(
        plan, fifth_kernel, [recv, tiles, source, state],
        [slot(1), (2 * blocks, width)],
        [ring, ring, tile, packed, rows],
    )
    recv = exchange(send)
    star, pressure = call(
        plan, last_kernel, [recv, speeds, final, ends],
        [(3 * blocks, 1, width), (blocks, 1, width)], [tile],
    )
    star = star.reshape(3, 1, blocks, 1, width).transpose(0, 1, 3, 2, 4)
    pressure = pressure.reshape(1, blocks, 1, width).transpose(0, 2, 1, 3)
    return star, pressure


def solution(mesh):
    in_specs = (
        P(None, "gx", "gy", "gz", None),
        P(None, "gx", "gy", "gz", None),
        P("gx", "gy", "gz"),
        P("gx", "gy", "gz", None),
    )
    out_specs = (P(None, "gx", "gy", "gz", None), P("gx", "gy", "gz", None))
    return jax.shard_map(
        functools.partial(local, mesh),
        mesh=mesh, in_specs=in_specs, out_specs=out_specs, check_vma=False,
    )
```

```python
import functools

import jax
import jax.numpy as jnp
from jax import lax
from jax.experimental import pallas as pl
from jax.experimental.pallas import tpu as pltpu
from jax.sharding import PartitionSpec as P

VISCOUS = 4.0
STIFFNESS = 0.25
GRAVITY_STEP = 0.5
AXES = ("gx", "gy", "gz")
FAR = 1.0e3
LANES = 128


def exchange(send):
    return lax.all_to_all(send, AXES, 0, 0, tiled=True)


def exchange_layers(plan, send):
    level = lax.all_to_all(send, AXES[:2], 0, 0, tiled=True)
    deep = plan.count[2]
    if deep == 2:
        return [level, lax.ppermute(level, AXES[2], [(0, 1), (1, 0)])]
    forward = [(i, i + 1) for i in range(deep - 1)]
    backward = [(target, source) for source, target in forward]
    return [level] + [lax.ppermute(level, AXES[2], pairs) for pairs in (forward, backward)]


class Plan:
    def __init__(self, mesh, blocks, width):
        self.count = [mesh.shape[axis] for axis in AXES]
        self.devices = self.count[0] * self.count[1] * self.count[2]
        self.blocks = blocks
        self.width = width
        self.deep = blocks + 2
        self.ring = 9 * self.deep
        self.cube = (2.0 / width) ** (1.0 / 3.0)
        self.unit = self.cube ** 0.5

    def own(self, block):
        return 4 * self.deep + block + 1


def slots(plan, axes=3):
    place = [lax.axis_index(axis) for axis in AXES]
    found = {}
    for code in range(27):
        at = [place[0] + code // 9 - 1, place[1] + code // 3 % 3 - 1, place[2] + code % 3 - 1]
        present = None
        slot = 0
        for axis, (value, count) in enumerate(zip(at, plan.count)):
            inside = jnp.logical_and(value >= 0, value < count)
            present = inside if present is None else jnp.logical_and(present, inside)
            if axis < axes:
                slot = slot * count + jnp.clip(value, 0, count - 1)
        found[code] = (slot, present)
    return found


def gather_ring(plan, found, layers, fields, store, levels=None):
    for column in range(9):
        for level in levels or range(plan.deep):
            if level == 0:
                step, block = 0, plan.blocks - 1
            elif level == plan.deep - 1:
                step, block = 2, 0
            else:
                step, block = 1, level - 1
            slot, present = found[column * 3 + step]
            rows = [layers[step][slot, field * plan.blocks + block] for field in range(fields)]
            store(column * plan.deep + level, column, level, rows, present)


def ring_into(plan, found, recv, fields, ref):
    def store(at, column, level, rows, present):
        for field, row in enumerate(rows):
            ref[at, pl.ds(field, 1), :] = row

    gather_ring(plan, found, [recv] * 3, fields, store)


def lane_ids(sublanes=1):
    return lax.broadcasted_iota(jnp.int32, (sublanes, LANES), 1)


def sublane_ids():
    return lax.broadcasted_iota(jnp.int32, (8, LANES), 0)


def totals(recv, row, number):
    summed = jnp.broadcast_to(jnp.sum(recv[:, row], axis=0), (8, LANES))
    place = lane_ids(8) - sublane_ids()
    return [
        jnp.broadcast_to(
            jnp.sum(jnp.where(place == 8 * m, summed, 0.0), axis=1, keepdims=True), (8, LANES)
        )
        for m in range(number)
    ]


def pack(groups):
    lane = lane_ids()
    row = jnp.zeros((1, LANES), jnp.float32)
    for m, group in enumerate(groups):
        for c, partial in enumerate(group):
            row = jnp.where(lane == 8 * m + c, jnp.sum(partial, axis=1, keepdims=True), row)
    return row


def dot(first, second):
    total = first[0] * second[0]
    for a, b in zip(first[1:], second[1:]):
        total = total + a * b
    return total


def spread(send, rows):
    def body(slot, carry):
        for r, row in enumerate(rows):
            send[slot, r] = row
        return carry

    lax.fori_loop(0, send.shape[0], body, 0, unroll=4)


def coarse(value):
    return value.astype(jnp.bfloat16).astype(jnp.float32)


def split(value):
    first = coarse(value)
    rest = value - first
    second = coarse(rest)
    return first, second, rest - second


def split_ring(plan, ring, packed, levels=None):
    for column in range(9):
        for level in levels or range(plan.deep):
            at = column * plan.deep + level
            first, second, third = split(ring[at])
            stacked = jnp.concatenate([first, second, third, jnp.zeros_like(third)], axis=0)
            packed[:, pl.ds(at * LANES, LANES)] = stacked.astype(jnp.bfloat16)


def inner_span(plan, block):
    low = max(block, 1)
    return low, min(block + 2, plan.blocks) + 1 - low


def inner_base(plan, block):
    return 9 * sum(inner_span(plan, before)[1] for before in range(block)) * plan.width


def edges(plan):
    return [(0, 0), (plan.blocks - 1, plan.blocks + 1)]


def groups_of(number):
    size = 3 if number % 2 == 0 else 4 if number == 1 else 2
    return [range(c, min(c + size, 9)) for c in range(0, 9, size)]


def tile_sum(plan, tiles, base, packed, level, number, columns):
    span = number * plan.width
    ahead = [packed[:, pl.ds((c * plan.deep + level) * LANES, span)] for c in columns]
    return jnp.dot(
        jnp.concatenate(ahead, axis=1) if len(ahead) > 1 else ahead[0],
        tiles[pl.ds(base + columns[0] * span, len(ahead) * span), :],
        preferred_element_type=jnp.float32,
    )


def fold(total):
    both = total[:, :LANES] + total[:, LANES:]
    return both[0:8] + both[8:16] + both[16:24]


def apply_tiles(plan, tiles, rims, ring, packed, rows):
    split_ring(plan, ring, packed)
    for block in range(plan.blocks):
        low, number = inner_span(plan, block)
        base = inner_base(plan, block)
        parts = [
            tile_sum(plan, tiles, base, packed, low, number, columns)
            for columns in groups_of(number)
        ]
        for edge, (at, level) in enumerate(edges(plan)):
            if at == block:
                base = edge * 9 * plan.width
                parts += [
                    tile_sum(plan, rims, base, packed, level, 1, columns)
                    for columns in groups_of(1)
                ]
        total = parts[0]
        for part in parts[1:]:
            total = total + part
        rows[block] = fold(total)


def pack_kernel(plan, counts_in, offsets_in, velocity_in, send, counts, offsets, velocity, sems):
    pairs = [(counts_in, counts), (offsets_in, offsets), (velocity_in, velocity)]
    copies = [pltpu.make_async_copy(a, b, sems.at[i]) for i, (a, b) in enumerate(pairs)]
    for copy in copies:
        copy.start()
    for copy in copies:
        copy.wait()
    lane = lane_ids()
    rows = []
    for axis in range(3):
        for block in range(plan.blocks):
            valid = lane < counts[0, block]
            row = offsets[axis * plan.blocks + block]
            rows.append(jnp.where(valid, row, FAR) if axis == 0 else row)
    for axis in range(3):
        for block in range(plan.blocks):
            valid = lane < counts[0, block]
            row = velocity[axis * plan.blocks + block]
            if axis == 0:
                row = row + GRAVITY_STEP
            rows.append(jnp.where(valid, row, 0.0))
    spread(send, rows)


def place_ring(plan, found, layers, levels, points, mixed, where, right):
    def store(at, column, level, got, present):
        shift = (column // 3 - 1, column % 3 - 1, level - (plan.deep - 1) // 2)
        spots = [plan.unit * (got[axis] + shift[axis]) for axis in range(3)]
        spots[0] = jnp.where(present, spots[0], FAR)
        points[at, pl.ds(3, 1), :] = spots[0] * spots[0] + spots[1] * spots[1] + spots[2] * spots[2]
        points[at, pl.ds(4, 1), :] = jnp.ones((1, LANES), jnp.float32)
        points[at, pl.ds(5, 3), :] = jnp.zeros((3, LANES), jnp.float32)
        mixed[at, pl.ds(3, 1), :] = jnp.ones((1, LANES), jnp.float32)
        mixed[at, pl.ds(7, 1), :] = jnp.zeros((1, LANES), jnp.float32)
        for axis in range(3):
            points[at, pl.ds(axis, 1), :] = spots[axis]
            where[at, pl.ds(axis, 1), :] = spots[axis]
            mixed[at, pl.ds(4 + axis, 1), :] = spots[axis]
            field = jnp.where(present, got[3 + axis], 0.0)
            right[at, pl.ds(axis, 1), :] = field
            mixed[at, pl.ds(axis, 1), :] = field

    gather_ring(plan, found, layers, 6, store, levels)


def flip_points(plan, levels, points, flipped):
    for column in range(9):
        for level in levels:
            at = column * plan.deep + level
            first, second, third = split(points[at])
            stacked = jnp.concatenate([first, second, third, first, second, first], axis=0)
            padded = jnp.concatenate([stacked, jnp.zeros((LANES - 48, LANES), jnp.float32)], axis=0)
            flipped[pl.ds(at * plan.width, plan.width), :] = jnp.transpose(padded).astype(jnp.bfloat16)


def weigh(plan, flipped, centre, level, number, columns, tiles, base):
    for column in columns:
        span = number * plan.width
        rest = jnp.dot(
            flipped[pl.ds((column * plan.deep + level) * plan.width, span), :],
            centre, preferred_element_type=jnp.float32,
        )
        bump = jnp.maximum(rest, 0.0)
        weight = bump * bump * bump
        high = weight.astype(jnp.bfloat16)
        spot = pl.ds(base + column * span, span)
        tiles[spot, pl.ds(0, LANES)] = high
        tiles[spot, pl.ds(LANES, LANES)] = (weight - high.astype(jnp.float32)).astype(jnp.bfloat16)


def inner_kernel(plan, recv, tiles, where, right, centres, partial, points, flipped, mixed, packed):
    levels = range(1, plan.blocks + 1)
    place_ring(plan, slots(plan, 2), [None, recv, None], levels, points, mixed, where, right)
    flip_points(plan, levels, points, flipped)
    split_ring(plan, mixed, packed, levels)
    sub = sublane_ids()
    for block in range(plan.blocks):
        own = points[plan.own(block)]
        own = jnp.where(jnp.logical_and(sub == 0, own > 0.25 * FAR), -FAR, own)
        square = jnp.broadcast_to(own[3:4], (8, LANES))
        own = jnp.where(sub < 3, 2.0 * own, 0.0)
        own = jnp.where(sub == 3, -1.0, own)
        own = jnp.where(sub == 4, plan.cube - square, own)
        first, second, third = split(own)
        stacked = jnp.concatenate([first, first, first, second, second, third], axis=0)
        padded = jnp.concatenate([stacked, jnp.zeros((LANES - 48, LANES), jnp.float32)], axis=0)
        centre = padded.astype(jnp.bfloat16)
        centres[block] = centre
        low, number = inner_span(plan, block)
        base = inner_base(plan, block)
        total = None
        for columns in groups_of(number):
            weigh(plan, flipped, centre, low, number, columns, tiles, base)
            part = tile_sum(plan, tiles, base, packed, low, number, columns)
            total = part if total is None else total + part
        partial[block] = fold(total)


def edge_kernel(plan, *refs):
    others = refs[:-14]
    (
        near_where, near_right, centres, partial,
        send, rims, where, right, state, points, flipped, mixed, packed, rows,
    ) = refs[-14:]
    levels = [0, plan.deep - 1]
    place_ring(
        plan, slots(plan, 2), [others[0], None, others[-1]], levels, points, mixed, where, right
    )
    for column in range(9):
        for level in range(1, plan.blocks + 1):
            at = column * plan.deep + level
            where[at] = near_where[at]
            right[at] = near_right[at]
    flip_points(plan, levels, points, flipped)
    split_ring(plan, mixed, packed, levels)
    for block in range(plan.blocks):
        rows[block] = partial[block]
    for edge, (block, level) in enumerate(edges(plan)):
        base = edge * 9 * plan.width
        total = None
        for columns in groups_of(1):
            weigh(plan, flipped, centres[block], level, 1, columns, rims, base)
            part = tile_sum(plan, rims, base, packed, level, 1, columns)
            total = part if total is None else total + part
        rows[block] = rows[block] + fold(total)
    image = [[None] * plan.blocks for _ in range(3)]
    whole = [[None] * plan.blocks for _ in range(3)]
    start = [[None] * plan.blocks for _ in range(3)]
    for block in range(plan.blocks):
        own = plan.own(block)
        reach = rows[block, pl.ds(3, 1), :]
        state[pl.ds(block, 1), :] = reach
        for axis in range(3):
            field = right[own, pl.ds(axis, 1), :]
            start[axis][block] = field
            image[axis][block] = reach * field - rows[block, pl.ds(axis, 1), :]
            whole[axis][block] = field + VISCOUS * image[axis][block]
            spot = where[own, pl.ds(axis, 1), :]
            state[pl.ds((1 + axis) * plan.blocks + block, 1), :] = (
                reach * spot - rows[block, pl.ds(4 + axis, 1), :]
            )
    groups = [
        [dot(start[axis], start[axis]) for axis in range(3)],
        [dot(start[axis], whole[axis]) for axis in range(3)],
        [dot(whole[axis], whole[axis]) for axis in range(3)],
    ]
    spread(send, sum(image, []) + [pack(groups)])


def second_kernel(plan, recv, tiles, rims, right, state, send, residual, direction, scalars, image, packed, rows):
    found = slots(plan)
    ring_into(plan, found, recv, 3, image)
    current, curve, square = totals(recv, 3 * plan.blocks, 3)
    alpha = current / curve
    following = jnp.maximum(alpha * alpha * square - current, 0.0)
    beta = following / current
    for at in range(plan.ring):
        field = right[at]
        left = field - alpha * (field + VISCOUS * image[at])
        residual[at] = left
        direction[at] = left + beta * field
    scalars[plan.blocks] = alpha
    for block in range(plan.blocks):
        scalars[block] = image[plan.own(block)]
    apply_tiles(plan, tiles, rims, direction, packed, rows)
    out = []
    groups = [[], [], [], []]
    for axis in range(3):
        left, ahead, shot, whole = [], [], [], []
        for block in range(plan.blocks):
            own = plan.own(block)
            left.append(residual[own, pl.ds(axis, 1), :])
            ahead.append(direction[own, pl.ds(axis, 1), :])
            shot.append(state[pl.ds(block, 1), :] * ahead[block] - rows[block, pl.ds(axis, 1), :])
            whole.append(ahead[block] + VISCOUS * shot[block])
        out.extend(shot)
        groups[0].append(dot(left, left))
        groups[1].append(dot(ahead, whole))
        groups[2].append(dot(left, whole))
        groups[3].append(dot(whole, whole))
    spread(send, out + [pack(groups)])


def third_kernel(
    plan, recv, tiles, rims, where, right, residual, direction, state, scalars,
    send, ends, image, sofar, ahead, steps, packed, rows,
):
    found = slots(plan)
    ring_into(plan, found, recv, 3, image)
    current, curve, cross, square = totals(recv, 3 * plan.blocks, 4)
    alpha = current / curve
    following = jnp.maximum(current - 2.0 * alpha * cross + alpha * alpha * square, 0.0)
    beta = following / current
    first = scalars[plan.blocks]
    steps[...] = alpha
    sub = sublane_ids()
    for block in range(plan.blocks):
        own = plan.own(block)
        rows[block] = first * scalars[block] + alpha * image[own]
    latest = [
        [rows[block, pl.ds(axis, 1), :] for axis in range(3)] for block in range(plan.blocks)
    ]
    for at in range(plan.ring):
        field = direction[at]
        rest = residual[at] - alpha * (field + VISCOUS * image[at])
        fresh = rest + beta * field
        spot = where[at]
        made = first * right[at] + alpha * field
        moved = made * spot
        moved = pltpu.roll(moved, 6, 0) + pltpu.roll(moved, 5, 0) + pltpu.roll(moved, 4, 0)
        joined = jnp.where(sub < 3, fresh, pltpu.roll(fresh * spot, 3, 0))
        ahead[at] = jnp.where(sub < 6, joined, moved)
        if at - plan.own(0) in range(plan.blocks):
            image[at] = rest
            sofar[at - plan.own(0)] = made
    apply_tiles(plan, tiles, rims, ahead, packed, rows)
    scale = 1.0 / plan.unit
    base = []
    each = [[None] * plan.blocks for _ in range(3)]
    rests = [[None] * plan.blocks for _ in range(3)]
    heads = [[None] * plan.blocks for _ in range(3)]
    wholes = [[None] * plan.blocks for _ in range(3)]
    for block in range(plan.blocks):
        reach = state[pl.ds(block, 1), :]
        own = plan.own(block)
        total = rows[block, pl.ds(6, 1), :] - reach * ahead[own, pl.ds(6, 1), :]
        for axis in range(3):
            head = ahead[own, pl.ds(axis, 1), :]
            spot = where[own, pl.ds(axis, 1), :]
            lean = state[pl.ds((1 + axis) * plan.blocks + block, 1), :]
            shot = reach * head - rows[block, pl.ds(axis, 1), :]
            twice = reach * ahead[own, pl.ds(3 + axis, 1), :] - rows[block, pl.ds(3 + axis, 1), :]
            each[axis][block] = scale * (spot * shot + head * lean - twice)
            made = sofar[block, pl.ds(axis, 1), :]
            total = total + spot * latest[block][axis] + made * lean
            rests[axis][block] = image[own, pl.ds(axis, 1), :]
            heads[axis][block] = head
            wholes[axis][block] = head + VISCOUS * shot
            ends[pl.ds(axis * plan.blocks + block, 1), :] = made
            ends[pl.ds((3 + axis) * plan.blocks + block, 1), :] = head
        base.append(scale * total)
    groups = [
        [dot(rests[axis], rests[axis]) for axis in range(3)],
        [dot(heads[axis], wholes[axis]) for axis in range(3)],
    ]
    spread(send, base + sum(each, []) + [pack(groups)])


def fourth_kernel(plan, recv, tiles, rims, state, send, source, steps, parts, packed, rows):
    found = slots(plan)
    ring_into(plan, found, recv, 4, parts)
    current, curve = totals(recv, 4 * plan.blocks, 2)
    sub = sublane_ids()
    steps[...] = current / curve
    factor = jnp.where(sub == 0, 1.0, pltpu.roll(steps[...], 1, 0))
    for at in range(plan.ring):
        gathered = jnp.where(sub < 4, parts[at] * factor, 0.0)
        source[at] = jnp.broadcast_to(-jnp.sum(gathered, axis=0, keepdims=True), (8, LANES))
    apply_tiles(plan, tiles, rims, source, packed, rows)
    field, shot, whole = [], [], []
    for block in range(plan.blocks):
        field.append(source[plan.own(block), pl.ds(0, 1), :])
        shot.append(state[pl.ds(block, 1), :] * field[block] - rows[block, pl.ds(0, 1), :])
        whole.append(STIFFNESS * field[block] + shot[block])
    groups = [[dot(field, field)], [dot(field, whole)], [dot(whole, whole)]]
    spread(send, shot + [pack(groups)])


def fifth_kernel(plan, recv, tiles, rims, source, state, send, ends, image, ahead, steps, packed, rows):
    found = slots(plan)
    ring_into(plan, found, recv, 1, image)
    current, curve, square = totals(recv, plan.blocks, 3)
    steps[...] = current / curve
    alpha = steps[pl.ds(0, 1), :]
    steps[...] = jnp.maximum(alpha * alpha * square - current, 0.0) / current
    beta = steps[pl.ds(0, 1), :]
    for at in range(plan.ring):
        field = source[at]
        left = field - alpha * (STIFFNESS * field + image[at])
        image[at] = left
        ahead[at] = left + beta * field
    apply_tiles(plan, tiles, rims, ahead, packed, rows)
    rests, heads, wholes = [], [], []
    for block in range(plan.blocks):
        own = plan.own(block)
        rests.append(image[own, pl.ds(0, 1), :])
        heads.append(ahead[own, pl.ds(0, 1), :])
        shot = state[pl.ds(block, 1), :] * heads[block] - rows[block, pl.ds(0, 1), :]
        wholes.append(STIFFNESS * heads[block] + shot)
        ends[pl.ds(block, 1), :] = alpha * source[own, pl.ds(0, 1), :]
        ends[pl.ds(plan.blocks + block, 1), :] = heads[block]
    spread(send, [pack([[dot(rests, rests)], [dot(heads, wholes)]])])


def last_kernel(plan, recv, speeds, final, ends, star, pressure, steps):
    current, curve = totals(recv, 0, 2)
    steps[...] = current / curve
    alpha = steps[pl.ds(0, 1), :]
    for block in range(plan.blocks):
        pressure[block] = (
            ends[pl.ds(block, 1), :] + alpha * ends[pl.ds(plan.blocks + block, 1), :]
        )
    for axis in range(3):
        alpha = final[pl.ds(axis, 1), :]
        for block in range(plan.blocks):
            at = axis * plan.blocks + block
            star[at] = (
                speeds[pl.ds(at, 1), :] + alpha * speeds[pl.ds(3 * plan.blocks + at, 1), :]
            )


def call(plan, kernel, operands, outs, scratch=(), space=pltpu.VMEM):
    typed = lambda shape: (shape, jnp.float32) if isinstance(shape[0], int) else shape
    held = lambda item: pltpu.VMEM(*typed(item)) if isinstance(item, tuple) else item
    return pl.pallas_call(
        functools.partial(kernel, plan),
        out_shape=[jax.ShapeDtypeStruct(*typed(shape)) for shape in outs],
        in_specs=[pl.BlockSpec(memory_space=space) for _ in operands],
        out_specs=[pl.BlockSpec(memory_space=pltpu.VMEM) for _ in outs],
        scratch_shapes=[held(item) for item in scratch],
        compiler_params=pltpu.CompilerParams(vmem_limit_bytes=24 * 1024 * 1024),
        name=kernel.__name__,
    )(*operands)


def local(mesh, offsets, velocity, counts, neighbours):
    blocks = counts.shape[2]
    width = offsets.shape[-1]
    plan = Plan(mesh, blocks, width)
    lined = lambda field: field.transpose(0, 1, 3, 2, 4).reshape(3 * blocks, 1, width)
    slot = lambda rows: (plan.devices, rows, 1, width)
    ring = (plan.ring, 8, width)
    tile = (8, width)
    rows = (blocks, 8, width)
    packed = ((32, plan.ring * width), jnp.bfloat16)
    (send,) = call(
        plan, pack_kernel,
        [
            pltpu.with_memory_space_constraint(field, pltpu.HBM)
            for field in (counts.reshape(1, blocks), lined(offsets), lined(velocity))
        ],
        [(plan.count[0] * plan.count[1], 6 * blocks, 1, width)],
        [
            pltpu.SMEM((1, blocks), jnp.int32), (3 * blocks, 1, width), (3 * blocks, 1, width),
            pltpu.SemaphoreType.DMA((3,)),
        ],
        pltpu.HBM,
    )
    level, *others = exchange_layers(plan, send)
    flipped = ((plan.ring * width, LANES), jnp.bfloat16)
    tiles, where, right, centres, partial = call(
        plan, inner_kernel, [level],
        [
            ((inner_base(plan, blocks), 2 * width), jnp.bfloat16), ring, ring,
            ((blocks, LANES, width), jnp.bfloat16), rows,
        ],
        [ring, flipped, ring, packed],
    )
    send, rims, where, right, state = call(
        plan, edge_kernel, [*others, where, right, centres, partial],
        [
            slot(3 * blocks + 1), ((2 * 9 * width, 2 * width), jnp.bfloat16),
            ring, ring, (4 * blocks, width),
        ],
        [ring, flipped, ring, packed, rows],
    )
    recv = exchange(send)
    send, residual, direction, scalars = call(
        plan, second_kernel, [recv, tiles, rims, right, state],
        [slot(3 * blocks + 1), ring, ring, (blocks + 1, 8, width)],
        [ring, packed, rows],
    )
    recv = exchange(send)
    send, speeds = call(
        plan, third_kernel, [recv, tiles, rims, where, right, residual, direction, state, scalars],
        [slot(4 * blocks + 1), (6 * blocks, width)],
        [ring, rows, ring, tile, packed, rows],
    )
    recv = exchange(send)
    send, source, final = call(
        plan, fourth_kernel, [recv, tiles, rims, state],
        [slot(blocks + 1), ring, tile],
        [ring, packed, rows],
    )
    recv = exchange(send)
    send, ends = call(
        plan, fifth_kernel, [recv, tiles, rims, source, state],
        [slot(1), (2 * blocks, width)],
        [ring, ring, tile, packed, rows],
    )
    recv = exchange(send)
    star, pressure = call(
        plan, last_kernel, [recv, speeds, final, ends],
        [(3 * blocks, 1, width), (blocks, 1, width)], [tile],
    )
    star = star.reshape(3, 1, blocks, 1, width).transpose(0, 1, 3, 2, 4)
    pressure = pressure.reshape(1, blocks, 1, width).transpose(0, 2, 1, 3)
    return star, pressure


def solution(mesh):
    in_specs = (
        P(None, "gx", "gy", "gz", None),
        P(None, "gx", "gy", "gz", None),
        P("gx", "gy", "gz"),
        P("gx", "gy", "gz", None),
    )
    out_specs = (P(None, "gx", "gy", "gz", None), P("gx", "gy", "gz", None))
    return jax.shard_map(
        functools.partial(local, mesh),
        mesh=mesh, in_specs=in_specs, out_specs=out_specs, check_vma=False,
    )
```

```python
import functools

import jax
import jax.numpy as jnp
from jax import lax
from jax.experimental import pallas as pl
from jax.experimental.pallas import tpu as pltpu
from jax.sharding import PartitionSpec as P

VISCOUS = 4.0
STIFFNESS = 0.25
GRAVITY_STEP = 0.5
AXES = ("gx", "gy", "gz")
FAR = 1.0e3
LANES = 128


def exchange(send):
    return lax.all_to_all(send, AXES, 0, 0, tiled=True)


def exchange_layers(plan, send):
    level = lax.all_to_all(send, AXES[:2], 0, 0, tiled=True)
    deep = plan.count[2]
    if deep == 2:
        return [level, lax.ppermute(level, AXES[2], [(0, 1), (1, 0)])]
    forward = [(i, i + 1) for i in range(deep - 1)]
    backward = [(target, source) for source, target in forward]
    return [level] + [lax.ppermute(level, AXES[2], pairs) for pairs in (forward, backward)]


class Plan:
    def __init__(self, mesh, blocks, width):
        self.count = [mesh.shape[axis] for axis in AXES]
        self.devices = self.count[0] * self.count[1] * self.count[2]
        self.blocks = blocks
        self.width = width
        self.rims = 1 if self.count[2] == 2 else 2
        self.deep = blocks + self.rims
        self.ring = 9 * self.deep
        self.cube = (2.0 / width) ** (1.0 / 3.0)
        self.unit = self.cube ** 0.5

    def own(self, block):
        return 4 * self.deep + block


def rims_of(plan):
    last = plan.blocks - 1
    if plan.rims == 2:
        return [(-1, 0, last, -1), (1, last, 0, plan.blocks)]
    above = lax.axis_index(AXES[2]) == 0
    choose = lambda yes, no: jnp.where(above, jnp.int32(yes), jnp.int32(no))
    return [(choose(1, -1), choose(last, 0), choose(0, last), choose(plan.blocks, -1))]


def slots(plan, rims, axes=3):
    place = [lax.axis_index(axis) for axis in AXES]
    found = []
    for column in range(9):
        beside = []
        for step in [0] + [rim[0] for rim in rims]:
            at = [place[0] + column // 3 - 1, place[1] + column % 3 - 1, place[2] + step]
            present = None
            slot = 0
            for axis, (value, count) in enumerate(zip(at, plan.count)):
                inside = jnp.logical_and(value >= 0, value < count)
                present = inside if present is None else jnp.logical_and(present, inside)
                if axis < axes:
                    slot = slot * count + jnp.clip(value, 0, count - 1)
            beside.append((slot, present))
        found.append(beside)
    return found


def gather_ring(plan, rims, found, layers, fields, store, levels=None):
    for column in range(9):
        for level in levels or range(plan.deep):
            layer, block, depth = 0, level, level
            if level >= plan.blocks:
                layer = level - plan.blocks + 1
                block, depth = rims[layer - 1][2:]
            slot, present = found[column][layer]
            rows = [layers[layer][slot, field * plan.blocks + block] for field in range(fields)]
            store(column * plan.deep + level, column, depth, rows, present)


def ring_into(plan, rims, recv, fields, ref):
    def store(at, column, depth, rows, present):
        for field, row in enumerate(rows):
            ref[at, pl.ds(field, 1), :] = row

    gather_ring(plan, rims, slots(plan, rims), [recv] * (1 + plan.rims), fields, store)


def lane_ids(sublanes=1):
    return lax.broadcasted_iota(jnp.int32, (sublanes, LANES), 1)


def sublane_ids():
    return lax.broadcasted_iota(jnp.int32, (8, LANES), 0)


def totals(recv, row, number):
    summed = jnp.broadcast_to(jnp.sum(recv[:, row], axis=0), (8, LANES))
    place = lane_ids(8) - sublane_ids()
    return [
        jnp.broadcast_to(
            jnp.sum(jnp.where(place == 8 * m, summed, 0.0), axis=1, keepdims=True), (8, LANES)
        )
        for m in range(number)
    ]


def pack(groups):
    lane = lane_ids()
    row = jnp.zeros((1, LANES), jnp.float32)
    for m, group in enumerate(groups):
        for c, partial in enumerate(group):
            row = jnp.where(lane == 8 * m + c, jnp.sum(partial, axis=1, keepdims=True), row)
    return row


def dot(first, second):
    total = first[0] * second[0]
    for a, b in zip(first[1:], second[1:]):
        total = total + a * b
    return total


def spread(send, rows):
    def body(slot, carry):
        for r, row in enumerate(rows):
            send[slot, r] = row
        return carry

    lax.fori_loop(0, send.shape[0], body, 0, unroll=4)


def coarse(value):
    return value.astype(jnp.bfloat16).astype(jnp.float32)


def split(value):
    first = coarse(value)
    rest = value - first
    second = coarse(rest)
    return first, second, rest - second


def split_ring(plan, ring, packed, levels=None):
    for column in range(9):
        for level in levels or range(plan.deep):
            at = column * plan.deep + level
            first, second, third = split(ring[at])
            stacked = jnp.concatenate([first, second, third, jnp.zeros_like(third)], axis=0)
            packed[:, pl.ds(at * LANES, LANES)] = stacked.astype(jnp.bfloat16)


def inner_span(plan, block):
    low = max(block - 1, 0)
    return low, min(block + 2, plan.blocks) - low


def inner_base(plan, block):
    return 9 * sum(inner_span(plan, before)[1] for before in range(block)) * plan.width


def groups_of(number):
    size = 3 if number % 2 == 0 else 4 if number == 1 else 2
    return [range(c, min(c + size, 9)) for c in range(0, 9, size)]


def tile_sum(plan, tiles, base, packed, level, number, columns):
    span = number * plan.width
    ahead = [packed[:, pl.ds((c * plan.deep + level) * LANES, span)] for c in columns]
    return jnp.dot(
        jnp.concatenate(ahead, axis=1) if len(ahead) > 1 else ahead[0],
        tiles[pl.ds(base + columns[0] * span, len(ahead) * span), :],
        preferred_element_type=jnp.float32,
    )


def fold(total):
    both = total[:, :LANES] + total[:, LANES:]
    return both[0:8] + both[8:16] + both[16:24]


def apply_tiles(plan, rims, tiles, outer, ring, packed, rows):
    split_ring(plan, ring, packed)
    for block in range(plan.blocks):
        low, number = inner_span(plan, block)
        base = inner_base(plan, block)
        total = None
        for columns in groups_of(number):
            part = tile_sum(plan, tiles, base, packed, low, number, columns)
            total = part if total is None else total + part
        rows[block] = fold(total)
    add_rims(plan, rims, outer, packed, rows, lambda e, columns: None)


def add_rims(plan, rims, outer, packed, rows, before):
    for e, rim in enumerate(rims):
        total = None
        for columns in groups_of(1):
            before(e, columns)
            base = e * 9 * plan.width
            part = tile_sum(plan, outer, base, packed, plan.blocks + e, 1, columns)
            total = part if total is None else total + part
        rows[rim[1]] = rows[rim[1]] + fold(total)


def pack_kernel(plan, counts_in, offsets_in, velocity_in, send, counts, offsets, velocity, sems):
    pairs = [(counts_in, counts), (offsets_in, offsets), (velocity_in, velocity)]
    copies = [pltpu.make_async_copy(a, b, sems.at[i]) for i, (a, b) in enumerate(pairs)]
    for copy in copies:
        copy.start()
    for copy in copies:
        copy.wait()
    lane = lane_ids()
    rows = []
    for axis in range(3):
        for block in range(plan.blocks):
            valid = lane < counts[0, block]
            row = offsets[axis * plan.blocks + block]
            rows.append(jnp.where(valid, row, FAR) if axis == 0 else row)
    for axis in range(3):
        for block in range(plan.blocks):
            valid = lane < counts[0, block]
            row = velocity[axis * plan.blocks + block]
            if axis == 0:
                row = row + GRAVITY_STEP
            rows.append(jnp.where(valid, row, 0.0))
    spread(send, rows)


def place_ring(plan, rims, layers, levels, points, mixed, where, right):
    def store(at, column, depth, got, present):
        shift = (column // 3 - 1, column % 3 - 1, depth - (plan.blocks - 1) // 2)
        spots = [
            plan.unit * (got[axis] + jnp.asarray(shift[axis], jnp.float32)) for axis in range(3)
        ]
        spots[0] = jnp.where(present, spots[0], FAR)
        points[at, pl.ds(3, 1), :] = spots[0] * spots[0] + spots[1] * spots[1] + spots[2] * spots[2]
        points[at, pl.ds(4, 1), :] = jnp.ones((1, LANES), jnp.float32)
        points[at, pl.ds(5, 3), :] = jnp.zeros((3, LANES), jnp.float32)
        mixed[at, pl.ds(3, 1), :] = jnp.ones((1, LANES), jnp.float32)
        mixed[at, pl.ds(7, 1), :] = jnp.zeros((1, LANES), jnp.float32)
        for axis in range(3):
            points[at, pl.ds(axis, 1), :] = spots[axis]
            where[at, pl.ds(axis, 1), :] = spots[axis]
            mixed[at, pl.ds(4 + axis, 1), :] = spots[axis]
            field = jnp.where(present, got[3 + axis], 0.0)
            right[at, pl.ds(axis, 1), :] = field
            mixed[at, pl.ds(axis, 1), :] = field

    gather_ring(plan, rims, slots(plan, rims, 2), layers, 6, store, levels)


def flip_points(plan, levels, points, flipped):
    for column in range(9):
        for level in levels:
            at = column * plan.deep + level
            first, second, third = split(points[at])
            stacked = jnp.concatenate([first, second, third, first, second, first], axis=0)
            flipped[pl.ds(at * plan.width, plan.width), :] = jnp.transpose(stacked).astype(jnp.bfloat16)


def weigh(plan, flipped, centre, level, number, columns, tiles, base):
    for column in columns:
        span = number * plan.width
        rest = jnp.dot(
            flipped[pl.ds((column * plan.deep + level) * plan.width, span), :],
            centre, preferred_element_type=jnp.float32,
        )
        bump = jnp.maximum(rest, 0.0)
        weight = bump * bump * bump
        high = weight.astype(jnp.bfloat16)
        spot = pl.ds(base + column * span, span)
        tiles[spot, pl.ds(0, LANES)] = high
        tiles[spot, pl.ds(LANES, LANES)] = (weight - high.astype(jnp.float32)).astype(jnp.bfloat16)


def inner_kernel(plan, recv, tiles, where, right, centres, partial, points, flipped, mixed, packed):
    levels = range(plan.blocks)
    place_ring(plan, rims_of(plan), [recv], levels, points, mixed, where, right)
    flip_points(plan, levels, points, flipped)
    split_ring(plan, mixed, packed, levels)
    sub = sublane_ids()
    for block in range(plan.blocks):
        own = points[plan.own(block)]
        own = jnp.where(jnp.logical_and(sub == 0, own > 0.25 * FAR), -FAR, own)
        square = jnp.broadcast_to(own[3:4], (8, LANES))
        own = jnp.where(sub < 3, 2.0 * own, 0.0)
        own = jnp.where(sub == 3, -1.0, own)
        own = jnp.where(sub == 4, plan.cube - square, own)
        first, second, third = split(own)
        stacked = jnp.concatenate([first, first, first, second, second, third], axis=0)
        centre = stacked.astype(jnp.bfloat16)
        centres[block] = centre
        low, number = inner_span(plan, block)
        base = inner_base(plan, block)
        total = None
        for columns in groups_of(number):
            weigh(plan, flipped, centre, low, number, columns, tiles, base)
            part = tile_sum(plan, tiles, base, packed, low, number, columns)
            total = part if total is None else total + part
        partial[block] = fold(total)


def edge_kernel(plan, *refs):
    others = refs[:-14]
    (
        near_where, near_right, centres, partial,
        send, outer, where, right, state, points, flipped, mixed, packed, rows,
    ) = refs[-14:]
    rims = rims_of(plan)
    levels = range(plan.blocks, plan.deep)
    place_ring(plan, rims, [None, *others], levels, points, mixed, where, right)
    for column in range(9):
        for level in range(plan.blocks):
            at = column * plan.deep + level
            where[at] = near_where[at]
            right[at] = near_right[at]
    flip_points(plan, levels, points, flipped)
    split_ring(plan, mixed, packed, levels)
    for block in range(plan.blocks):
        rows[block] = partial[block]

    def before(e, columns):
        centre = centres[rims[e][1]]
        weigh(plan, flipped, centre, plan.blocks + e, 1, columns, outer, e * 9 * plan.width)

    add_rims(plan, rims, outer, packed, rows, before)
    image = [[None] * plan.blocks for _ in range(3)]
    whole = [[None] * plan.blocks for _ in range(3)]
    start = [[None] * plan.blocks for _ in range(3)]
    for block in range(plan.blocks):
        own = plan.own(block)
        reach = rows[block, pl.ds(3, 1), :]
        state[pl.ds(block, 1), :] = reach
        for axis in range(3):
            field = right[own, pl.ds(axis, 1), :]
            start[axis][block] = field
            image[axis][block] = reach * field - rows[block, pl.ds(axis, 1), :]
            whole[axis][block] = field + VISCOUS * image[axis][block]
            spot = where[own, pl.ds(axis, 1), :]
            state[pl.ds((1 + axis) * plan.blocks + block, 1), :] = (
                reach * spot - rows[block, pl.ds(4 + axis, 1), :]
            )
    groups = [
        [dot(start[axis], start[axis]) for axis in range(3)],
        [dot(start[axis], whole[axis]) for axis in range(3)],
        [dot(whole[axis], whole[axis]) for axis in range(3)],
    ]
    spread(send, sum(image, []) + [pack(groups)])


def second_kernel(plan, recv, tiles, outer, right, state, send, residual, direction, scalars, image, packed, rows):
    rims = rims_of(plan)
    ring_into(plan, rims, recv, 3, image)
    current, curve, square = totals(recv, 3 * plan.blocks, 3)
    alpha = current / curve
    following = jnp.maximum(alpha * alpha * square - current, 0.0)
    beta = following / current
    for at in range(plan.ring):
        field = right[at]
        left = field - alpha * (field + VISCOUS * image[at])
        residual[at] = left
        direction[at] = left + beta * field
    scalars[plan.blocks] = alpha
    for block in range(plan.blocks):
        scalars[block] = image[plan.own(block)]
    apply_tiles(plan, rims, tiles, outer, direction, packed, rows)
    out = []
    groups = [[], [], [], []]
    for axis in range(3):
        left, ahead, shot, whole = [], [], [], []
        for block in range(plan.blocks):
            own = plan.own(block)
            left.append(residual[own, pl.ds(axis, 1), :])
            ahead.append(direction[own, pl.ds(axis, 1), :])
            shot.append(state[pl.ds(block, 1), :] * ahead[block] - rows[block, pl.ds(axis, 1), :])
            whole.append(ahead[block] + VISCOUS * shot[block])
        out.extend(shot)
        groups[0].append(dot(left, left))
        groups[1].append(dot(ahead, whole))
        groups[2].append(dot(left, whole))
        groups[3].append(dot(whole, whole))
    spread(send, out + [pack(groups)])


def third_kernel(
    plan, recv, tiles, outer, where, right, residual, direction, state, scalars,
    send, ends, image, sofar, ahead, steps, packed, rows,
):
    rims = rims_of(plan)
    ring_into(plan, rims, recv, 3, image)
    current, curve, cross, square = totals(recv, 3 * plan.blocks, 4)
    alpha = current / curve
    following = jnp.maximum(current - 2.0 * alpha * cross + alpha * alpha * square, 0.0)
    beta = following / current
    first = scalars[plan.blocks]
    steps[...] = alpha
    sub = sublane_ids()
    for block in range(plan.blocks):
        own = plan.own(block)
        rows[block] = first * scalars[block] + alpha * image[own]
    latest = [
        [rows[block, pl.ds(axis, 1), :] for axis in range(3)] for block in range(plan.blocks)
    ]
    for at in range(plan.ring):
        field = direction[at]
        rest = residual[at] - alpha * (field + VISCOUS * image[at])
        fresh = rest + beta * field
        spot = where[at]
        made = first * right[at] + alpha * field
        moved = made * spot
        moved = pltpu.roll(moved, 6, 0) + pltpu.roll(moved, 5, 0) + pltpu.roll(moved, 4, 0)
        joined = jnp.where(sub < 3, fresh, pltpu.roll(fresh * spot, 3, 0))
        ahead[at] = jnp.where(sub < 6, joined, moved)
        if at - plan.own(0) in range(plan.blocks):
            image[at] = rest
            sofar[at - plan.own(0)] = made
    apply_tiles(plan, rims, tiles, outer, ahead, packed, rows)
    scale = 1.0 / plan.unit
    base = []
    each = [[None] * plan.blocks for _ in range(3)]
    rests = [[None] * plan.blocks for _ in range(3)]
    heads = [[None] * plan.blocks for _ in range(3)]
    wholes = [[None] * plan.blocks for _ in range(3)]
    for block in range(plan.blocks):
        reach = state[pl.ds(block, 1), :]
        own = plan.own(block)
        total = rows[block, pl.ds(6, 1), :] - reach * ahead[own, pl.ds(6, 1), :]
        for axis in range(3):
            head = ahead[own, pl.ds(axis, 1), :]
            spot = where[own, pl.ds(axis, 1), :]
            lean = state[pl.ds((1 + axis) * plan.blocks + block, 1), :]
            shot = reach * head - rows[block, pl.ds(axis, 1), :]
            twice = reach * ahead[own, pl.ds(3 + axis, 1), :] - rows[block, pl.ds(3 + axis, 1), :]
            each[axis][block] = scale * (spot * shot + head * lean - twice)
            made = sofar[block, pl.ds(axis, 1), :]
            total = total + spot * latest[block][axis] + made * lean
            rests[axis][block] = image[own, pl.ds(axis, 1), :]
            heads[axis][block] = head
            wholes[axis][block] = head + VISCOUS * shot
            ends[pl.ds(axis * plan.blocks + block, 1), :] = made
            ends[pl.ds((3 + axis) * plan.blocks + block, 1), :] = head
        base.append(scale * total)
    groups = [
        [dot(rests[axis], rests[axis]) for axis in range(3)],
        [dot(heads[axis], wholes[axis]) for axis in range(3)],
    ]
    spread(send, base + sum(each, []) + [pack(groups)])


def fourth_kernel(plan, recv, tiles, outer, state, send, source, steps, parts, packed, rows):
    rims = rims_of(plan)
    ring_into(plan, rims, recv, 4, parts)
    current, curve = totals(recv, 4 * plan.blocks, 2)
    sub = sublane_ids()
    steps[...] = current / curve
    factor = jnp.where(sub == 0, 1.0, pltpu.roll(steps[...], 1, 0))
    for at in range(plan.ring):
        gathered = jnp.where(sub < 4, parts[at] * factor, 0.0)
        source[at] = jnp.broadcast_to(-jnp.sum(gathered, axis=0, keepdims=True), (8, LANES))
    apply_tiles(plan, rims, tiles, outer, source, packed, rows)
    field, shot, whole = [], [], []
    for block in range(plan.blocks):
        field.append(source[plan.own(block), pl.ds(0, 1), :])
        shot.append(state[pl.ds(block, 1), :] * field[block] - rows[block, pl.ds(0, 1), :])
        whole.append(STIFFNESS * field[block] + shot[block])
    groups = [[dot(field, field)], [dot(field, whole)], [dot(whole, whole)]]
    spread(send, shot + [pack(groups)])


def fifth_kernel(plan, recv, tiles, outer, source, state, send, ends, image, ahead, steps, packed, rows):
    rims = rims_of(plan)
    ring_into(plan, rims, recv, 1, image)
    current, curve, square = totals(recv, plan.blocks, 3)
    steps[...] = current / curve
    alpha = steps[pl.ds(0, 1), :]
    steps[...] = jnp.maximum(alpha * alpha * square - current, 0.0) / current
    beta = steps[pl.ds(0, 1), :]
    for at in range(plan.ring):
        field = source[at]
        left = field - alpha * (STIFFNESS * field + image[at])
        image[at] = left
        ahead[at] = left + beta * field
    apply_tiles(plan, rims, tiles, outer, ahead, packed, rows)
    rests, heads, wholes = [], [], []
    for block in range(plan.blocks):
        own = plan.own(block)
        rests.append(image[own, pl.ds(0, 1), :])
        heads.append(ahead[own, pl.ds(0, 1), :])
        shot = state[pl.ds(block, 1), :] * heads[block] - rows[block, pl.ds(0, 1), :]
        wholes.append(STIFFNESS * heads[block] + shot)
        ends[pl.ds(block, 1), :] = alpha * source[own, pl.ds(0, 1), :]
        ends[pl.ds(plan.blocks + block, 1), :] = heads[block]
    spread(send, [pack([[dot(rests, rests)], [dot(heads, wholes)]])])


def last_kernel(plan, recv, speeds, final, ends, star, pressure, steps):
    current, curve = totals(recv, 0, 2)
    steps[...] = current / curve
    alpha = steps[pl.ds(0, 1), :]
    for block in range(plan.blocks):
        pressure[block] = (
            ends[pl.ds(block, 1), :] + alpha * ends[pl.ds(plan.blocks + block, 1), :]
        )
    for axis in range(3):
        alpha = final[pl.ds(axis, 1), :]
        for block in range(plan.blocks):
            at = axis * plan.blocks + block
            star[at] = (
                speeds[pl.ds(at, 1), :] + alpha * speeds[pl.ds(3 * plan.blocks + at, 1), :]
            )


def call(plan, kernel, operands, outs, scratch=(), space=pltpu.VMEM):
    typed = lambda shape: (shape, jnp.float32) if isinstance(shape[0], int) else shape
    held = lambda item: pltpu.VMEM(*typed(item)) if isinstance(item, tuple) else item
    return pl.pallas_call(
        functools.partial(kernel, plan),
        out_shape=[jax.ShapeDtypeStruct(*typed(shape)) for shape in outs],
        in_specs=[pl.BlockSpec(memory_space=space) for _ in operands],
        out_specs=[pl.BlockSpec(memory_space=pltpu.VMEM) for _ in outs],
        scratch_shapes=[held(item) for item in scratch],
        compiler_params=pltpu.CompilerParams(vmem_limit_bytes=24 * 1024 * 1024),
        name=kernel.__name__,
    )(*operands)


def local(mesh, offsets, velocity, counts, neighbours):
    blocks = counts.shape[2]
    width = offsets.shape[-1]
    plan = Plan(mesh, blocks, width)
    lined = lambda field: field.transpose(0, 1, 3, 2, 4).reshape(3 * blocks, 1, width)
    slot = lambda rows: (plan.devices, rows, 1, width)
    ring = (plan.ring, 8, width)
    tile = (8, width)
    rows = (blocks, 8, width)
    packed = ((32, plan.ring * width), jnp.bfloat16)
    (send,) = call(
        plan, pack_kernel,
        [
            pltpu.with_memory_space_constraint(field, pltpu.HBM)
            for field in (counts.reshape(1, blocks), lined(offsets), lined(velocity))
        ],
        [(plan.count[0] * plan.count[1], 6 * blocks, 1, width)],
        [
            pltpu.SMEM((1, blocks), jnp.int32), (3 * blocks, 1, width), (3 * blocks, 1, width),
            pltpu.SemaphoreType.DMA((3,)),
        ],
        pltpu.HBM,
    )
    level, *others = exchange_layers(plan, send)
    flipped = ((plan.ring * width, 48), jnp.bfloat16)
    tiles, where, right, centres, partial = call(
        plan, inner_kernel, [level],
        [
            ((inner_base(plan, blocks), 2 * width), jnp.bfloat16), ring, ring,
            ((blocks, 48, width), jnp.bfloat16), rows,
        ],
        [ring, flipped, ring, packed],
    )
    send, outer, where, right, state = call(
        plan, edge_kernel, [*others, where, right, centres, partial],
        [
            slot(3 * blocks + 1), ((plan.rims * 9 * width, 2 * width), jnp.bfloat16),
            ring, ring, (4 * blocks, width),
        ],
        [ring, flipped, ring, packed, rows],
    )
    recv = exchange(send)
    send, residual, direction, scalars = call(
        plan, second_kernel, [recv, tiles, outer, right, state],
        [slot(3 * blocks + 1), ring, ring, (blocks + 1, 8, width)],
        [ring, packed, rows],
    )
    recv = exchange(send)
    send, speeds = call(
        plan, third_kernel, [recv, tiles, outer, where, right, residual, direction, state, scalars],
        [slot(4 * blocks + 1), (6 * blocks, width)],
        [ring, rows, ring, tile, packed, rows],
    )
    recv = exchange(send)
    send, source, final = call(
        plan, fourth_kernel, [recv, tiles, outer, state],
        [slot(blocks + 1), ring, tile],
        [ring, packed, rows],
    )
    recv = exchange(send)
    send, ends = call(
        plan, fifth_kernel, [recv, tiles, outer, source, state],
        [slot(1), (2 * blocks, width)],
        [ring, ring, tile, packed, rows],
    )
    recv = exchange(send)
    star, pressure = call(
        plan, last_kernel, [recv, speeds, final, ends],
        [(3 * blocks, 1, width), (blocks, 1, width)], [tile],
    )
    star = star.reshape(3, 1, blocks, 1, width).transpose(0, 1, 3, 2, 4)
    pressure = pressure.reshape(1, blocks, 1, width).transpose(0, 2, 1, 3)
    return star, pressure


def solution(mesh):
    in_specs = (
        P(None, "gx", "gy", "gz", None),
        P(None, "gx", "gy", "gz", None),
        P("gx", "gy", "gz"),
        P("gx", "gy", "gz", None),
    )
    out_specs = (P(None, "gx", "gy", "gz", None), P("gx", "gy", "gz", None))
    return jax.shard_map(
        functools.partial(local, mesh),
        mesh=mesh, in_specs=in_specs, out_specs=out_specs, check_vma=False,
    )
```

```python
import functools

import jax
import jax.numpy as jnp
from jax import lax
from jax.experimental import pallas as pl
from jax.experimental.pallas import tpu as pltpu
from jax.sharding import PartitionSpec as P

VISCOUS = 4.0
STIFFNESS = 0.25
GRAVITY_STEP = 0.5
AXES = ("gx", "gy", "gz")
FAR = 1.0e3
LANES = 128


def exchange(send):
    return lax.all_to_all(send, AXES, 0, 0, tiled=True)


def exchange_layers(plan, send):
    level = lax.all_to_all(send, AXES[:2], 0, 0, tiled=True)
    deep = plan.count[2]
    if deep == 2:
        return [level, lax.ppermute(level, AXES[2], [(0, 1), (1, 0)])]
    forward = [(i, i + 1) for i in range(deep - 1)]
    backward = [(target, source) for source, target in forward]
    return [level] + [lax.ppermute(level, AXES[2], pairs) for pairs in (forward, backward)]


class Plan:
    def __init__(self, mesh, blocks, width):
        self.count = [mesh.shape[axis] for axis in AXES]
        self.devices = self.count[0] * self.count[1] * self.count[2]
        self.blocks = blocks
        self.width = width
        self.rims = 1 if self.count[2] == 2 else 2
        self.deep = blocks + self.rims
        self.ring = 9 * self.deep
        self.cube = (2.0 / width) ** (1.0 / 3.0)
        self.unit = self.cube ** 0.5

    def own(self, block):
        return 4 * self.deep + block


def rims_of(plan):
    last = plan.blocks - 1
    if plan.rims == 2:
        return [(-1, 0, last, -1), (1, last, 0, plan.blocks)]
    above = lax.axis_index(AXES[2]) == 0
    choose = lambda yes, no: jnp.where(above, jnp.int32(yes), jnp.int32(no))
    return [(choose(1, -1), choose(last, 0), choose(0, last), choose(plan.blocks, -1))]


def slots(plan, rims, axes=3):
    place = [lax.axis_index(axis) for axis in AXES]
    found = []
    for column in range(9):
        beside = []
        for step in [0] + [rim[0] for rim in rims]:
            at = [place[0] + column // 3 - 1, place[1] + column % 3 - 1, place[2] + step]
            present = None
            slot = 0
            for axis, (value, count) in enumerate(zip(at, plan.count)):
                inside = jnp.logical_and(value >= 0, value < count)
                present = inside if present is None else jnp.logical_and(present, inside)
                if axis < axes:
                    slot = slot * count + jnp.clip(value, 0, count - 1)
            beside.append((slot, present))
        found.append(beside)
    return found


def gather_ring(plan, rims, found, layers, fields, store, levels=None):
    for column in range(9):
        for level in levels or range(plan.deep):
            layer, block, depth = 0, level, level
            if level >= plan.blocks:
                layer = level - plan.blocks + 1
                block, depth = rims[layer - 1][2:]
            slot, present = found[column][layer]
            rows = [layers[layer][slot, field * plan.blocks + block] for field in range(fields)]
            store(column * plan.deep + level, column, depth, rows, present)


def ring_into(plan, rims, recv, fields, ref):
    def store(at, column, depth, rows, present):
        for field, row in enumerate(rows):
            ref[at, pl.ds(field, 1), :] = row

    gather_ring(plan, rims, slots(plan, rims), [recv] * (1 + plan.rims), fields, store)


def lane_ids(sublanes=1):
    return lax.broadcasted_iota(jnp.int32, (sublanes, LANES), 1)


def sublane_ids():
    return lax.broadcasted_iota(jnp.int32, (8, LANES), 0)


def totals(recv, row, number):
    summed = jnp.broadcast_to(jnp.sum(recv[:, row], axis=0), (8, LANES))
    place = lane_ids(8) - sublane_ids()
    return [
        jnp.broadcast_to(
            jnp.sum(jnp.where(place == 8 * m, summed, 0.0), axis=1, keepdims=True), (8, LANES)
        )
        for m in range(number)
    ]


def pack(groups):
    lane = lane_ids()
    row = jnp.zeros((1, LANES), jnp.float32)
    for m, group in enumerate(groups):
        for c, partial in enumerate(group):
            row = jnp.where(lane == 8 * m + c, jnp.sum(partial, axis=1, keepdims=True), row)
    return row


def dot(first, second):
    total = first[0] * second[0]
    for a, b in zip(first[1:], second[1:]):
        total = total + a * b
    return total


def spread(send, rows):
    def body(slot, carry):
        for r, row in enumerate(rows):
            send[slot, r] = row
        return carry

    lax.fori_loop(0, send.shape[0], body, 0, unroll=4)


def coarse(value):
    return value.astype(jnp.bfloat16).astype(jnp.float32)


def split(value):
    first = coarse(value)
    rest = value - first
    second = coarse(rest)
    return first, second, rest - second


def stack_full(value):
    first, second, third = split(value)
    return jnp.concatenate([first, second, third, jnp.zeros_like(third)], axis=0)


def fold_full(total):
    both = total[:, :LANES] + total[:, LANES:]
    return both[0:8] + both[8:16] + both[16:24]


def stack_three(value):
    first, second, third = split(value)
    joined = jnp.where(sublane_ids() < 3, first, pltpu.roll(second, 3, 0))
    return jnp.concatenate([joined, third], axis=0)


def fold_three(total):
    both = total[:, :LANES] + total[:, LANES:]
    return both[0:8] + pltpu.roll(both[0:8], 5, 0) + both[8:16]


def stack_one(value):
    first, second, third = split(value)
    sub = sublane_ids()
    joined = jnp.where(sub == 0, first, jnp.where(sub == 1, second, third))
    return jnp.concatenate([jnp.where(sub < 3, joined, 0.0), jnp.zeros_like(third)], axis=0)


def fold_one(total):
    both = total[0:8, :LANES] + total[0:8, LANES:]
    return jnp.broadcast_to(jnp.sum(both, axis=0, keepdims=True), (8, LANES))


FULL = (stack_full, fold_full)
THREE = (stack_three, fold_three)
ONE = (stack_one, fold_one)


def split_ring(plan, ring, packed, form, levels=None):
    for column in range(9):
        for level in levels or range(plan.deep):
            at = column * plan.deep + level
            packed[:, pl.ds(at * LANES, LANES)] = form[0](ring[at]).astype(jnp.bfloat16)


def inner_span(plan, block):
    low = max(block - 1, 0)
    return low, min(block + 2, plan.blocks) - low


def inner_base(plan, block):
    return 9 * sum(inner_span(plan, before)[1] for before in range(block)) * plan.width


def groups_of(number):
    size = 3 if number % 2 == 0 else 4 if number == 1 else 2
    return [range(c, min(c + size, 9)) for c in range(0, 9, size)]


def tile_sum(plan, tiles, base, packed, level, number, columns):
    span = number * plan.width
    ahead = [packed[:, pl.ds((c * plan.deep + level) * LANES, span)] for c in columns]
    return jnp.dot(
        jnp.concatenate(ahead, axis=1) if len(ahead) > 1 else ahead[0],
        tiles[pl.ds(base + columns[0] * span, len(ahead) * span), :],
        preferred_element_type=jnp.float32,
    )


def apply_tiles(plan, rims, tiles, outer, ring, packed, rows, form):
    split_ring(plan, ring, packed, form)
    for block in range(plan.blocks):
        low, number = inner_span(plan, block)
        base = inner_base(plan, block)
        total = None
        for columns in groups_of(number):
            part = tile_sum(plan, tiles, base, packed, low, number, columns)
            total = part if total is None else total + part
        rows[block] = form[1](total)
    add_rims(plan, rims, outer, packed, rows, form, lambda e, columns: None)


def add_rims(plan, rims, outer, packed, rows, form, before):
    for e, rim in enumerate(rims):
        total = None
        for columns in groups_of(1):
            before(e, columns)
            base = e * 9 * plan.width
            part = tile_sum(plan, outer, base, packed, plan.blocks + e, 1, columns)
            total = part if total is None else total + part
        rows[rim[1]] = rows[rim[1]] + form[1](total)


def pack_kernel(plan, counts_in, offsets_in, velocity_in, send, counts, offsets, velocity, sems):
    pairs = [(counts_in, counts), (offsets_in, offsets), (velocity_in, velocity)]
    copies = [pltpu.make_async_copy(a, b, sems.at[i]) for i, (a, b) in enumerate(pairs)]
    for copy in copies:
        copy.start()
    for copy in copies:
        copy.wait()
    lane = lane_ids()
    rows = []
    for axis in range(3):
        for block in range(plan.blocks):
            valid = lane < counts[0, block]
            row = offsets[axis * plan.blocks + block]
            rows.append(jnp.where(valid, row, FAR) if axis == 0 else row)
    for axis in range(3):
        for block in range(plan.blocks):
            valid = lane < counts[0, block]
            row = velocity[axis * plan.blocks + block]
            if axis == 0:
                row = row + GRAVITY_STEP
            rows.append(jnp.where(valid, row, 0.0))
    spread(send, rows)


def place_ring(plan, rims, layers, levels, points, mixed, where, right):
    def store(at, column, depth, got, present):
        shift = (column // 3 - 1, column % 3 - 1, depth - (plan.blocks - 1) // 2)
        spots = [
            plan.unit * (got[axis] + jnp.asarray(shift[axis], jnp.float32)) for axis in range(3)
        ]
        spots[0] = jnp.where(present, spots[0], FAR)
        points[at, pl.ds(3, 1), :] = spots[0] * spots[0] + spots[1] * spots[1] + spots[2] * spots[2]
        points[at, pl.ds(4, 1), :] = jnp.ones((1, LANES), jnp.float32)
        points[at, pl.ds(5, 3), :] = jnp.zeros((3, LANES), jnp.float32)
        mixed[at, pl.ds(3, 1), :] = jnp.ones((1, LANES), jnp.float32)
        mixed[at, pl.ds(7, 1), :] = jnp.zeros((1, LANES), jnp.float32)
        for axis in range(3):
            points[at, pl.ds(axis, 1), :] = spots[axis]
            where[at, pl.ds(axis, 1), :] = spots[axis]
            mixed[at, pl.ds(4 + axis, 1), :] = spots[axis]
            field = jnp.where(present, got[3 + axis], 0.0)
            right[at, pl.ds(axis, 1), :] = field
            mixed[at, pl.ds(axis, 1), :] = field

    gather_ring(plan, rims, slots(plan, rims, 2), layers, 6, store, levels)


def flip_points(plan, levels, points, flipped):
    for column in range(9):
        for level in levels:
            at = column * plan.deep + level
            first, second, third = split(points[at])
            stacked = jnp.concatenate([first, second, third, first, second, first], axis=0)
            flipped[pl.ds(at * plan.width, plan.width), :] = jnp.transpose(stacked).astype(jnp.bfloat16)


def weigh(plan, flipped, centre, level, number, columns, tiles, base):
    for column in columns:
        span = number * plan.width
        rest = jnp.dot(
            flipped[pl.ds((column * plan.deep + level) * plan.width, span), :],
            centre, preferred_element_type=jnp.float32,
        )
        bump = jnp.maximum(rest, 0.0)
        weight = bump * bump * bump
        high = weight.astype(jnp.bfloat16)
        spot = pl.ds(base + column * span, span)
        tiles[spot, pl.ds(0, LANES)] = high
        tiles[spot, pl.ds(LANES, LANES)] = (weight - high.astype(jnp.float32)).astype(jnp.bfloat16)


def inner_kernel(plan, recv, tiles, where, right, centres, partial, points, flipped, mixed, packed):
    levels = range(plan.blocks)
    place_ring(plan, rims_of(plan), [recv], levels, points, mixed, where, right)
    flip_points(plan, levels, points, flipped)
    split_ring(plan, mixed, packed, FULL, levels)
    sub = sublane_ids()
    for block in range(plan.blocks):
        own = points[plan.own(block)]
        own = jnp.where(jnp.logical_and(sub == 0, own > 0.25 * FAR), -FAR, own)
        square = jnp.broadcast_to(own[3:4], (8, LANES))
        own = jnp.where(sub < 3, 2.0 * own, 0.0)
        own = jnp.where(sub == 3, -1.0, own)
        own = jnp.where(sub == 4, plan.cube - square, own)
        first, second, third = split(own)
        stacked = jnp.concatenate([first, first, first, second, second, third], axis=0)
        centre = stacked.astype(jnp.bfloat16)
        centres[block] = centre
        low, number = inner_span(plan, block)
        base = inner_base(plan, block)
        total = None
        for columns in groups_of(number):
            weigh(plan, flipped, centre, low, number, columns, tiles, base)
            part = tile_sum(plan, tiles, base, packed, low, number, columns)
            total = part if total is None else total + part
        partial[block] = fold_full(total)


def edge_kernel(plan, *refs):
    others = refs[:-14]
    (
        near_where, near_right, centres, partial,
        send, outer, where, right, state, points, flipped, mixed, packed, rows,
    ) = refs[-14:]
    rims = rims_of(plan)
    levels = range(plan.blocks, plan.deep)
    place_ring(plan, rims, [None, *others], levels, points, mixed, where, right)
    for column in range(9):
        for level in range(plan.blocks):
            at = column * plan.deep + level
            where[at] = near_where[at]
            right[at] = near_right[at]
    flip_points(plan, levels, points, flipped)
    split_ring(plan, mixed, packed, FULL, levels)
    for block in range(plan.blocks):
        rows[block] = partial[block]

    def before(e, columns):
        centre = centres[rims[e][1]]
        weigh(plan, flipped, centre, plan.blocks + e, 1, columns, outer, e * 9 * plan.width)

    add_rims(plan, rims, outer, packed, rows, FULL, before)
    image = [[None] * plan.blocks for _ in range(3)]
    whole = [[None] * plan.blocks for _ in range(3)]
    start = [[None] * plan.blocks for _ in range(3)]
    for block in range(plan.blocks):
        own = plan.own(block)
        reach = rows[block, pl.ds(3, 1), :]
        state[pl.ds(block, 1), :] = reach
        for axis in range(3):
            field = right[own, pl.ds(axis, 1), :]
            start[axis][block] = field
            image[axis][block] = reach * field - rows[block, pl.ds(axis, 1), :]
            whole[axis][block] = field + VISCOUS * image[axis][block]
            spot = where[own, pl.ds(axis, 1), :]
            state[pl.ds((1 + axis) * plan.blocks + block, 1), :] = (
                reach * spot - rows[block, pl.ds(4 + axis, 1), :]
            )
    groups = [
        [dot(start[axis], start[axis]) for axis in range(3)],
        [dot(start[axis], whole[axis]) for axis in range(3)],
        [dot(whole[axis], whole[axis]) for axis in range(3)],
    ]
    spread(send, sum(image, []) + [pack(groups)])


def second_kernel(plan, recv, tiles, outer, right, state, send, residual, direction, scalars, image, packed, rows):
    rims = rims_of(plan)
    ring_into(plan, rims, recv, 3, image)
    current, curve, square = totals(recv, 3 * plan.blocks, 3)
    alpha = current / curve
    following = jnp.maximum(alpha * alpha * square - current, 0.0)
    beta = following / current
    for at in range(plan.ring):
        field = right[at]
        left = field - alpha * (field + VISCOUS * image[at])
        residual[at] = left
        direction[at] = left + beta * field
    scalars[plan.blocks] = alpha
    for block in range(plan.blocks):
        scalars[block] = image[plan.own(block)]
    apply_tiles(plan, rims, tiles, outer, direction, packed, rows, THREE)
    out = []
    groups = [[], [], [], []]
    for axis in range(3):
        left, ahead, shot, whole = [], [], [], []
        for block in range(plan.blocks):
            own = plan.own(block)
            left.append(residual[own, pl.ds(axis, 1), :])
            ahead.append(direction[own, pl.ds(axis, 1), :])
            shot.append(state[pl.ds(block, 1), :] * ahead[block] - rows[block, pl.ds(axis, 1), :])
            whole.append(ahead[block] + VISCOUS * shot[block])
        out.extend(shot)
        groups[0].append(dot(left, left))
        groups[1].append(dot(ahead, whole))
        groups[2].append(dot(left, whole))
        groups[3].append(dot(whole, whole))
    spread(send, out + [pack(groups)])


def third_kernel(
    plan, recv, tiles, outer, where, right, residual, direction, state, scalars,
    send, ends, image, sofar, ahead, steps, packed, rows,
):
    rims = rims_of(plan)
    ring_into(plan, rims, recv, 3, image)
    current, curve, cross, square = totals(recv, 3 * plan.blocks, 4)
    alpha = current / curve
    following = jnp.maximum(current - 2.0 * alpha * cross + alpha * alpha * square, 0.0)
    beta = following / current
    first = scalars[plan.blocks]
    steps[...] = alpha
    sub = sublane_ids()
    for block in range(plan.blocks):
        own = plan.own(block)
        rows[block] = first * scalars[block] + alpha * image[own]
    latest = [
        [rows[block, pl.ds(axis, 1), :] for axis in range(3)] for block in range(plan.blocks)
    ]
    for at in range(plan.ring):
        field = direction[at]
        rest = residual[at] - alpha * (field + VISCOUS * image[at])
        fresh = rest + beta * field
        spot = where[at]
        made = first * right[at] + alpha * field
        moved = made * spot
        moved = pltpu.roll(moved, 6, 0) + pltpu.roll(moved, 5, 0) + pltpu.roll(moved, 4, 0)
        joined = jnp.where(sub < 3, fresh, pltpu.roll(fresh * spot, 3, 0))
        ahead[at] = jnp.where(sub < 6, joined, moved)
        if at - plan.own(0) in range(plan.blocks):
            image[at] = rest
            sofar[at - plan.own(0)] = made
    apply_tiles(plan, rims, tiles, outer, ahead, packed, rows, FULL)
    scale = 1.0 / plan.unit
    base = []
    each = [[None] * plan.blocks for _ in range(3)]
    rests = [[None] * plan.blocks for _ in range(3)]
    heads = [[None] * plan.blocks for _ in range(3)]
    wholes = [[None] * plan.blocks for _ in range(3)]
    for block in range(plan.blocks):
        reach = state[pl.ds(block, 1), :]
        own = plan.own(block)
        total = rows[block, pl.ds(6, 1), :] - reach * ahead[own, pl.ds(6, 1), :]
        for axis in range(3):
            head = ahead[own, pl.ds(axis, 1), :]
            spot = where[own, pl.ds(axis, 1), :]
            lean = state[pl.ds((1 + axis) * plan.blocks + block, 1), :]
            shot = reach * head - rows[block, pl.ds(axis, 1), :]
            twice = reach * ahead[own, pl.ds(3 + axis, 1), :] - rows[block, pl.ds(3 + axis, 1), :]
            each[axis][block] = scale * (spot * shot + head * lean - twice)
            made = sofar[block, pl.ds(axis, 1), :]
            total = total + spot * latest[block][axis] + made * lean
            rests[axis][block] = image[own, pl.ds(axis, 1), :]
            heads[axis][block] = head
            wholes[axis][block] = head + VISCOUS * shot
            ends[pl.ds(axis * plan.blocks + block, 1), :] = made
            ends[pl.ds((3 + axis) * plan.blocks + block, 1), :] = head
        base.append(scale * total)
    groups = [
        [dot(rests[axis], rests[axis]) for axis in range(3)],
        [dot(heads[axis], wholes[axis]) for axis in range(3)],
    ]
    spread(send, base + sum(each, []) + [pack(groups)])


def fourth_kernel(plan, recv, tiles, outer, state, send, source, steps, parts, packed, rows):
    rims = rims_of(plan)
    ring_into(plan, rims, recv, 4, parts)
    current, curve = totals(recv, 4 * plan.blocks, 2)
    sub = sublane_ids()
    steps[...] = current / curve
    factor = jnp.where(sub == 0, 1.0, pltpu.roll(steps[...], 1, 0))
    for at in range(plan.ring):
        gathered = jnp.where(sub < 4, parts[at] * factor, 0.0)
        source[at] = jnp.broadcast_to(-jnp.sum(gathered, axis=0, keepdims=True), (8, LANES))
    apply_tiles(plan, rims, tiles, outer, source, packed, rows, ONE)
    field, shot, whole = [], [], []
    for block in range(plan.blocks):
        field.append(source[plan.own(block), pl.ds(0, 1), :])
        shot.append(state[pl.ds(block, 1), :] * field[block] - rows[block, pl.ds(0, 1), :])
        whole.append(STIFFNESS * field[block] + shot[block])
    groups = [[dot(field, field)], [dot(field, whole)], [dot(whole, whole)]]
    spread(send, shot + [pack(groups)])


def fifth_kernel(plan, recv, tiles, outer, source, state, send, ends, image, ahead, steps, packed, rows):
    rims = rims_of(plan)
    ring_into(plan, rims, recv, 1, image)
    current, curve, square = totals(recv, plan.blocks, 3)
    steps[...] = current / curve
    alpha = steps[pl.ds(0, 1), :]
    steps[...] = jnp.maximum(alpha * alpha * square - current, 0.0) / current
    beta = steps[pl.ds(0, 1), :]
    for at in range(plan.ring):
        field = source[at]
        left = field - alpha * (STIFFNESS * field + image[at, pl.ds(0, 1), :])
        image[at] = left
        ahead[at] = left + beta * field
    apply_tiles(plan, rims, tiles, outer, ahead, packed, rows, ONE)
    rests, heads, wholes = [], [], []
    for block in range(plan.blocks):
        own = plan.own(block)
        rests.append(image[own, pl.ds(0, 1), :])
        heads.append(ahead[own, pl.ds(0, 1), :])
        shot = state[pl.ds(block, 1), :] * heads[block] - rows[block, pl.ds(0, 1), :]
        wholes.append(STIFFNESS * heads[block] + shot)
        ends[pl.ds(block, 1), :] = alpha * source[own, pl.ds(0, 1), :]
        ends[pl.ds(plan.blocks + block, 1), :] = heads[block]
    spread(send, [pack([[dot(rests, rests)], [dot(heads, wholes)]])])


def last_kernel(plan, recv, speeds, final, ends, star, pressure, steps):
    current, curve = totals(recv, 0, 2)
    steps[...] = current / curve
    alpha = steps[pl.ds(0, 1), :]
    for block in range(plan.blocks):
        pressure[block] = (
            ends[pl.ds(block, 1), :] + alpha * ends[pl.ds(plan.blocks + block, 1), :]
        )
    for axis in range(3):
        alpha = final[pl.ds(axis, 1), :]
        for block in range(plan.blocks):
            at = axis * plan.blocks + block
            star[at] = (
                speeds[pl.ds(at, 1), :] + alpha * speeds[pl.ds(3 * plan.blocks + at, 1), :]
            )


def call(plan, kernel, operands, outs, scratch=(), space=pltpu.VMEM):
    typed = lambda shape: (shape, jnp.float32) if isinstance(shape[0], int) else shape
    held = lambda item: pltpu.VMEM(*typed(item)) if isinstance(item, tuple) else item
    return pl.pallas_call(
        functools.partial(kernel, plan),
        out_shape=[jax.ShapeDtypeStruct(*typed(shape)) for shape in outs],
        in_specs=[pl.BlockSpec(memory_space=space) for _ in operands],
        out_specs=[pl.BlockSpec(memory_space=pltpu.VMEM) for _ in outs],
        scratch_shapes=[held(item) for item in scratch],
        compiler_params=pltpu.CompilerParams(vmem_limit_bytes=24 * 1024 * 1024),
        name=kernel.__name__,
    )(*operands)


def local(mesh, offsets, velocity, counts, neighbours):
    blocks = counts.shape[2]
    width = offsets.shape[-1]
    plan = Plan(mesh, blocks, width)
    lined = lambda field: field.transpose(0, 1, 3, 2, 4).reshape(3 * blocks, 1, width)
    slot = lambda rows: (plan.devices, rows, 1, width)
    ring = (plan.ring, 8, width)
    tile = (8, width)
    rows = (blocks, 8, width)
    packed = ((32, plan.ring * width), jnp.bfloat16)
    packed_low = ((16, plan.ring * width), jnp.bfloat16)
    (send,) = call(
        plan, pack_kernel,
        [
            pltpu.with_memory_space_constraint(field, pltpu.HBM)
            for field in (counts.reshape(1, blocks), lined(offsets), lined(velocity))
        ],
        [(plan.count[0] * plan.count[1], 6 * blocks, 1, width)],
        [
            pltpu.SMEM((1, blocks), jnp.int32), (3 * blocks, 1, width), (3 * blocks, 1, width),
            pltpu.SemaphoreType.DMA((3,)),
        ],
        pltpu.HBM,
    )
    level, *others = exchange_layers(plan, send)
    flipped = ((plan.ring * width, 48), jnp.bfloat16)
    tiles, where, right, centres, partial = call(
        plan, inner_kernel, [level],
        [
            ((inner_base(plan, blocks), 2 * width), jnp.bfloat16), ring, ring,
            ((blocks, 48, width), jnp.bfloat16), rows,
        ],
        [ring, flipped, ring, packed],
    )
    send, outer, where, right, state = call(
        plan, edge_kernel, [*others, where, right, centres, partial],
        [
            slot(3 * blocks + 1), ((plan.rims * 9 * width, 2 * width), jnp.bfloat16),
            ring, ring, (4 * blocks, width),
        ],
        [ring, flipped, ring, packed, rows],
    )
    recv = exchange(send)
    send, residual, direction, scalars = call(
        plan, second_kernel, [recv, tiles, outer, right, state],
        [slot(3 * blocks + 1), ring, ring, (blocks + 1, 8, width)],
        [ring, packed_low, rows],
    )
    recv = exchange(send)
    send, speeds = call(
        plan, third_kernel, [recv, tiles, outer, where, right, residual, direction, state, scalars],
        [slot(4 * blocks + 1), (6 * blocks, width)],
        [ring, rows, ring, tile, packed, rows],
    )
    recv = exchange(send)
    send, source, final = call(
        plan, fourth_kernel, [recv, tiles, outer, state],
        [slot(blocks + 1), ring, tile],
        [ring, packed_low, rows],
    )
    recv = exchange(send)
    send, ends = call(
        plan, fifth_kernel, [recv, tiles, outer, source, state],
        [slot(1), (2 * blocks, width)],
        [ring, ring, tile, packed_low, rows],
    )
    recv = exchange(send)
    star, pressure = call(
        plan, last_kernel, [recv, speeds, final, ends],
        [(3 * blocks, 1, width), (blocks, 1, width)], [tile],
    )
    star = star.reshape(3, 1, blocks, 1, width).transpose(0, 1, 3, 2, 4)
    pressure = pressure.reshape(1, blocks, 1, width).transpose(0, 2, 1, 3)
    return star, pressure


def solution(mesh):
    in_specs = (
        P(None, "gx", "gy", "gz", None),
        P(None, "gx", "gy", "gz", None),
        P("gx", "gy", "gz"),
        P("gx", "gy", "gz", None),
    )
    out_specs = (P(None, "gx", "gy", "gz", None), P("gx", "gy", "gz", None))
    return jax.shard_map(
        functools.partial(local, mesh),
        mesh=mesh, in_specs=in_specs, out_specs=out_specs, check_vma=False,
    )
```

```python
import functools

import jax
import jax.numpy as jnp
from jax import lax
from jax.experimental import pallas as pl
from jax.experimental.pallas import tpu as pltpu
from jax.sharding import PartitionSpec as P

VISCOUS = 4.0
STIFFNESS = 0.25
GRAVITY_STEP = 0.5
AXES = ("gx", "gy", "gz")
FAR = 1.0e3
LANES = 128


def exchange(send):
    return lax.all_to_all(send, AXES, 0, 0, tiled=True)


def exchange_layers(plan, send):
    level = lax.all_to_all(send, AXES[:2], 0, 0, tiled=True)
    deep = plan.count[2]
    if deep == 2:
        return [level, lax.ppermute(level, AXES[2], [(0, 1), (1, 0)])]
    forward = [(i, i + 1) for i in range(deep - 1)]
    backward = [(target, source) for source, target in forward]
    return [level] + [lax.ppermute(level, AXES[2], pairs) for pairs in (forward, backward)]


class Plan:
    def __init__(self, mesh, blocks, width):
        self.count = [mesh.shape[axis] for axis in AXES]
        self.devices = self.count[0] * self.count[1] * self.count[2]
        self.blocks = blocks
        self.width = width
        self.rims = 1 if self.count[2] == 2 else 2
        self.deep = blocks + self.rims
        self.ring = 9 * self.deep
        self.cube = (2.0 / width) ** (1.0 / 3.0)
        self.unit = self.cube ** 0.5

    def own(self, block):
        return 4 * self.deep + block


def rims_of(plan):
    last = plan.blocks - 1
    if plan.rims == 2:
        return [(-1, 0, last, -1), (1, last, 0, plan.blocks)]
    above = lax.axis_index(AXES[2]) == 0
    choose = lambda yes, no: jnp.where(above, jnp.int32(yes), jnp.int32(no))
    return [(choose(1, -1), choose(last, 0), choose(0, last), choose(plan.blocks, -1))]


def slots(plan, rims, axes=3):
    place = [lax.axis_index(axis) for axis in AXES]
    found = []
    for column in range(9):
        beside = []
        for step in [0] + [rim[0] for rim in rims]:
            at = [place[0] + column // 3 - 1, place[1] + column % 3 - 1, place[2] + step]
            present = None
            slot = 0
            for axis, (value, count) in enumerate(zip(at, plan.count)):
                inside = jnp.logical_and(value >= 0, value < count)
                present = inside if present is None else jnp.logical_and(present, inside)
                if axis < axes:
                    slot = slot * count + jnp.clip(value, 0, count - 1)
            beside.append((slot, present))
        found.append(beside)
    return found


def take(recv, slot, row):
    if recv.shape[2] == 1:
        return recv[slot, row]
    return recv[slot, row // 2, pl.ds(row % 2, 1), :]


def gather_ring(plan, rims, found, layers, fields, store, levels=None):
    for column in range(9):
        for level in levels or range(plan.deep):
            layer, block, depth = 0, level, level
            if level >= plan.blocks:
                layer = level - plan.blocks + 1
                block, depth = rims[layer - 1][2:]
            slot, present = found[column][layer]
            got = layers[layer]
            rows = [take(got, slot, field * plan.blocks + block) for field in range(fields)]
            store(column * plan.deep + level, column, depth, rows, present)


def ring_into(plan, rims, recv, fields, ref):
    def store(at, column, depth, rows, present):
        for field, row in enumerate(rows):
            ref[at, pl.ds(field, 1), :] = row

    gather_ring(plan, rims, slots(plan, rims), [recv] * (1 + plan.rims), fields, store)


def lane_ids(sublanes=1):
    return lax.broadcasted_iota(jnp.int32, (sublanes, LANES), 1)


def sublane_ids():
    return lax.broadcasted_iota(jnp.int32, (8, LANES), 0)


def totals(recv, row, number):
    summed = jnp.broadcast_to(jnp.sum(take(recv, slice(None), row), axis=0), (8, LANES))
    place = lane_ids(8) - sublane_ids()
    return [
        jnp.broadcast_to(
            jnp.sum(jnp.where(place == 8 * m, summed, 0.0), axis=1, keepdims=True), (8, LANES)
        )
        for m in range(number)
    ]


def pack(groups):
    lane = lane_ids()
    row = jnp.zeros((1, LANES), jnp.float32)
    for m, group in enumerate(groups):
        for c, partial in enumerate(group):
            row = jnp.where(lane == 8 * m + c, jnp.sum(partial, axis=1, keepdims=True), row)
    return row


def dot(first, second):
    total = first[0] * second[0]
    for a, b in zip(first[1:], second[1:]):
        total = total + a * b
    return total


def spread(send, rows):
    size = send.shape[2]
    rows = [jnp.concatenate(rows[r : r + size], axis=0) for r in range(0, len(rows), size)]

    def body(slot, carry):
        for r, row in enumerate(rows):
            send[slot, r] = row
        return carry

    lax.fori_loop(0, send.shape[0], body, 0, unroll=4)


def coarse(value):
    return value.astype(jnp.bfloat16).astype(jnp.float32)


def split(value):
    first = coarse(value)
    rest = value - first
    second = coarse(rest)
    return first, second, rest - second


def stack_full(value):
    first, second, third = split(value)
    return jnp.concatenate([first, second, third, jnp.zeros_like(third)], axis=0)


def fold_full(total):
    both = total[:, :LANES] + total[:, LANES:]
    return both[0:8] + both[8:16] + both[16:24]


def stack_three(value):
    first, second, third = split(value)
    joined = jnp.where(sublane_ids() < 3, first, pltpu.roll(second, 3, 0))
    return jnp.concatenate([joined, third], axis=0)


def fold_three(total):
    both = total[:, :LANES] + total[:, LANES:]
    return both[0:8] + pltpu.roll(both[0:8], 5, 0) + both[8:16]


def stack_one(value):
    first, second, third = split(value)
    sub = sublane_ids()
    joined = jnp.where(sub == 0, first, jnp.where(sub == 1, second, third))
    return jnp.concatenate([jnp.where(sub < 3, joined, 0.0), jnp.zeros_like(third)], axis=0)


def fold_one(total):
    both = total[0:8, :LANES] + total[0:8, LANES:]
    return jnp.broadcast_to(jnp.sum(both, axis=0, keepdims=True), (8, LANES))


FULL = (stack_full, fold_full)
THREE = (stack_three, fold_three)
ONE = (stack_one, fold_one)


def split_ring(plan, ring, packed, form, levels=None):
    for column in range(9):
        for level in levels or range(plan.deep):
            at = column * plan.deep + level
            packed[:, pl.ds(at * LANES, LANES)] = form[0](ring[at]).astype(jnp.bfloat16)


def inner_span(plan, block):
    low = max(block - 1, 0)
    return low, min(block + 2, plan.blocks) - low


def inner_base(plan, block):
    return 9 * sum(inner_span(plan, before)[1] for before in range(block)) * plan.width


def groups_of(number):
    size = 3 if number % 2 == 0 else 4 if number == 1 else 2
    return [range(c, min(c + size, 9)) for c in range(0, 9, size)]


def tile_sum(plan, tiles, base, packed, level, number, columns):
    span = number * plan.width
    ahead = [packed[:, pl.ds((c * plan.deep + level) * LANES, span)] for c in columns]
    return jnp.dot(
        jnp.concatenate(ahead, axis=1) if len(ahead) > 1 else ahead[0],
        tiles[pl.ds(base + columns[0] * span, len(ahead) * span), :],
        preferred_element_type=jnp.float32,
    )


def apply_tiles(plan, rims, tiles, outer, ring, packed, rows, form):
    split_ring(plan, ring, packed, form)
    for block in range(plan.blocks):
        low, number = inner_span(plan, block)
        base = inner_base(plan, block)
        total = None
        for columns in groups_of(number):
            part = tile_sum(plan, tiles, base, packed, low, number, columns)
            total = part if total is None else total + part
        rows[block] = form[1](total)
    add_rims(plan, rims, outer, packed, rows, form, lambda e, columns: None)


def add_rims(plan, rims, outer, packed, rows, form, before):
    for e, rim in enumerate(rims):
        total = None
        for columns in groups_of(1):
            before(e, columns)
            base = e * 9 * plan.width
            part = tile_sum(plan, outer, base, packed, plan.blocks + e, 1, columns)
            total = part if total is None else total + part
        rows[rim[1]] = rows[rim[1]] + form[1](total)


def pack_kernel(plan, counts_in, offsets_in, velocity_in, send, counts, offsets, velocity, sems):
    pairs = [(counts_in, counts), (offsets_in, offsets), (velocity_in, velocity)]
    copies = [pltpu.make_async_copy(a, b, sems.at[i]) for i, (a, b) in enumerate(pairs)]
    for copy in copies:
        copy.start()
    for copy in copies:
        copy.wait()
    lane = lane_ids()
    rows = []
    for axis in range(3):
        for block in range(plan.blocks):
            valid = lane < counts[0, block]
            row = offsets[axis * plan.blocks + block]
            rows.append(jnp.where(valid, row, FAR) if axis == 0 else row)
    for axis in range(3):
        for block in range(plan.blocks):
            valid = lane < counts[0, block]
            row = velocity[axis * plan.blocks + block]
            if axis == 0:
                row = row + GRAVITY_STEP
            rows.append(jnp.where(valid, row, 0.0))
    spread(send, rows)


def place_ring(plan, rims, layers, levels, mixed):
    blank = jnp.where(sublane_ids() == 3, 1.0, 0.0)

    def store(at, column, depth, got, present):
        shift = (column // 3 - 1, column % 3 - 1, depth - (plan.blocks - 1) // 2)
        spots = [
            plan.unit * (got[axis] + jnp.asarray(shift[axis], jnp.float32)) for axis in range(3)
        ]
        spots[0] = jnp.where(present, spots[0], FAR)
        mixed[at] = blank
        for axis in range(3):
            mixed[at, pl.ds(axis, 1), :] = jnp.where(present, got[3 + axis], 0.0)
            mixed[at, pl.ds(4 + axis, 1), :] = spots[axis]

    gather_ring(plan, rims, slots(plan, rims, 2), layers, 6, store, levels)


def spot_of(tile):
    return pltpu.roll(tile, 4, 0)


def point_of(tile):
    sub = sublane_ids()
    spot = jnp.where(sub < 3, spot_of(tile), 0.0)
    square = jnp.sum(spot * spot, axis=0, keepdims=True)
    return jnp.where(sub == 3, square, jnp.where(sub == 4, 1.0, spot))


def flip_points(plan, levels, mixed, flipped):
    for column in range(9):
        for level in levels:
            at = column * plan.deep + level
            first, second, third = split(point_of(mixed[at]))
            stacked = jnp.concatenate([first, second, third, first, second, first], axis=0)
            flipped[pl.ds(at * plan.width, plan.width), :] = jnp.transpose(stacked).astype(jnp.bfloat16)


def weigh(plan, flipped, centre, level, number, columns, tiles, base):
    for column in columns:
        span = number * plan.width
        rest = jnp.dot(
            flipped[pl.ds((column * plan.deep + level) * plan.width, span), :],
            centre, preferred_element_type=jnp.float32,
        )
        bump = jnp.maximum(rest, 0.0)
        weight = bump * bump * bump
        high = weight.astype(jnp.bfloat16)
        spot = pl.ds(base + column * span, span)
        tiles[spot, pl.ds(0, LANES)] = high
        tiles[spot, pl.ds(LANES, LANES)] = (weight - high.astype(jnp.float32)).astype(jnp.bfloat16)


def inner_kernel(plan, recv, tiles, mixed, centres, partial, flipped, packed):
    levels = range(plan.blocks)
    place_ring(plan, rims_of(plan), [recv], levels, mixed)
    flip_points(plan, levels, mixed, flipped)
    split_ring(plan, mixed, packed, FULL, levels)
    sub = sublane_ids()
    for block in range(plan.blocks):
        own = point_of(mixed[plan.own(block)])
        own = jnp.where(jnp.logical_and(sub == 0, own > 0.25 * FAR), -FAR, own)
        square = jnp.broadcast_to(own[3:4], (8, LANES))
        own = jnp.where(sub < 3, 2.0 * own, 0.0)
        own = jnp.where(sub == 3, -1.0, own)
        own = jnp.where(sub == 4, plan.cube - square, own)
        first, second, third = split(own)
        stacked = jnp.concatenate([first, first, first, second, second, third], axis=0)
        centre = stacked.astype(jnp.bfloat16)
        centres[block] = centre
        low, number = inner_span(plan, block)
        base = inner_base(plan, block)
        total = None
        for columns in groups_of(number):
            weigh(plan, flipped, centre, low, number, columns, tiles, base)
            part = tile_sum(plan, tiles, base, packed, low, number, columns)
            total = part if total is None else total + part
        partial[block] = fold_full(total)


def edge_kernel(plan, *refs):
    others = refs[:-10]
    near, centres, partial, send, outer, mixed, state, flipped, packed, rows = refs[-10:]
    rims = rims_of(plan)
    levels = range(plan.blocks, plan.deep)
    place_ring(plan, rims, [None, *others], levels, mixed)
    for column in range(9):
        for level in range(plan.blocks):
            at = column * plan.deep + level
            mixed[at] = near[at]
    flip_points(plan, levels, mixed, flipped)
    split_ring(plan, mixed, packed, FULL, levels)
    for block in range(plan.blocks):
        rows[block] = partial[block]

    def before(e, columns):
        centre = centres[rims[e][1]]
        weigh(plan, flipped, centre, plan.blocks + e, 1, columns, outer, e * 9 * plan.width)

    add_rims(plan, rims, outer, packed, rows, FULL, before)
    image = [[None] * plan.blocks for _ in range(3)]
    whole = [[None] * plan.blocks for _ in range(3)]
    start = [[None] * plan.blocks for _ in range(3)]
    for block in range(plan.blocks):
        own = plan.own(block)
        reach = rows[block, pl.ds(3, 1), :]
        state[pl.ds(block, 1), :] = reach
        for axis in range(3):
            field = mixed[own, pl.ds(axis, 1), :]
            start[axis][block] = field
            image[axis][block] = reach * field - rows[block, pl.ds(axis, 1), :]
            whole[axis][block] = field + VISCOUS * image[axis][block]
            spot = mixed[own, pl.ds(4 + axis, 1), :]
            state[pl.ds((1 + axis) * plan.blocks + block, 1), :] = (
                reach * spot - rows[block, pl.ds(4 + axis, 1), :]
            )
    groups = [
        [dot(start[axis], start[axis]) for axis in range(3)],
        [dot(start[axis], whole[axis]) for axis in range(3)],
        [dot(whole[axis], whole[axis]) for axis in range(3)],
    ]
    spread(send, sum(image, []) + [pack(groups)])


def second_kernel(plan, recv, tiles, outer, mixed, state, send, residual, direction, scalars, image, packed, rows):
    rims = rims_of(plan)
    ring_into(plan, rims, recv, 3, image)
    current, curve, square = totals(recv, 3 * plan.blocks, 3)
    alpha = current / curve
    following = jnp.maximum(alpha * alpha * square - current, 0.0)
    beta = following / current
    for at in range(plan.ring):
        field = mixed[at]
        left = field - alpha * (field + VISCOUS * image[at])
        residual[at] = left
        direction[at] = left + beta * field
    scalars[plan.blocks] = alpha
    for block in range(plan.blocks):
        scalars[block] = image[plan.own(block)]
    apply_tiles(plan, rims, tiles, outer, direction, packed, rows, THREE)
    out = []
    groups = [[], [], [], []]
    for axis in range(3):
        left, ahead, shot, whole = [], [], [], []
        for block in range(plan.blocks):
            own = plan.own(block)
            left.append(residual[own, pl.ds(axis, 1), :])
            ahead.append(direction[own, pl.ds(axis, 1), :])
            shot.append(state[pl.ds(block, 1), :] * ahead[block] - rows[block, pl.ds(axis, 1), :])
            whole.append(ahead[block] + VISCOUS * shot[block])
        out.extend(shot)
        groups[0].append(dot(left, left))
        groups[1].append(dot(ahead, whole))
        groups[2].append(dot(left, whole))
        groups[3].append(dot(whole, whole))
    spread(send, out + [pack(groups)])


def third_kernel(
    plan, recv, tiles, outer, mixed, residual, direction, state, scalars,
    send, ends, image, sofar, ahead, steps, packed, rows,
):
    rims = rims_of(plan)
    ring_into(plan, rims, recv, 3, image)
    current, curve, cross, square = totals(recv, 3 * plan.blocks, 4)
    alpha = current / curve
    following = jnp.maximum(current - 2.0 * alpha * cross + alpha * alpha * square, 0.0)
    beta = following / current
    first = scalars[plan.blocks]
    steps[...] = alpha
    sub = sublane_ids()
    for block in range(plan.blocks):
        own = plan.own(block)
        rows[block] = first * scalars[block] + alpha * image[own]
    latest = [
        [rows[block, pl.ds(axis, 1), :] for axis in range(3)] for block in range(plan.blocks)
    ]
    for at in range(plan.ring):
        field = direction[at]
        rest = residual[at] - alpha * (field + VISCOUS * image[at])
        fresh = rest + beta * field
        spot = spot_of(mixed[at])
        made = first * mixed[at] + alpha * field
        moved = made * spot
        moved = pltpu.roll(moved, 6, 0) + pltpu.roll(moved, 5, 0) + pltpu.roll(moved, 4, 0)
        joined = jnp.where(sub < 3, fresh, pltpu.roll(fresh * spot, 3, 0))
        ahead[at] = jnp.where(sub < 6, joined, moved)
        if at - plan.own(0) in range(plan.blocks):
            image[at] = rest
            sofar[at - plan.own(0)] = made
    apply_tiles(plan, rims, tiles, outer, ahead, packed, rows, FULL)
    scale = 1.0 / plan.unit
    base = []
    each = [[None] * plan.blocks for _ in range(3)]
    rests = [[None] * plan.blocks for _ in range(3)]
    heads = [[None] * plan.blocks for _ in range(3)]
    wholes = [[None] * plan.blocks for _ in range(3)]
    for block in range(plan.blocks):
        reach = state[pl.ds(block, 1), :]
        own = plan.own(block)
        total = rows[block, pl.ds(6, 1), :] - reach * ahead[own, pl.ds(6, 1), :]
        for axis in range(3):
            head = ahead[own, pl.ds(axis, 1), :]
            spot = mixed[own, pl.ds(4 + axis, 1), :]
            lean = state[pl.ds((1 + axis) * plan.blocks + block, 1), :]
            shot = reach * head - rows[block, pl.ds(axis, 1), :]
            twice = reach * ahead[own, pl.ds(3 + axis, 1), :] - rows[block, pl.ds(3 + axis, 1), :]
            each[axis][block] = scale * (spot * shot + head * lean - twice)
            made = sofar[block, pl.ds(axis, 1), :]
            total = total + spot * latest[block][axis] + made * lean
            rests[axis][block] = image[own, pl.ds(axis, 1), :]
            heads[axis][block] = head
            wholes[axis][block] = head + VISCOUS * shot
            ends[pl.ds(axis * plan.blocks + block, 1), :] = made
            ends[pl.ds((3 + axis) * plan.blocks + block, 1), :] = head
        base.append(scale * total)
    groups = [
        [dot(rests[axis], rests[axis]) for axis in range(3)],
        [dot(heads[axis], wholes[axis]) for axis in range(3)],
    ]
    spread(send, base + sum(each, []) + [pack(groups)])


def fourth_kernel(plan, recv, tiles, outer, state, send, source, steps, parts, packed, rows):
    rims = rims_of(plan)
    ring_into(plan, rims, recv, 4, parts)
    current, curve = totals(recv, 4 * plan.blocks, 2)
    sub = sublane_ids()
    steps[...] = current / curve
    factor = jnp.where(sub == 0, 1.0, pltpu.roll(steps[...], 1, 0))
    for at in range(plan.ring):
        gathered = jnp.where(sub < 4, parts[at] * factor, 0.0)
        source[at] = jnp.broadcast_to(-jnp.sum(gathered, axis=0, keepdims=True), (8, LANES))
    apply_tiles(plan, rims, tiles, outer, source, packed, rows, ONE)
    field, shot, whole = [], [], []
    for block in range(plan.blocks):
        field.append(source[plan.own(block), pl.ds(0, 1), :])
        shot.append(state[pl.ds(block, 1), :] * field[block] - rows[block, pl.ds(0, 1), :])
        whole.append(STIFFNESS * field[block] + shot[block])
    groups = [[dot(field, field)], [dot(field, whole)], [dot(whole, whole)]]
    spread(send, shot + [pack(groups)])


def fifth_kernel(plan, recv, tiles, outer, source, state, send, ends, image, ahead, steps, packed, rows):
    rims = rims_of(plan)
    ring_into(plan, rims, recv, 1, image)
    current, curve, square = totals(recv, plan.blocks, 3)
    steps[...] = current / curve
    alpha = steps[pl.ds(0, 1), :]
    steps[...] = jnp.maximum(alpha * alpha * square - current, 0.0) / current
    beta = steps[pl.ds(0, 1), :]
    for at in range(plan.ring):
        field = source[at]
        left = field - alpha * (STIFFNESS * field + image[at, pl.ds(0, 1), :])
        image[at] = left
        ahead[at] = left + beta * field
    apply_tiles(plan, rims, tiles, outer, ahead, packed, rows, ONE)
    rests, heads, wholes = [], [], []
    for block in range(plan.blocks):
        own = plan.own(block)
        rests.append(image[own, pl.ds(0, 1), :])
        heads.append(ahead[own, pl.ds(0, 1), :])
        shot = state[pl.ds(block, 1), :] * heads[block] - rows[block, pl.ds(0, 1), :]
        wholes.append(STIFFNESS * heads[block] + shot)
        ends[pl.ds(block, 1), :] = alpha * source[own, pl.ds(0, 1), :]
        ends[pl.ds(plan.blocks + block, 1), :] = heads[block]
    spread(send, [pack([[dot(rests, rests)], [dot(heads, wholes)]])])


def last_kernel(plan, recv, speeds, final, ends, star, pressure, steps):
    current, curve = totals(recv, 0, 2)
    steps[...] = current / curve
    alpha = steps[pl.ds(0, 1), :]
    for block in range(plan.blocks):
        pressure[block] = (
            ends[pl.ds(block, 1), :] + alpha * ends[pl.ds(plan.blocks + block, 1), :]
        )
    for axis in range(3):
        alpha = final[pl.ds(axis, 1), :]
        for block in range(plan.blocks):
            at = axis * plan.blocks + block
            star[at] = (
                speeds[pl.ds(at, 1), :] + alpha * speeds[pl.ds(3 * plan.blocks + at, 1), :]
            )


def call(plan, kernel, operands, outs, scratch=(), space=pltpu.VMEM):
    typed = lambda shape: (shape, jnp.float32) if isinstance(shape[0], int) else shape
    held = lambda item: pltpu.VMEM(*typed(item)) if isinstance(item, tuple) else item
    return pl.pallas_call(
        functools.partial(kernel, plan),
        out_shape=[jax.ShapeDtypeStruct(*typed(shape)) for shape in outs],
        in_specs=[pl.BlockSpec(memory_space=space) for _ in operands],
        out_specs=[pl.BlockSpec(memory_space=pltpu.VMEM) for _ in outs],
        scratch_shapes=[held(item) for item in scratch],
        compiler_params=pltpu.CompilerParams(vmem_limit_bytes=24 * 1024 * 1024),
        name=kernel.__name__,
    )(*operands)


def local(mesh, offsets, velocity, counts, neighbours):
    blocks = counts.shape[2]
    width = offsets.shape[-1]
    plan = Plan(mesh, blocks, width)
    lined = lambda field: field.transpose(0, 1, 3, 2, 4).reshape(3 * blocks, 1, width)
    paired = lambda rows: (rows // 2, 2, width) if rows % 2 == 0 else (rows, 1, width)
    slot = lambda rows: (plan.devices, *paired(rows))
    ring = (plan.ring, 8, width)
    tile = (8, width)
    rows = (blocks, 8, width)
    packed = ((32, plan.ring * width), jnp.bfloat16)
    packed_low = ((16, plan.ring * width), jnp.bfloat16)
    (send,) = call(
        plan, pack_kernel,
        [
            pltpu.with_memory_space_constraint(field, pltpu.HBM)
            for field in (counts.reshape(1, blocks), lined(offsets), lined(velocity))
        ],
        [(plan.count[0] * plan.count[1], *paired(6 * blocks))],
        [
            pltpu.SMEM((1, blocks), jnp.int32), (3 * blocks, 1, width), (3 * blocks, 1, width),
            pltpu.SemaphoreType.DMA((3,)),
        ],
        pltpu.HBM,
    )
    level, *others = exchange_layers(plan, send)
    flipped = ((plan.ring * width, 48), jnp.bfloat16)
    tiles, mixed, centres, partial = call(
        plan, inner_kernel, [level],
        [
            ((inner_base(plan, blocks), 2 * width), jnp.bfloat16), ring,
            ((blocks, 48, width), jnp.bfloat16), rows,
        ],
        [flipped, packed],
    )
    send, outer, mixed, state = call(
        plan, edge_kernel, [*others, mixed, centres, partial],
        [
            slot(3 * blocks + 1), ((plan.rims * 9 * width, 2 * width), jnp.bfloat16),
            ring, (4 * blocks, width),
        ],
        [flipped, packed, rows],
    )
    recv = exchange(send)
    send, residual, direction, scalars = call(
        plan, second_kernel, [recv, tiles, outer, mixed, state],
        [slot(3 * blocks + 1), ring, ring, (blocks + 1, 8, width)],
        [ring, packed_low, rows],
    )
    recv = exchange(send)
    send, speeds = call(
        plan, third_kernel, [recv, tiles, outer, mixed, residual, direction, state, scalars],
        [slot(4 * blocks + 1), (6 * blocks, width)],
        [ring, rows, ring, tile, packed, rows],
    )
    recv = exchange(send)
    send, source, final = call(
        plan, fourth_kernel, [recv, tiles, outer, state],
        [slot(blocks + 1), ring, tile],
        [ring, packed_low, rows],
    )
    recv = exchange(send)
    send, ends = call(
        plan, fifth_kernel, [recv, tiles, outer, source, state],
        [slot(1), (2 * blocks, width)],
        [ring, ring, tile, packed_low, rows],
    )
    recv = exchange(send)
    star, pressure = call(
        plan, last_kernel, [recv, speeds, final, ends],
        [(3 * blocks, 1, width), (blocks, 1, width)], [tile],
    )
    star = star.reshape(3, 1, blocks, 1, width).transpose(0, 1, 3, 2, 4)
    pressure = pressure.reshape(1, blocks, 1, width).transpose(0, 2, 1, 3)
    return star, pressure


def solution(mesh):
    in_specs = (
        P(None, "gx", "gy", "gz", None),
        P(None, "gx", "gy", "gz", None),
        P("gx", "gy", "gz"),
        P("gx", "gy", "gz", None),
    )
    out_specs = (P(None, "gx", "gy", "gz", None), P("gx", "gy", "gz", None))
    return jax.shard_map(
        functools.partial(local, mesh),
        mesh=mesh, in_specs=in_specs, out_specs=out_specs, check_vma=False,
    )
```

```python
import functools

import jax
import jax.numpy as jnp
from jax import lax
from jax.experimental import pallas as pl
from jax.experimental.pallas import tpu as pltpu
from jax.sharding import PartitionSpec as P

VISCOUS = 4.0
STIFFNESS = 0.25
GRAVITY_STEP = 0.5
AXES = ("gx", "gy", "gz")
FAR = 1.0e3
LANES = 128


def exchange(send):
    return lax.all_to_all(send, AXES, 0, 0, tiled=True)


def exchange_layers(plan, send):
    level = lax.all_to_all(send, AXES[:2], 0, 0, tiled=True)
    deep = plan.count[2]
    if deep == 2:
        return [level, lax.ppermute(level, AXES[2], [(0, 1), (1, 0)])]
    forward = [(i, i + 1) for i in range(deep - 1)]
    backward = [(target, source) for source, target in forward]
    return [level] + [lax.ppermute(level, AXES[2], pairs) for pairs in (forward, backward)]


class Plan:
    def __init__(self, mesh, blocks, width):
        self.count = [mesh.shape[axis] for axis in AXES]
        self.devices = self.count[0] * self.count[1] * self.count[2]
        self.blocks = blocks
        self.width = width
        self.rims = 1 if self.count[2] == 2 else 2
        self.deep = blocks + self.rims
        self.ring = 9 * self.deep
        self.cube = (2.0 / width) ** (1.0 / 3.0)
        self.unit = self.cube ** 0.5

    def own(self, block):
        return 4 * self.deep + block


def rims_of(plan):
    last = plan.blocks - 1
    if plan.rims == 2:
        return [(-1, 0, last, -1), (1, last, 0, plan.blocks)]
    above = lax.axis_index(AXES[2]) == 0
    choose = lambda yes, no: jnp.where(above, jnp.int32(yes), jnp.int32(no))
    return [(choose(1, -1), choose(last, 0), choose(0, last), choose(plan.blocks, -1))]


def slots(plan, rims, axes=3):
    place = [lax.axis_index(axis) for axis in AXES]
    found = []
    for column in range(9):
        beside = []
        for step in [0] + [rim[0] for rim in rims]:
            at = [place[0] + column // 3 - 1, place[1] + column % 3 - 1, place[2] + step]
            present = None
            slot = 0
            for axis, (value, count) in enumerate(zip(at, plan.count)):
                inside = jnp.logical_and(value >= 0, value < count)
                present = inside if present is None else jnp.logical_and(present, inside)
                if axis < axes:
                    slot = slot * count + jnp.clip(value, 0, count - 1)
            beside.append((slot, present))
        found.append(beside)
    return found


def take(recv, slot, row):
    if recv.shape[2] == 1:
        return recv[slot, row]
    return recv[slot, row // 2, pl.ds(row % 2, 1), :]


def gather_ring(plan, rims, found, layers, fields, store, levels=None):
    for column in range(9):
        for level in levels or range(plan.deep):
            layer, block, depth = 0, level, level
            if level >= plan.blocks:
                layer = level - plan.blocks + 1
                block, depth = rims[layer - 1][2:]
            slot, present = found[column][layer]
            got = layers[layer]
            rows = [take(got, slot, field * plan.blocks + block) for field in range(fields)]
            store(column * plan.deep + level, column, depth, rows, present)


def ring_into(plan, rims, recv, fields, ref):
    def store(at, column, depth, rows, present):
        for field, row in enumerate(rows):
            ref[at, pl.ds(field, 1), :] = row

    gather_ring(plan, rims, slots(plan, rims), [recv] * (1 + plan.rims), fields, store)


def lane_ids(sublanes=1):
    return lax.broadcasted_iota(jnp.int32, (sublanes, LANES), 1)


def sublane_ids():
    return lax.broadcasted_iota(jnp.int32, (8, LANES), 0)


def totals(recv, row, number):
    summed = jnp.broadcast_to(jnp.sum(take(recv, slice(None), row), axis=0), (8, LANES))
    place = lane_ids(8) - sublane_ids()
    return [
        jnp.broadcast_to(
            jnp.sum(jnp.where(place == 8 * m, summed, 0.0), axis=1, keepdims=True), (8, LANES)
        )
        for m in range(number)
    ]


def pack(groups):
    lane = lane_ids()
    row = jnp.zeros((1, LANES), jnp.float32)
    for m, group in enumerate(groups):
        for c, partial in enumerate(group):
            row = jnp.where(lane == 8 * m + c, jnp.sum(partial, axis=1, keepdims=True), row)
    return row


def dot(first, second):
    total = first[0] * second[0]
    for a, b in zip(first[1:], second[1:]):
        total = total + a * b
    return total


def spread(send, rows):
    size = send.shape[2]
    rows = [jnp.concatenate(rows[r : r + size], axis=0) for r in range(0, len(rows), size)]

    def body(slot, carry):
        for r, row in enumerate(rows):
            send[slot, r] = row
        return carry

    lax.fori_loop(0, send.shape[0], body, 0, unroll=4)


def coarse(value):
    return value.astype(jnp.bfloat16).astype(jnp.float32)


def split(value):
    first = coarse(value)
    rest = value - first
    second = coarse(rest)
    return first, second, rest - second


def stack_full(value):
    first, second, third = split(value)
    return jnp.concatenate([first, second, third, jnp.zeros_like(third)], axis=0)


def fold_full(total):
    both = total[:, :LANES] + total[:, LANES:]
    return both[0:8] + both[8:16] + both[16:24]


def stack_three(value):
    first, second, third = split(value)
    joined = jnp.where(sublane_ids() < 3, first, pltpu.roll(second, 3, 0))
    return jnp.concatenate([joined, third], axis=0)


def fold_three(total):
    both = total[:, :LANES] + total[:, LANES:]
    return both[0:8] + pltpu.roll(both[0:8], 5, 0) + both[8:16]


def stack_one(value):
    first, second, third = split(value)
    sub = sublane_ids()
    joined = jnp.where(sub == 0, first, jnp.where(sub == 1, second, third))
    return jnp.concatenate([jnp.where(sub < 3, joined, 0.0), jnp.zeros_like(third)], axis=0)


def fold_one(total):
    both = total[0:8, :LANES] + total[0:8, LANES:]
    return jnp.broadcast_to(jnp.sum(both, axis=0, keepdims=True), (8, LANES))


FULL = (stack_full, fold_full)
THREE = (stack_three, fold_three)
ONE = (stack_one, fold_one)


def split_ring(plan, ring, packed, form, levels=None):
    for column in range(9):
        for level in levels or range(plan.deep):
            at = column * plan.deep + level
            packed[:, pl.ds(at * LANES, LANES)] = form[0](ring[at]).astype(jnp.bfloat16)


def inner_span(plan, block):
    low = max(block - 1, 0)
    return low, min(block + 2, plan.blocks) - low


def inner_base(plan, block):
    return 9 * sum(inner_span(plan, before)[1] for before in range(block)) * plan.width


def groups_of(number):
    size = 3 if number % 2 == 0 else 9 if number == 1 else 2
    return [range(c, min(c + size, 9)) for c in range(0, 9, size)]


def tile_sum(plan, tiles, base, packed, level, number, columns):
    span = number * plan.width
    ahead = [packed[:, pl.ds((c * plan.deep + level) * LANES, span)] for c in columns]
    return jnp.dot(
        jnp.concatenate(ahead, axis=1) if len(ahead) > 1 else ahead[0],
        tiles[pl.ds(base + columns[0] * span, len(ahead) * span), :],
        preferred_element_type=jnp.float32,
    )


def apply_tiles(plan, rims, tiles, outer, ring, packed, rows, form):
    split_ring(plan, ring, packed, form)
    for block in range(plan.blocks):
        low, number = inner_span(plan, block)
        base = inner_base(plan, block)
        total = None
        for columns in groups_of(number):
            part = tile_sum(plan, tiles, base, packed, low, number, columns)
            total = part if total is None else total + part
        rows[block] = form[1](total)
    add_rims(plan, rims, outer, packed, rows, form, lambda e, columns: None)


def add_rims(plan, rims, outer, packed, rows, form, before):
    for e, rim in enumerate(rims):
        total = None
        for columns in groups_of(1):
            before(e, columns)
            base = e * 9 * plan.width
            part = tile_sum(plan, outer, base, packed, plan.blocks + e, 1, columns)
            total = part if total is None else total + part
        rows[rim[1]] = rows[rim[1]] + form[1](total)


def pack_kernel(plan, counts_in, offsets_in, velocity_in, send, counts, offsets, velocity, sems):
    pairs = [(counts_in, counts), (offsets_in, offsets), (velocity_in, velocity)]
    copies = [pltpu.make_async_copy(a, b, sems.at[i]) for i, (a, b) in enumerate(pairs)]
    for copy in copies:
        copy.start()
    for copy in copies:
        copy.wait()
    lane = lane_ids()
    rows = []
    for axis in range(3):
        for block in range(plan.blocks):
            valid = lane < counts[0, block]
            row = offsets[axis * plan.blocks + block]
            rows.append(jnp.where(valid, row, FAR) if axis == 0 else row)
    for axis in range(3):
        for block in range(plan.blocks):
            valid = lane < counts[0, block]
            row = velocity[axis * plan.blocks + block]
            if axis == 0:
                row = row + GRAVITY_STEP
            rows.append(jnp.where(valid, row, 0.0))
    spread(send, rows)


def place_ring(plan, rims, layers, levels, mixed):
    blank = jnp.where(sublane_ids() == 3, 1.0, 0.0)

    def store(at, column, depth, got, present):
        shift = (column // 3 - 1, column % 3 - 1, depth - (plan.blocks - 1) // 2)
        spots = [
            plan.unit * (got[axis] + jnp.asarray(shift[axis], jnp.float32)) for axis in range(3)
        ]
        spots[0] = jnp.where(present, spots[0], FAR)
        mixed[at] = blank
        for axis in range(3):
            mixed[at, pl.ds(axis, 1), :] = jnp.where(present, got[3 + axis], 0.0)
            mixed[at, pl.ds(4 + axis, 1), :] = spots[axis]

    gather_ring(plan, rims, slots(plan, rims, 2), layers, 6, store, levels)


def spot_of(tile):
    return pltpu.roll(tile, 4, 0)


def point_of(tile):
    sub = sublane_ids()
    spot = jnp.where(sub < 3, spot_of(tile), 0.0)
    square = jnp.sum(spot * spot, axis=0, keepdims=True)
    return jnp.where(sub == 3, square, jnp.where(sub == 4, 1.0, spot))


def flip_points(plan, levels, mixed, flipped):
    for column in range(9):
        for level in levels:
            at = column * plan.deep + level
            first, second, third = split(point_of(mixed[at]))
            stacked = jnp.concatenate([first, second, third, first, second, first], axis=0)
            flipped[pl.ds(at * plan.width, plan.width), :] = jnp.transpose(stacked).astype(jnp.bfloat16)


def weigh(plan, flipped, centre, level, number, columns, tiles, base):
    for column in columns:
        span = number * plan.width
        rest = jnp.dot(
            flipped[pl.ds((column * plan.deep + level) * plan.width, span), :],
            centre, preferred_element_type=jnp.float32,
        )
        bump = jnp.maximum(rest, 0.0)
        weight = bump * bump * bump
        high = weight.astype(jnp.bfloat16)
        spot = pl.ds(base + column * span, span)
        tiles[spot, pl.ds(0, LANES)] = high
        tiles[spot, pl.ds(LANES, LANES)] = (weight - high.astype(jnp.float32)).astype(jnp.bfloat16)


def inner_kernel(plan, recv, tiles, mixed, centres, partial, flipped, packed):
    levels = range(plan.blocks)
    place_ring(plan, rims_of(plan), [recv], levels, mixed)
    flip_points(plan, levels, mixed, flipped)
    split_ring(plan, mixed, packed, FULL, levels)
    sub = sublane_ids()
    for block in range(plan.blocks):
        own = point_of(mixed[plan.own(block)])
        own = jnp.where(jnp.logical_and(sub == 0, own > 0.25 * FAR), -FAR, own)
        square = jnp.broadcast_to(own[3:4], (8, LANES))
        own = jnp.where(sub < 3, 2.0 * own, 0.0)
        own = jnp.where(sub == 3, -1.0, own)
        own = jnp.where(sub == 4, plan.cube - square, own)
        first, second, third = split(own)
        stacked = jnp.concatenate([first, first, first, second, second, third], axis=0)
        centre = stacked.astype(jnp.bfloat16)
        centres[block] = centre
        low, number = inner_span(plan, block)
        base = inner_base(plan, block)
        total = None
        for columns in groups_of(number):
            weigh(plan, flipped, centre, low, number, columns, tiles, base)
            part = tile_sum(plan, tiles, base, packed, low, number, columns)
            total = part if total is None else total + part
        partial[block] = fold_full(total)


def edge_kernel(plan, *refs):
    others = refs[:-10]
    near, centres, partial, send, outer, mixed, state, flipped, packed, rows = refs[-10:]
    rims = rims_of(plan)
    levels = range(plan.blocks, plan.deep)
    place_ring(plan, rims, [None, *others], levels, mixed)
    for column in range(9):
        for level in range(plan.blocks):
            at = column * plan.deep + level
            mixed[at] = near[at]
    flip_points(plan, levels, mixed, flipped)
    split_ring(plan, mixed, packed, FULL, levels)
    for block in range(plan.blocks):
        rows[block] = partial[block]

    def before(e, columns):
        centre = centres[rims[e][1]]
        weigh(plan, flipped, centre, plan.blocks + e, 1, columns, outer, e * 9 * plan.width)

    add_rims(plan, rims, outer, packed, rows, FULL, before)
    image = [[None] * plan.blocks for _ in range(3)]
    whole = [[None] * plan.blocks for _ in range(3)]
    start = [[None] * plan.blocks for _ in range(3)]
    for block in range(plan.blocks):
        own = plan.own(block)
        reach = rows[block, pl.ds(3, 1), :]
        state[pl.ds(block, 1), :] = reach
        for axis in range(3):
            field = mixed[own, pl.ds(axis, 1), :]
            start[axis][block] = field
            image[axis][block] = reach * field - rows[block, pl.ds(axis, 1), :]
            whole[axis][block] = field + VISCOUS * image[axis][block]
            spot = mixed[own, pl.ds(4 + axis, 1), :]
            state[pl.ds((1 + axis) * plan.blocks + block, 1), :] = (
                reach * spot - rows[block, pl.ds(4 + axis, 1), :]
            )
    groups = [
        [dot(start[axis], start[axis]) for axis in range(3)],
        [dot(start[axis], whole[axis]) for axis in range(3)],
        [dot(whole[axis], whole[axis]) for axis in range(3)],
    ]
    spread(send, sum(image, []) + [pack(groups)])


def second_kernel(plan, recv, tiles, outer, mixed, state, send, residual, direction, scalars, image, packed, rows):
    rims = rims_of(plan)
    ring_into(plan, rims, recv, 3, image)
    current, curve, square = totals(recv, 3 * plan.blocks, 3)
    alpha = current / curve
    following = jnp.maximum(alpha * alpha * square - current, 0.0)
    beta = following / current
    for at in range(plan.ring):
        field = mixed[at]
        left = field - alpha * (field + VISCOUS * image[at])
        residual[at] = left
        direction[at] = left + beta * field
    scalars[plan.blocks] = alpha
    for block in range(plan.blocks):
        scalars[block] = image[plan.own(block)]
    apply_tiles(plan, rims, tiles, outer, direction, packed, rows, THREE)
    out = []
    groups = [[], [], [], []]
    for axis in range(3):
        left, ahead, shot, whole = [], [], [], []
        for block in range(plan.blocks):
            own = plan.own(block)
            left.append(residual[own, pl.ds(axis, 1), :])
            ahead.append(direction[own, pl.ds(axis, 1), :])
            shot.append(state[pl.ds(block, 1), :] * ahead[block] - rows[block, pl.ds(axis, 1), :])
            whole.append(ahead[block] + VISCOUS * shot[block])
        out.extend(shot)
        groups[0].append(dot(left, left))
        groups[1].append(dot(ahead, whole))
        groups[2].append(dot(left, whole))
        groups[3].append(dot(whole, whole))
    spread(send, out + [pack(groups)])


def third_kernel(
    plan, recv, tiles, outer, mixed, residual, direction, state, scalars,
    send, ends, image, sofar, ahead, steps, packed, rows,
):
    rims = rims_of(plan)
    ring_into(plan, rims, recv, 3, image)
    current, curve, cross, square = totals(recv, 3 * plan.blocks, 4)
    alpha = current / curve
    following = jnp.maximum(current - 2.0 * alpha * cross + alpha * alpha * square, 0.0)
    beta = following / current
    first = scalars[plan.blocks]
    steps[...] = alpha
    sub = sublane_ids()
    for block in range(plan.blocks):
        own = plan.own(block)
        rows[block] = first * scalars[block] + alpha * image[own]
    latest = [
        [rows[block, pl.ds(axis, 1), :] for axis in range(3)] for block in range(plan.blocks)
    ]
    for at in range(plan.ring):
        field = direction[at]
        rest = residual[at] - alpha * (field + VISCOUS * image[at])
        fresh = rest + beta * field
        spot = spot_of(mixed[at])
        made = first * mixed[at] + alpha * field
        moved = made * spot
        moved = pltpu.roll(moved, 6, 0) + pltpu.roll(moved, 5, 0) + pltpu.roll(moved, 4, 0)
        joined = jnp.where(sub < 3, fresh, pltpu.roll(fresh * spot, 3, 0))
        ahead[at] = jnp.where(sub < 6, joined, moved)
        if at - plan.own(0) in range(plan.blocks):
            image[at] = rest
            sofar[at - plan.own(0)] = made
    apply_tiles(plan, rims, tiles, outer, ahead, packed, rows, FULL)
    scale = 1.0 / plan.unit
    base = []
    each = [[None] * plan.blocks for _ in range(3)]
    rests = [[None] * plan.blocks for _ in range(3)]
    heads = [[None] * plan.blocks for _ in range(3)]
    wholes = [[None] * plan.blocks for _ in range(3)]
    for block in range(plan.blocks):
        reach = state[pl.ds(block, 1), :]
        own = plan.own(block)
        total = rows[block, pl.ds(6, 1), :] - reach * ahead[own, pl.ds(6, 1), :]
        for axis in range(3):
            head = ahead[own, pl.ds(axis, 1), :]
            spot = mixed[own, pl.ds(4 + axis, 1), :]
            lean = state[pl.ds((1 + axis) * plan.blocks + block, 1), :]
            shot = reach * head - rows[block, pl.ds(axis, 1), :]
            twice = reach * ahead[own, pl.ds(3 + axis, 1), :] - rows[block, pl.ds(3 + axis, 1), :]
            each[axis][block] = scale * (spot * shot + head * lean - twice)
            made = sofar[block, pl.ds(axis, 1), :]
            total = total + spot * latest[block][axis] + made * lean
            rests[axis][block] = image[own, pl.ds(axis, 1), :]
            heads[axis][block] = head
            wholes[axis][block] = head + VISCOUS * shot
            ends[pl.ds(axis * plan.blocks + block, 1), :] = made
            ends[pl.ds((3 + axis) * plan.blocks + block, 1), :] = head
        base.append(scale * total)
    groups = [
        [dot(rests[axis], rests[axis]) for axis in range(3)],
        [dot(heads[axis], wholes[axis]) for axis in range(3)],
    ]
    spread(send, base + sum(each, []) + [pack(groups)])


def fourth_kernel(plan, recv, tiles, outer, state, send, source, steps, parts, packed, rows):
    rims = rims_of(plan)
    ring_into(plan, rims, recv, 4, parts)
    current, curve = totals(recv, 4 * plan.blocks, 2)
    sub = sublane_ids()
    steps[...] = current / curve
    factor = jnp.where(sub == 0, 1.0, pltpu.roll(steps[...], 1, 0))
    for at in range(plan.ring):
        gathered = jnp.where(sub < 4, parts[at] * factor, 0.0)
        source[at] = jnp.broadcast_to(-jnp.sum(gathered, axis=0, keepdims=True), (8, LANES))
    apply_tiles(plan, rims, tiles, outer, source, packed, rows, ONE)
    field, shot, whole = [], [], []
    for block in range(plan.blocks):
        field.append(source[plan.own(block), pl.ds(0, 1), :])
        shot.append(state[pl.ds(block, 1), :] * field[block] - rows[block, pl.ds(0, 1), :])
        whole.append(STIFFNESS * field[block] + shot[block])
    groups = [[dot(field, field)], [dot(field, whole)], [dot(whole, whole)]]
    spread(send, shot + [pack(groups)])


def fifth_kernel(plan, recv, tiles, outer, source, state, send, ends, image, ahead, steps, packed, rows):
    rims = rims_of(plan)
    ring_into(plan, rims, recv, 1, image)
    current, curve, square = totals(recv, plan.blocks, 3)
    steps[...] = current / curve
    alpha = steps[pl.ds(0, 1), :]
    steps[...] = jnp.maximum(alpha * alpha * square - current, 0.0) / current
    beta = steps[pl.ds(0, 1), :]
    for at in range(plan.ring):
        field = source[at]
        left = field - alpha * (STIFFNESS * field + image[at, pl.ds(0, 1), :])
        image[at] = left
        ahead[at] = left + beta * field
    apply_tiles(plan, rims, tiles, outer, ahead, packed, rows, ONE)
    rests, heads, wholes = [], [], []
    for block in range(plan.blocks):
        own = plan.own(block)
        rests.append(image[own, pl.ds(0, 1), :])
        heads.append(ahead[own, pl.ds(0, 1), :])
        shot = state[pl.ds(block, 1), :] * heads[block] - rows[block, pl.ds(0, 1), :]
        wholes.append(STIFFNESS * heads[block] + shot)
        ends[pl.ds(block, 1), :] = alpha * source[own, pl.ds(0, 1), :]
        ends[pl.ds(plan.blocks + block, 1), :] = heads[block]
    spread(send, [pack([[dot(rests, rests)], [dot(heads, wholes)]])])


def last_kernel(plan, recv, speeds, final, ends, star, pressure, steps):
    current, curve = totals(recv, 0, 2)
    steps[...] = current / curve
    alpha = steps[pl.ds(0, 1), :]
    for block in range(plan.blocks):
        pressure[block] = (
            ends[pl.ds(block, 1), :] + alpha * ends[pl.ds(plan.blocks + block, 1), :]
        )
    for axis in range(3):
        alpha = final[pl.ds(axis, 1), :]
        for block in range(plan.blocks):
            at = axis * plan.blocks + block
            star[at] = (
                speeds[pl.ds(at, 1), :] + alpha * speeds[pl.ds(3 * plan.blocks + at, 1), :]
            )


def call(plan, kernel, operands, outs, scratch=(), space=pltpu.VMEM):
    typed = lambda shape: (shape, jnp.float32) if isinstance(shape[0], int) else shape
    held = lambda item: pltpu.VMEM(*typed(item)) if isinstance(item, tuple) else item
    return pl.pallas_call(
        functools.partial(kernel, plan),
        out_shape=[jax.ShapeDtypeStruct(*typed(shape)) for shape in outs],
        in_specs=[pl.BlockSpec(memory_space=space) for _ in operands],
        out_specs=[pl.BlockSpec(memory_space=pltpu.VMEM) for _ in outs],
        scratch_shapes=[held(item) for item in scratch],
        compiler_params=pltpu.CompilerParams(vmem_limit_bytes=24 * 1024 * 1024),
        name=kernel.__name__,
    )(*operands)


def local(mesh, offsets, velocity, counts, neighbours):
    blocks = counts.shape[2]
    width = offsets.shape[-1]
    plan = Plan(mesh, blocks, width)
    lined = lambda field: field.transpose(0, 1, 3, 2, 4).reshape(3 * blocks, 1, width)
    paired = lambda rows: (rows // 2, 2, width) if rows % 2 == 0 else (rows, 1, width)
    slot = lambda rows: (plan.devices, *paired(rows))
    ring = (plan.ring, 8, width)
    tile = (8, width)
    rows = (blocks, 8, width)
    packed = ((32, plan.ring * width), jnp.bfloat16)
    packed_low = ((16, plan.ring * width), jnp.bfloat16)
    (send,) = call(
        plan, pack_kernel,
        [
            pltpu.with_memory_space_constraint(field, pltpu.HBM)
            for field in (counts.reshape(1, blocks), lined(offsets), lined(velocity))
        ],
        [(plan.count[0] * plan.count[1], *paired(6 * blocks))],
        [
            pltpu.SMEM((1, blocks), jnp.int32), (3 * blocks, 1, width), (3 * blocks, 1, width),
            pltpu.SemaphoreType.DMA((3,)),
        ],
        pltpu.HBM,
    )
    level, *others = exchange_layers(plan, send)
    flipped = ((plan.ring * width, 48), jnp.bfloat16)
    tiles, mixed, centres, partial = call(
        plan, inner_kernel, [level],
        [
            ((inner_base(plan, blocks), 2 * width), jnp.bfloat16), ring,
            ((blocks, 48, width), jnp.bfloat16), rows,
        ],
        [flipped, packed],
    )
    send, outer, mixed, state = call(
        plan, edge_kernel, [*others, mixed, centres, partial],
        [
            slot(3 * blocks + 1), ((plan.rims * 9 * width, 2 * width), jnp.bfloat16),
            ring, (4 * blocks, width),
        ],
        [flipped, packed, rows],
    )
    recv = exchange(send)
    send, residual, direction, scalars = call(
        plan, second_kernel, [recv, tiles, outer, mixed, state],
        [slot(3 * blocks + 1), ring, ring, (blocks + 1, 8, width)],
        [ring, packed_low, rows],
    )
    recv = exchange(send)
    send, speeds = call(
        plan, third_kernel, [recv, tiles, outer, mixed, residual, direction, state, scalars],
        [slot(4 * blocks + 1), (6 * blocks, width)],
        [ring, rows, ring, tile, packed, rows],
    )
    recv = exchange(send)
    send, source, final = call(
        plan, fourth_kernel, [recv, tiles, outer, state],
        [slot(blocks + 1), ring, tile],
        [ring, packed_low, rows],
    )
    recv = exchange(send)
    send, ends = call(
        plan, fifth_kernel, [recv, tiles, outer, source, state],
        [slot(1), (2 * blocks, width)],
        [ring, ring, tile, packed_low, rows],
    )
    recv = exchange(send)
    star, pressure = call(
        plan, last_kernel, [recv, speeds, final, ends],
        [(3 * blocks, 1, width), (blocks, 1, width)], [tile],
    )
    star = star.reshape(3, 1, blocks, 1, width).transpose(0, 1, 3, 2, 4)
    pressure = pressure.reshape(1, blocks, 1, width).transpose(0, 2, 1, 3)
    return star, pressure


def solution(mesh):
    in_specs = (
        P(None, "gx", "gy", "gz", None),
        P(None, "gx", "gy", "gz", None),
        P("gx", "gy", "gz"),
        P("gx", "gy", "gz", None),
    )
    out_specs = (P(None, "gx", "gy", "gz", None), P("gx", "gy", "gz", None))
    return jax.shard_map(
        functools.partial(local, mesh),
        mesh=mesh, in_specs=in_specs, out_specs=out_specs, check_vma=False,
    )
```

```python
import functools

import jax
import jax.numpy as jnp
from jax import lax
from jax.experimental import pallas as pl
from jax.experimental.pallas import tpu as pltpu
from jax.sharding import PartitionSpec as P

VISCOUS = 4.0
STIFFNESS = 0.25
GRAVITY_STEP = 0.5
AXES = ("gx", "gy", "gz")
FAR = 1.0e3
LANES = 128


def exchange(send):
    return lax.all_to_all(send, AXES, 0, 0, tiled=True)


def exchange_layers(plan, send):
    level = lax.all_to_all(send, AXES[:2], 0, 0, tiled=True)
    deep = plan.count[2]
    if deep == 2:
        return [level, lax.ppermute(level, AXES[2], [(0, 1), (1, 0)])]
    forward = [(i, i + 1) for i in range(deep - 1)]
    backward = [(target, source) for source, target in forward]
    return [level] + [lax.ppermute(level, AXES[2], pairs) for pairs in (forward, backward)]


class Plan:
    def __init__(self, mesh, blocks, width):
        self.count = [mesh.shape[axis] for axis in AXES]
        self.devices = self.count[0] * self.count[1] * self.count[2]
        self.blocks = blocks
        self.width = width
        self.rims = 1 if self.count[2] == 2 else 2
        self.deep = blocks + self.rims
        self.ring = 9 * self.deep
        self.cube = (2.0 / width) ** (1.0 / 3.0)
        self.unit = self.cube ** 0.5

    def own(self, block):
        return 4 * self.deep + block


def rims_of(plan):
    last = plan.blocks - 1
    if plan.rims == 2:
        return [(-1, 0, last, -1), (1, last, 0, plan.blocks)]
    above = lax.axis_index(AXES[2]) == 0
    choose = lambda yes, no: jnp.where(above, jnp.int32(yes), jnp.int32(no))
    return [(choose(1, -1), choose(last, 0), choose(0, last), choose(plan.blocks, -1))]


def slots(plan, rims, axes=3):
    place = [lax.axis_index(axis) for axis in AXES]
    found = []
    for column in range(9):
        beside = []
        for step in [0] + [rim[0] for rim in rims]:
            at = [place[0] + column // 3 - 1, place[1] + column % 3 - 1, place[2] + step]
            present = None
            slot = 0
            for axis, (value, count) in enumerate(zip(at, plan.count)):
                inside = jnp.logical_and(value >= 0, value < count)
                present = inside if present is None else jnp.logical_and(present, inside)
                if axis < axes:
                    slot = slot * count + jnp.clip(value, 0, count - 1)
            beside.append((slot, present))
        found.append(beside)
    return found


def take(recv, slot, row):
    if recv.shape[2] == 1:
        return recv[slot, row]
    return recv[slot, row // 2, pl.ds(row % 2, 1), :]


def gather_ring(plan, rims, found, layers, fields, store, levels=None):
    for column in range(9):
        for level in levels or range(plan.deep):
            layer, block, depth = 0, level, level
            if level >= plan.blocks:
                layer = level - plan.blocks + 1
                block, depth = rims[layer - 1][2:]
            slot, present = found[column][layer]
            got = layers[layer]
            rows = [take(got, slot, field * plan.blocks + block) for field in range(fields)]
            store(column * plan.deep + level, column, depth, rows, present)


def ring_into(plan, rims, recv, fields, ref):
    def store(at, column, depth, rows, present):
        for field, row in enumerate(rows):
            ref[at, pl.ds(field, 1), :] = row

    gather_ring(plan, rims, slots(plan, rims), [recv] * (1 + plan.rims), fields, store)


def lane_ids(sublanes=1):
    return lax.broadcasted_iota(jnp.int32, (sublanes, LANES), 1)


def sublane_ids():
    return lax.broadcasted_iota(jnp.int32, (8, LANES), 0)


def totals(recv, row, number):
    summed = jnp.broadcast_to(jnp.sum(take(recv, slice(None), row), axis=0), (8, LANES))
    place = lane_ids(8) - sublane_ids()
    return [
        jnp.broadcast_to(
            jnp.sum(jnp.where(place == 8 * m, summed, 0.0), axis=1, keepdims=True), (8, LANES)
        )
        for m in range(number)
    ]


def pack(groups):
    lane = lane_ids()
    row = jnp.zeros((1, LANES), jnp.float32)
    for m, group in enumerate(groups):
        for c, partial in enumerate(group):
            row = jnp.where(lane == 8 * m + c, jnp.sum(partial, axis=1, keepdims=True), row)
    return row


def dot(first, second):
    total = first[0] * second[0]
    for a, b in zip(first[1:], second[1:]):
        total = total + a * b
    return total


def spread(send, rows):
    size = send.shape[2]
    rows = [jnp.concatenate(rows[r : r + size], axis=0) for r in range(0, len(rows), size)]

    def body(slot, carry):
        for r, row in enumerate(rows):
            send[slot, r] = row
        return carry

    lax.fori_loop(0, send.shape[0], body, 0, unroll=16)


def coarse(value):
    return value.astype(jnp.bfloat16).astype(jnp.float32)


def split(value):
    first = coarse(value)
    rest = value - first
    second = coarse(rest)
    return first, second, rest - second


def stack_full(value):
    first, second, third = split(value)
    return jnp.concatenate([first, second, third, jnp.zeros_like(third)], axis=0)


def fold_full(total):
    both = total[:, :LANES] + total[:, LANES:]
    return both[0:8] + both[8:16] + both[16:24]


def stack_three(value):
    first, second, third = split(value)
    joined = jnp.where(sublane_ids() < 3, first, pltpu.roll(second, 3, 0))
    return jnp.concatenate([joined, third], axis=0)


def fold_three(total):
    both = total[:, :LANES] + total[:, LANES:]
    return both[0:8] + pltpu.roll(both[0:8], 5, 0) + both[8:16]


def stack_one(value):
    first, second, third = split(value)
    sub = sublane_ids()
    joined = jnp.where(sub == 0, first, jnp.where(sub == 1, second, third))
    return jnp.concatenate([jnp.where(sub < 3, joined, 0.0), jnp.zeros_like(third)], axis=0)


def fold_one(total):
    both = total[0:8, :LANES] + total[0:8, LANES:]
    return jnp.broadcast_to(jnp.sum(both, axis=0, keepdims=True), (8, LANES))


FULL = (stack_full, fold_full)
THREE = (stack_three, fold_three)
ONE = (stack_one, fold_one)


def split_ring(plan, ring, packed, form, levels=None):
    for column in range(9):
        for level in levels or range(plan.deep):
            at = column * plan.deep + level
            packed[:, pl.ds(at * LANES, LANES)] = form[0](ring[at]).astype(jnp.bfloat16)


def inner_span(plan, block):
    low = max(block - 1, 0)
    return low, min(block + 2, plan.blocks) - low


def inner_base(plan, block):
    return 9 * sum(inner_span(plan, before)[1] for before in range(block)) * plan.width


def groups_of(number):
    size = 3 if number % 2 == 0 else 9 if number == 1 else 2
    return [range(c, min(c + size, 9)) for c in range(0, 9, size)]


def tile_sum(plan, tiles, base, packed, level, number, columns):
    span = number * plan.width
    ahead = [packed[:, pl.ds((c * plan.deep + level) * LANES, span)] for c in columns]
    return jnp.dot(
        jnp.concatenate(ahead, axis=1) if len(ahead) > 1 else ahead[0],
        tiles[pl.ds(base + columns[0] * span, len(ahead) * span), :],
        preferred_element_type=jnp.float32,
    )


def apply_tiles(plan, rims, tiles, outer, ring, packed, rows, form):
    split_ring(plan, ring, packed, form)
    for block in range(plan.blocks):
        low, number = inner_span(plan, block)
        base = inner_base(plan, block)
        total = None
        for columns in groups_of(number):
            part = tile_sum(plan, tiles, base, packed, low, number, columns)
            total = part if total is None else total + part
        rows[block] = form[1](total)
    add_rims(plan, rims, outer, packed, rows, form, lambda e, columns: None)


def add_rims(plan, rims, outer, packed, rows, form, before):
    for e, rim in enumerate(rims):
        total = None
        for columns in groups_of(1):
            before(e, columns)
            base = e * 9 * plan.width
            part = tile_sum(plan, outer, base, packed, plan.blocks + e, 1, columns)
            total = part if total is None else total + part
        rows[rim[1]] = rows[rim[1]] + form[1](total)


def pack_kernel(plan, counts_in, offsets_in, velocity_in, send, counts, offsets, velocity, sems):
    pairs = [(counts_in, counts), (offsets_in, offsets), (velocity_in, velocity)]
    copies = [pltpu.make_async_copy(a, b, sems.at[i]) for i, (a, b) in enumerate(pairs)]
    for copy in copies:
        copy.start()
    for copy in copies:
        copy.wait()
    lane = lane_ids()
    rows = []
    for axis in range(3):
        for block in range(plan.blocks):
            valid = lane < counts[0, block]
            row = offsets[axis * plan.blocks + block]
            rows.append(jnp.where(valid, row, FAR) if axis == 0 else row)
    for axis in range(3):
        for block in range(plan.blocks):
            valid = lane < counts[0, block]
            row = velocity[axis * plan.blocks + block]
            if axis == 0:
                row = row + GRAVITY_STEP
            rows.append(jnp.where(valid, row, 0.0))
    spread(send, rows)


def place_ring(plan, rims, layers, levels, mixed):
    blank = jnp.where(sublane_ids() == 3, 1.0, 0.0)

    def store(at, column, depth, got, present):
        shift = (column // 3 - 1, column % 3 - 1, depth - (plan.blocks - 1) // 2)
        spots = [
            plan.unit * (got[axis] + jnp.asarray(shift[axis], jnp.float32)) for axis in range(3)
        ]
        spots[0] = jnp.where(present, spots[0], FAR)
        mixed[at] = blank
        for axis in range(3):
            mixed[at, pl.ds(axis, 1), :] = jnp.where(present, got[3 + axis], 0.0)
            mixed[at, pl.ds(4 + axis, 1), :] = spots[axis]

    gather_ring(plan, rims, slots(plan, rims, 2), layers, 6, store, levels)


def spot_of(tile):
    return pltpu.roll(tile, 4, 0)


def point_of(tile):
    sub = sublane_ids()
    spot = jnp.where(sub < 3, spot_of(tile), 0.0)
    square = jnp.sum(spot * spot, axis=0, keepdims=True)
    return jnp.where(sub == 3, square, jnp.where(sub == 4, 1.0, spot))


def flip_points(plan, levels, mixed, flipped):
    for column in range(9):
        for level in levels:
            at = column * plan.deep + level
            first, second, third = split(point_of(mixed[at]))
            stacked = jnp.concatenate([first, second, third, first, second, first], axis=0)
            flipped[pl.ds(at * plan.width, plan.width), :] = jnp.transpose(stacked).astype(jnp.bfloat16)


def weigh(plan, flipped, centre, level, number, columns, tiles, base):
    for column in columns:
        span = number * plan.width
        rest = jnp.dot(
            flipped[pl.ds((column * plan.deep + level) * plan.width, span), :],
            centre, preferred_element_type=jnp.float32,
        )
        bump = jnp.maximum(rest, 0.0)
        weight = bump * bump * bump
        high = weight.astype(jnp.bfloat16)
        spot = pl.ds(base + column * span, span)
        tiles[spot, pl.ds(0, LANES)] = high
        tiles[spot, pl.ds(LANES, LANES)] = (weight - high.astype(jnp.float32)).astype(jnp.bfloat16)


def inner_kernel(plan, recv, tiles, mixed, centres, partial, flipped, packed):
    levels = range(plan.blocks)
    place_ring(plan, rims_of(plan), [recv], levels, mixed)
    flip_points(plan, levels, mixed, flipped)
    split_ring(plan, mixed, packed, FULL, levels)
    sub = sublane_ids()
    for block in range(plan.blocks):
        own = point_of(mixed[plan.own(block)])
        own = jnp.where(jnp.logical_and(sub == 0, own > 0.25 * FAR), -FAR, own)
        square = jnp.broadcast_to(own[3:4], (8, LANES))
        own = jnp.where(sub < 3, 2.0 * own, 0.0)
        own = jnp.where(sub == 3, -1.0, own)
        own = jnp.where(sub == 4, plan.cube - square, own)
        first, second, third = split(own)
        stacked = jnp.concatenate([first, first, first, second, second, third], axis=0)
        centre = stacked.astype(jnp.bfloat16)
        centres[block] = centre
        low, number = inner_span(plan, block)
        base = inner_base(plan, block)
        total = None
        for columns in groups_of(number):
            weigh(plan, flipped, centre, low, number, columns, tiles, base)
            part = tile_sum(plan, tiles, base, packed, low, number, columns)
            total = part if total is None else total + part
        partial[block] = fold_full(total)


def edge_kernel(plan, *refs):
    others = refs[:-10]
    near, centres, partial, send, outer, mixed, state, flipped, packed, rows = refs[-10:]
    rims = rims_of(plan)
    levels = range(plan.blocks, plan.deep)
    place_ring(plan, rims, [None, *others], levels, mixed)
    for column in range(9):
        for level in range(plan.blocks):
            at = column * plan.deep + level
            mixed[at] = near[at]
    flip_points(plan, levels, mixed, flipped)
    split_ring(plan, mixed, packed, FULL, levels)
    for block in range(plan.blocks):
        rows[block] = partial[block]

    def before(e, columns):
        centre = centres[rims[e][1]]
        weigh(plan, flipped, centre, plan.blocks + e, 1, columns, outer, e * 9 * plan.width)

    add_rims(plan, rims, outer, packed, rows, FULL, before)
    image = [[None] * plan.blocks for _ in range(3)]
    whole = [[None] * plan.blocks for _ in range(3)]
    start = [[None] * plan.blocks for _ in range(3)]
    for block in range(plan.blocks):
        own = plan.own(block)
        reach = rows[block, pl.ds(3, 1), :]
        state[pl.ds(block, 1), :] = reach
        for axis in range(3):
            field = mixed[own, pl.ds(axis, 1), :]
            start[axis][block] = field
            image[axis][block] = reach * field - rows[block, pl.ds(axis, 1), :]
            whole[axis][block] = field + VISCOUS * image[axis][block]
            spot = mixed[own, pl.ds(4 + axis, 1), :]
            state[pl.ds((1 + axis) * plan.blocks + block, 1), :] = (
                reach * spot - rows[block, pl.ds(4 + axis, 1), :]
            )
    groups = [
        [dot(start[axis], start[axis]) for axis in range(3)],
        [dot(start[axis], whole[axis]) for axis in range(3)],
        [dot(whole[axis], whole[axis]) for axis in range(3)],
    ]
    spread(send, sum(image, []) + [pack(groups)])


def second_kernel(plan, recv, tiles, outer, mixed, state, send, residual, direction, scalars, image, packed, rows):
    rims = rims_of(plan)
    ring_into(plan, rims, recv, 3, image)
    current, curve, square = totals(recv, 3 * plan.blocks, 3)
    alpha = current / curve
    following = jnp.maximum(alpha * alpha * square - current, 0.0)
    beta = following / current
    for at in range(plan.ring):
        field = mixed[at]
        left = field - alpha * (field + VISCOUS * image[at])
        residual[at] = left
        direction[at] = left + beta * field
    scalars[plan.blocks] = alpha
    for block in range(plan.blocks):
        scalars[block] = image[plan.own(block)]
    apply_tiles(plan, rims, tiles, outer, direction, packed, rows, THREE)
    out = []
    groups = [[], [], [], []]
    for axis in range(3):
        left, ahead, shot, whole = [], [], [], []
        for block in range(plan.blocks):
            own = plan.own(block)
            left.append(residual[own, pl.ds(axis, 1), :])
            ahead.append(direction[own, pl.ds(axis, 1), :])
            shot.append(state[pl.ds(block, 1), :] * ahead[block] - rows[block, pl.ds(axis, 1), :])
            whole.append(ahead[block] + VISCOUS * shot[block])
        out.extend(shot)
        groups[0].append(dot(left, left))
        groups[1].append(dot(ahead, whole))
        groups[2].append(dot(left, whole))
        groups[3].append(dot(whole, whole))
    spread(send, out + [pack(groups)])


def third_kernel(
    plan, recv, tiles, outer, mixed, residual, direction, state, scalars,
    send, ends, image, sofar, ahead, steps, packed, rows,
):
    rims = rims_of(plan)
    ring_into(plan, rims, recv, 3, image)
    current, curve, cross, square = totals(recv, 3 * plan.blocks, 4)
    alpha = current / curve
    following = jnp.maximum(current - 2.0 * alpha * cross + alpha * alpha * square, 0.0)
    beta = following / current
    first = scalars[plan.blocks]
    steps[...] = alpha
    sub = sublane_ids()
    for block in range(plan.blocks):
        own = plan.own(block)
        rows[block] = first * scalars[block] + alpha * image[own]
    latest = [
        [rows[block, pl.ds(axis, 1), :] for axis in range(3)] for block in range(plan.blocks)
    ]
    for at in range(plan.ring):
        field = direction[at]
        rest = residual[at] - alpha * (field + VISCOUS * image[at])
        fresh = rest + beta * field
        spot = spot_of(mixed[at])
        made = first * mixed[at] + alpha * field
        moved = made * spot
        moved = pltpu.roll(moved, 6, 0) + pltpu.roll(moved, 5, 0) + pltpu.roll(moved, 4, 0)
        joined = jnp.where(sub < 3, fresh, pltpu.roll(fresh * spot, 3, 0))
        ahead[at] = jnp.where(sub < 6, joined, moved)
        if at - plan.own(0) in range(plan.blocks):
            image[at] = rest
            sofar[at - plan.own(0)] = made
    apply_tiles(plan, rims, tiles, outer, ahead, packed, rows, FULL)
    scale = 1.0 / plan.unit
    base = []
    each = [[None] * plan.blocks for _ in range(3)]
    rests = [[None] * plan.blocks for _ in range(3)]
    heads = [[None] * plan.blocks for _ in range(3)]
    wholes = [[None] * plan.blocks for _ in range(3)]
    for block in range(plan.blocks):
        reach = state[pl.ds(block, 1), :]
        own = plan.own(block)
        total = rows[block, pl.ds(6, 1), :] - reach * ahead[own, pl.ds(6, 1), :]
        for axis in range(3):
            head = ahead[own, pl.ds(axis, 1), :]
            spot = mixed[own, pl.ds(4 + axis, 1), :]
            lean = state[pl.ds((1 + axis) * plan.blocks + block, 1), :]
            shot = reach * head - rows[block, pl.ds(axis, 1), :]
            twice = reach * ahead[own, pl.ds(3 + axis, 1), :] - rows[block, pl.ds(3 + axis, 1), :]
            each[axis][block] = scale * (spot * shot + head * lean - twice)
            made = sofar[block, pl.ds(axis, 1), :]
            total = total + spot * latest[block][axis] + made * lean
            rests[axis][block] = image[own, pl.ds(axis, 1), :]
            heads[axis][block] = head
            wholes[axis][block] = head + VISCOUS * shot
            ends[pl.ds(axis * plan.blocks + block, 1), :] = made
            ends[pl.ds((3 + axis) * plan.blocks + block, 1), :] = head
        base.append(scale * total)
    groups = [
        [dot(rests[axis], rests[axis]) for axis in range(3)],
        [dot(heads[axis], wholes[axis]) for axis in range(3)],
    ]
    spread(send, base + sum(each, []) + [pack(groups)])


def fourth_kernel(plan, recv, tiles, outer, state, send, source, steps, parts, packed, rows):
    rims = rims_of(plan)
    ring_into(plan, rims, recv, 4, parts)
    current, curve = totals(recv, 4 * plan.blocks, 2)
    sub = sublane_ids()
    steps[...] = current / curve
    factor = jnp.where(sub == 0, 1.0, pltpu.roll(steps[...], 1, 0))
    for at in range(plan.ring):
        gathered = jnp.where(sub < 4, parts[at] * factor, 0.0)
        source[at] = jnp.broadcast_to(-jnp.sum(gathered, axis=0, keepdims=True), (8, LANES))
    apply_tiles(plan, rims, tiles, outer, source, packed, rows, ONE)
    field, shot, whole = [], [], []
    for block in range(plan.blocks):
        field.append(source[plan.own(block), pl.ds(0, 1), :])
        shot.append(state[pl.ds(block, 1), :] * field[block] - rows[block, pl.ds(0, 1), :])
        whole.append(STIFFNESS * field[block] + shot[block])
    groups = [[dot(field, field)], [dot(field, whole)], [dot(whole, whole)]]
    spread(send, shot + [pack(groups)])


def fifth_kernel(plan, recv, tiles, outer, source, state, send, ends, image, ahead, steps, packed, rows):
    rims = rims_of(plan)
    ring_into(plan, rims, recv, 1, image)
    current, curve, square = totals(recv, plan.blocks, 3)
    steps[...] = current / curve
    alpha = steps[pl.ds(0, 1), :]
    steps[...] = jnp.maximum(alpha * alpha * square - current, 0.0) / current
    beta = steps[pl.ds(0, 1), :]
    for at in range(plan.ring):
        field = source[at]
        left = field - alpha * (STIFFNESS * field + image[at, pl.ds(0, 1), :])
        image[at] = left
        ahead[at] = left + beta * field
    apply_tiles(plan, rims, tiles, outer, ahead, packed, rows, ONE)
    rests, heads, wholes = [], [], []
    for block in range(plan.blocks):
        own = plan.own(block)
        rests.append(image[own, pl.ds(0, 1), :])
        heads.append(ahead[own, pl.ds(0, 1), :])
        shot = state[pl.ds(block, 1), :] * heads[block] - rows[block, pl.ds(0, 1), :]
        wholes.append(STIFFNESS * heads[block] + shot)
        ends[pl.ds(block, 1), :] = alpha * source[own, pl.ds(0, 1), :]
        ends[pl.ds(plan.blocks + block, 1), :] = heads[block]
    spread(send, [pack([[dot(rests, rests)], [dot(heads, wholes)]])])


def last_kernel(plan, recv, speeds, final, ends, star, pressure, steps):
    current, curve = totals(recv, 0, 2)
    steps[...] = current / curve
    alpha = steps[pl.ds(0, 1), :]
    for block in range(plan.blocks):
        pressure[block] = (
            ends[pl.ds(block, 1), :] + alpha * ends[pl.ds(plan.blocks + block, 1), :]
        )
    for axis in range(3):
        alpha = final[pl.ds(axis, 1), :]
        for block in range(plan.blocks):
            at = axis * plan.blocks + block
            star[at] = (
                speeds[pl.ds(at, 1), :] + alpha * speeds[pl.ds(3 * plan.blocks + at, 1), :]
            )


def call(plan, kernel, operands, outs, scratch=(), space=pltpu.VMEM):
    typed = lambda shape: (shape, jnp.float32) if isinstance(shape[0], int) else shape
    held = lambda item: pltpu.VMEM(*typed(item)) if isinstance(item, tuple) else item
    return pl.pallas_call(
        functools.partial(kernel, plan),
        out_shape=[jax.ShapeDtypeStruct(*typed(shape)) for shape in outs],
        in_specs=[pl.BlockSpec(memory_space=space) for _ in operands],
        out_specs=[pl.BlockSpec(memory_space=pltpu.VMEM) for _ in outs],
        scratch_shapes=[held(item) for item in scratch],
        compiler_params=pltpu.CompilerParams(vmem_limit_bytes=24 * 1024 * 1024),
        name=kernel.__name__,
    )(*operands)


def local(mesh, offsets, velocity, counts, neighbours):
    blocks = counts.shape[2]
    width = offsets.shape[-1]
    plan = Plan(mesh, blocks, width)
    lined = lambda field: field.transpose(0, 1, 3, 2, 4).reshape(3 * blocks, 1, width)
    paired = lambda rows: (rows // 2, 2, width) if rows % 2 == 0 else (rows, 1, width)
    slot = lambda rows: (plan.devices, *paired(rows))
    ring = (plan.ring, 8, width)
    tile = (8, width)
    rows = (blocks, 8, width)
    packed = ((32, plan.ring * width), jnp.bfloat16)
    packed_low = ((16, plan.ring * width), jnp.bfloat16)
    (send,) = call(
        plan, pack_kernel,
        [
            pltpu.with_memory_space_constraint(field, pltpu.HBM)
            for field in (counts.reshape(1, blocks), lined(offsets), lined(velocity))
        ],
        [(plan.count[0] * plan.count[1], *paired(6 * blocks))],
        [
            pltpu.SMEM((1, blocks), jnp.int32), (3 * blocks, 1, width), (3 * blocks, 1, width),
            pltpu.SemaphoreType.DMA((3,)),
        ],
        pltpu.HBM,
    )
    level, *others = exchange_layers(plan, send)
    flipped = ((plan.ring * width, 48), jnp.bfloat16)
    tiles, mixed, centres, partial = call(
        plan, inner_kernel, [level],
        [
            ((inner_base(plan, blocks), 2 * width), jnp.bfloat16), ring,
            ((blocks, 48, width), jnp.bfloat16), rows,
        ],
        [flipped, packed],
    )
    send, outer, mixed, state = call(
        plan, edge_kernel, [*others, mixed, centres, partial],
        [
            slot(3 * blocks + 1), ((plan.rims * 9 * width, 2 * width), jnp.bfloat16),
            ring, (4 * blocks, width),
        ],
        [flipped, packed, rows],
    )
    recv = exchange(send)
    send, residual, direction, scalars = call(
        plan, second_kernel, [recv, tiles, outer, mixed, state],
        [slot(3 * blocks + 1), ring, ring, (blocks + 1, 8, width)],
        [ring, packed_low, rows],
    )
    recv = exchange(send)
    send, speeds = call(
        plan, third_kernel, [recv, tiles, outer, mixed, residual, direction, state, scalars],
        [slot(4 * blocks + 1), (6 * blocks, width)],
        [ring, rows, ring, tile, packed, rows],
    )
    recv = exchange(send)
    send, source, final = call(
        plan, fourth_kernel, [recv, tiles, outer, state],
        [slot(blocks + 1), ring, tile],
        [ring, packed_low, rows],
    )
    recv = exchange(send)
    send, ends = call(
        plan, fifth_kernel, [recv, tiles, outer, source, state],
        [slot(1), (2 * blocks, width)],
        [ring, ring, tile, packed_low, rows],
    )
    recv = exchange(send)
    star, pressure = call(
        plan, last_kernel, [recv, speeds, final, ends],
        [(3 * blocks, 1, width), (blocks, 1, width)], [tile],
    )
    star = star.reshape(3, 1, blocks, 1, width).transpose(0, 1, 3, 2, 4)
    pressure = pressure.reshape(1, blocks, 1, width).transpose(0, 2, 1, 3)
    return star, pressure


def solution(mesh):
    in_specs = (
        P(None, "gx", "gy", "gz", None),
        P(None, "gx", "gy", "gz", None),
        P("gx", "gy", "gz"),
        P("gx", "gy", "gz", None),
    )
    out_specs = (P(None, "gx", "gy", "gz", None), P("gx", "gy", "gz", None))
    return jax.shard_map(
        functools.partial(local, mesh),
        mesh=mesh, in_specs=in_specs, out_specs=out_specs, check_vma=False,
    )
```
